512 devices in a mesh: gx: 4 (over x), gy: 16 (over z_lo, core), gz: 8 (over y, z_hi).
Axes of the slice: x: 4, y: 4, z: 16 (z_hi: 2, z_lo: 8; z = z_hi * 8 + z_lo), core: 2. Of those that a mesh axis runs over, the one named last changes fastest.
Arguments:
- fractions: float32 [2, 3, 524288], P(None, None, ('gx', 'gy', 'gz')), may hold values from -0.5 to 0.5
- centers: int32 [2, 524288], P(None, ('gx', 'gy', 'gz')), may hold values from 0 to 2047, as said below
- deform: float32 [2, 9, 524288], P(None, None, ('gx', 'gy', 'gz')), may hold values from -0.12 to 1.4, as said below
- next_affine: float32 [2, 9, 524288], P(None, None, ('gx', 'gy', 'gz')), may hold values from -3 to 3
- cell_mass: float32 [2, 16, 64, 1024], P(None, 'gx', 'gy', 'gz'), may hold values from 0.25 to 4
- final_adjoint: float32 [21, 524288], P(None, ('gx', 'gy', 'gz')), may hold values from -6 to 6
- live_count: int32 [512, 2], P(('gx', 'gy', 'gz')), may hold values from 128 to 1024, as said below
- send_slot: int32 [512, 26, 32], P(('gx', 'gy', 'gz')), may hold values from 0 to 1023, as said below
- receive_slot: int32 [512, 26, 32], P(('gx', 'gy', 'gz')), may hold values from 0 to 1023, as said below
- receive_count: int32 [512, 26], P(('gx', 'gy', 'gz')), may hold values from 0 to 32, as said below
- prior_slot: int32 [524288], P(('gx', 'gy', 'gz')), may hold values from 0 to 1024, as said below
Outputs:
- initial_adjoint: float32 [21, 524288], P(None, ('gx', 'gy', 'gz'))
The draws below stay inside these ranges and needn't reach their ends.
Inputs may be any that keep to these rules, and one draw needn't show every extreme that they name: `live_count`: particles in use occupy the slots below the count; the counts differ between tiles. `receive_count`: zero toward offsets that leave the grid of tiles. For j below receive_count[t, d], receive_slot[t, d, j] are distinct in-use second-step slots of tile t; no slot is named both here and by a prior_slot entry below 1024, and together they name every in-use second-step slot once; later entries are arbitrary slots. send_slot[u, 25 - d, j] is the first-step slot on tile u of the particle named by receive_slot[t, d, j], u the tile at offset d from t; together with prior_slot these name every in-use first-step slot once; entries past the count are arbitrary slots. `prior_slot`: 1024 marks a second-step slot whose particle did not stay on the tile, or that is not in use. `centers`: the global node is at least one cell away from the grid's faces; within each tile and step the values do not fall from slot to slot. `deform`: each 3 x 3 matrix has diagonal entries in [0.7, 1.4] and other entries in [-0.12, 0.12].
All inputs are finite; a program needn't handle non-finite values.
Results may differ from the reference program's by a relative error of at most 0.0003.
Values sent between devices are 32-bit elements; how exact they have to be, the bound alone decides.
No kernel may reach another device: no remote copies, remote signals or barrier semaphores. Data moves between devices by JAX's collectives and lax.ppermute only.
A program may use at most 128 MiB of HBM per device.

```python
import math
import jax
import jax.numpy as jnp
import numpy as np

CX = 4
CY = 4
CZ = 128
PD = 1024
MIG = 32
TX = 4
TY = 16
TZ = 8
TILES = 512
NX = 16
NY = 64
NZ = 1024
NP = 524288


neighbour_table = np.array([[along_x, along_y, along_z] for along_x in (-1, 0, 1) for along_y in (-1, 0, 1) for along_z in (-1, 0, 1) if (along_x, along_y, along_z) != (0, 0, 0)], dtype=np.int32)


def ranked_slots(key, live):
    ranks = jnp.arange(PD, dtype=jnp.int32)
    scores = jax.random.randint(key, (TILES, PD), 0, 2 ** 14, dtype=jnp.int32) * PD + ranks[None] + (ranks[None] >= live[:, None]).astype(jnp.int32) * 2 ** 30
    return jnp.argsort(scores, axis=1, stable=True).astype(jnp.int32)


def migration_tables(key):
    base = jax.random.fold_in(key, 911)
    tiles = jnp.arange(TILES, dtype=jnp.int32)
    tile_x = tiles // (TY * TZ)
    tile_y = tiles // TZ % TY
    tile_z = tiles % TZ
    offsets = jnp.asarray(neighbour_table)
    near_x = tile_x[:, None] + offsets[None, :, 0]
    near_y = tile_y[:, None] + offsets[None, :, 1]
    near_z = tile_z[:, None] + offsets[None, :, 2]
    valid = ((near_x >= 0) & (near_x < TX) & (near_y >= 0) & (near_y < TY) & (near_z >= 0) & (near_z < TZ)).astype(jnp.int32)
    near = (jnp.clip(near_x, 0, TX - 1) * TY + jnp.clip(near_y, 0, TY - 1)) * TZ + jnp.clip(near_z, 0, TZ - 1)
    magnitude = jnp.abs(offsets)
    nonzero = jnp.sum(magnitude, axis=1)
    face_side = ((nonzero == 1) & (magnitude[:, 2] == 0)).astype(jnp.int32)
    face_end = ((nonzero == 1) & (magnitude[:, 2] == 1)).astype(jnp.int32)
    edge_long = ((nonzero == 2) & (magnitude[:, 2] == 0)).astype(jnp.int32)
    small_class = 1 - face_side - face_end - edge_long
    big = jax.random.randint(jax.random.fold_in(base, 1), (TILES, 26), MIG // 2, MIG + 1, dtype=jnp.int32)
    middle = jax.random.randint(jax.random.fold_in(base, 5), (TILES, 26), 0, MIG // 8 + 1, dtype=jnp.int32)
    little = jax.random.randint(jax.random.fold_in(base, 6), (TILES, 26), 0, 3, dtype=jnp.int32)
    outgoing = (big * face_side[None] + middle * (face_end + edge_long)[None] + little * small_class[None]) * valid
    outgoing = outgoing.at[0, 21].set(MIG)
    opposite = 25 - jnp.arange(26, dtype=jnp.int32)
    incoming = outgoing[near, opposite[None, :]] * valid
    out_total = jnp.sum(outgoing, axis=1)
    in_total = jnp.sum(incoming, axis=1)
    most_moving = jnp.maximum(out_total, in_total)
    upper = PD - 5 * MIG - 40
    stay = jax.random.randint(jax.random.fold_in(base, 2), (TILES,), PD // 2, upper + 1, dtype=jnp.int32)
    stay = jnp.minimum(stay, PD - most_moving)
    stay = stay.at[0].set(PD - most_moving[0])
    live_first = stay + out_total
    live_second = stay + in_total
    order_first = ranked_slots(jax.random.fold_in(base, 3), live_first)
    order_second = ranked_slots(jax.random.fold_in(base, 4), live_second)
    positions = jnp.arange(MIG, dtype=jnp.int32)
    start_first = stay[:, None] + jnp.cumsum(outgoing, axis=1) - outgoing
    start_second = stay[:, None] + jnp.cumsum(incoming, axis=1) - incoming
    send = jnp.take_along_axis(order_first, jnp.minimum(start_first[:, :, None] + positions, PD - 1).reshape(TILES, -1), axis=1).reshape(TILES, 26, MIG)
    receive = jnp.take_along_axis(order_second, jnp.minimum(start_second[:, :, None] + positions, PD - 1).reshape(TILES, -1), axis=1).reshape(TILES, 26, MIG)
    ranks = jnp.arange(PD, dtype=jnp.int32)
    by_rank = jnp.where(ranks[None] < stay[:, None], order_first, PD).astype(jnp.int32)
    inverse = jnp.argsort(order_second, axis=1, stable=True)
    prior = jnp.take_along_axis(by_rank, inverse, axis=1)
    live = jnp.stack([live_first, live_second], axis=1).astype(jnp.int32)
    return (live, send.astype(jnp.int32), receive.astype(jnp.int32), incoming.astype(jnp.int32), prior.reshape(-1).astype(jnp.int32))


def draw_live_count(key, part):
    return migration_tables(key)[0]


def draw_send_slot(key, part):
    return migration_tables(key)[1]


def draw_receive_slot(key, part):
    return migration_tables(key)[2]


def draw_receive_count(key, part):
    return migration_tables(key)[3]


def draw_prior_slot(key, part):
    return migration_tables(key)[4]


def draw_centers(key, part):
    slot = jnp.arange(NP, dtype=jnp.int32)
    tile = slot // PD
    tile_x = tile // (TY * TZ)
    tile_y = tile // TZ % TY
    tile_z = tile % TZ
    local_x = jax.random.randint(jax.random.fold_in(key, 31), (2, NP), 0, CX, dtype=jnp.int32)
    local_y = jax.random.randint(jax.random.fold_in(key, 32), (2, NP), 0, CY, dtype=jnp.int32)
    local_z = jax.random.randint(jax.random.fold_in(key, 33), (2, NP), 0, CZ, dtype=jnp.int32)
    place_x = jnp.clip(tile_x[None] * CX + local_x, 1, NX - 2) - tile_x[None] * CX
    place_y = jnp.clip(tile_y[None] * CY + local_y, 1, NY - 2) - tile_y[None] * CY
    place_z = jnp.clip(tile_z[None] * CZ + local_z, 1, NZ - 2) - tile_z[None] * CZ
    cells = ((place_x * CY + place_y) * CZ + place_z).astype(jnp.int32)
    return jnp.sort(cells.reshape(2, TILES, PD), axis=2).reshape(2, NP).astype(jnp.int32)


def draw_deform(key, part):
    lowest, highest, spread = (0.8, 1.25, 0.1)
    diagonal = jax.random.uniform(jax.random.fold_in(key, 41), (2, 3, NP), jnp.float32, lowest, highest)
    others = jax.random.uniform(jax.random.fold_in(key, 42), (2, 3, 3, NP), jnp.float32, -spread, spread)
    identity = jnp.eye(3, dtype=jnp.float32)
    full = others * (1.0 - identity)[None, :, :, None] + identity[None, :, :, None] * diagonal[:, :, None, :]
    return full.reshape(2, 9, NP)


def shard_levels(own_key, extent, shards, least, high):
    def one(position, blocks):
        heights = jax.random.uniform(jax.random.fold_in(jax.random.fold_in(own_key, 6), position), (blocks,), jnp.float32, least / len(shards), high / len(shards))
        return jnp.repeat(jnp.exp(heights), extent[position] // blocks).reshape((-1,) + (1,) * (len(extent) - position - 1))

    loudness = one(*shards[0])
    for cut in shards[1:]:
        loudness = loudness * one(*cut)
    return loudness


def gaussian(stream_key, extent, scale, reach, cuts=(), kind=jnp.bfloat16):
    level = shard_levels(stream_key, extent, cuts, -0.22, 0.18) if cuts else 1.0
    values = jax.random.normal(stream_key, extent, jnp.float32) * scale * level
    return jnp.minimum(jnp.maximum(values, -reach), reach).astype(kind)


def setup_inputs(seed: int = 0) -> dict:
    key_of = jax.random.split(jax.random.key(seed), 12)
    fractions = jnp.clip(jax.random.uniform(key_of[0], (2, 3, NP), jnp.float32, -0.5, 0.5) * shard_levels(key_of[0], (2, 3, NP), ((2, 512),), -0.4, 0.0), -0.5, 0.5)
    centers = draw_centers(jax.random.fold_in(key_of[11], 71), 0)
    deform = draw_deform(jax.random.fold_in(key_of[11], 71), 0)
    next_affine = gaussian(key_of[3], (2, 9, NP), 0.5, 3.0, ((2, 512),), jnp.float32)
    cell_mass = jnp.clip(jnp.exp(math.log(4.0) - 2.7725887 * jax.random.uniform(key_of[4], (2, NX, NY, NZ), jnp.float32) ** shard_levels(key_of[4], (2, NX, NY, NZ), ((1, 4), (2, 16), (3, 8)), -0.2, 0.2)), 0.25, 4.0)
    final_adjoint = gaussian(key_of[5], (21, NP), 1.0, 6.0, ((1, 512),), jnp.float32)
    live_count = draw_live_count(jax.random.fold_in(key_of[11], 71), 0)
    send_slot = draw_send_slot(jax.random.fold_in(key_of[11], 71), 0)
    receive_slot = draw_receive_slot(jax.random.fold_in(key_of[11], 71), 0)
    receive_count = draw_receive_count(jax.random.fold_in(key_of[11], 71), 0)
    prior_slot = draw_prior_slot(jax.random.fold_in(key_of[11], 71), 0)
    return dict(fractions=fractions, centers=centers, deform=deform, next_affine=next_affine, cell_mass=cell_mass, final_adjoint=final_adjoint, live_count=live_count, send_slot=send_slot, receive_slot=receive_slot, receive_count=receive_count, prior_slot=prior_slot)


TIME_STEP = 0.2
APIC_SCALE = 4.0
STRESS_SCALE = 0.3
SHEAR = 1.0
BULK = 1.0

stencil_rows = [[along_x, along_y, along_z] for along_x in (-1, 0, 1) for along_y in (-1, 0, 1) for along_z in (-1, 0, 1)]
neighbour_rows = [row for row in stencil_rows if row != [0, 0, 0]]
stencil = np.array(stencil_rows, dtype=np.int32)
neighbours = np.array(neighbour_rows, dtype=np.int32)


def spline_table(fraction):
    lower = 0.5 * (0.5 - fraction) * (0.5 - fraction)
    middle = 0.75 - fraction * fraction
    upper = 0.5 * (0.5 + fraction) * (0.5 + fraction)
    return jnp.stack([lower, middle, upper])


def transfer_rule(adjoint, deform_now, affine_next):
    count = adjoint.shape[1]
    velocity = adjoint[0:3]
    affine = adjoint[3:12].reshape(3, 3, count)
    gradient = adjoint[12:21].reshape(3, 3, count)
    deformation = deform_now.reshape(3, 3, count)
    successor = affine_next.reshape(3, 3, count)
    back_deform = gradient + TIME_STEP * jnp.sum(successor[:, :, None] * gradient[:, None], axis=0)
    back_affine = affine + TIME_STEP * jnp.sum(gradient[:, None] * deformation[None], axis=2)
    return velocity, back_affine, back_deform, deformation


def cofactors(deformation):
    rows = []
    for row in range(3):
        entries = []
        for column in range(3):
            entries.append(deformation[(row + 1) % 3, (column + 1) % 3] * deformation[(row + 2) % 3, (column + 2) % 3]
                           - deformation[(row + 1) % 3, (column + 2) % 3] * deformation[(row + 2) % 3, (column + 1) % 3])
        rows.append(jnp.stack(entries))
    return jnp.stack(rows)


def particle_rule(gathered, area, back_deform, deformation):
    count = gathered.shape[1]
    stress = -STRESS_SCALE * area
    symmetric = stress + jnp.swapaxes(stress, 0, 1)
    shear_term = jnp.sum(symmetric[:, :, None] * deformation[None], axis=1)
    cofactor = cofactors(deformation)
    determinant = jnp.sum(deformation[0] * cofactor[0], axis=0)
    trace_value = stress[0, 0] + stress[1, 1] + stress[2, 2]
    new_deform = back_deform + SHEAR * shear_term + BULK * (trace_value / determinant)[None, None] * cofactor
    return jnp.concatenate([gathered, area.reshape(9, count), new_deform.reshape(9, count)])


def reverse_global(adjoint, fraction, node, deform_now, affine_next, mass_flat, keep_flat, in_use):
    adjoint = adjoint * in_use[None]
    velocity, back_affine, back_deform, deformation = transfer_rule(adjoint, deform_now, affine_next)
    table = spline_table(fraction)
    field = jnp.zeros((3, NX * NY * NZ), jnp.float32)
    for offset in stencil_rows:
        weight = table[offset[0] + 1, 0] * table[offset[1] + 1, 1] * table[offset[2] + 1, 2]
        distance = jnp.asarray(offset, jnp.float32)[:, None] - fraction
        term = weight[None] * (velocity + APIC_SCALE * jnp.sum(back_affine * distance[None], axis=1))
        target = node + (offset[0] * NY * NZ + offset[1] * NZ + offset[2])
        field = field.at[:, target].add(term)
    values = field / mass_flat[None] * keep_flat[None]
    gathered = jnp.zeros((3, node.shape[0]), jnp.float32)
    area = jnp.zeros((3, 3, node.shape[0]), jnp.float32)
    for offset in stencil_rows:
        weight = table[offset[0] + 1, 0] * table[offset[1] + 1, 1] * table[offset[2] + 1, 2]
        distance = jnp.asarray(offset, jnp.float32)[:, None] - fraction
        target = node + (offset[0] * NY * NZ + offset[1] * NZ + offset[2])
        weighted = weight[None] * values[:, target]
        gathered = gathered + weighted
        area = area + weighted[:, None] * distance[None]
    return particle_rule(gathered, area, back_deform, deformation) * in_use[None]


def reference(fractions, centers, deform, next_affine, cell_mass, final_adjoint, live_count, send_slot, receive_slot, receive_count, prior_slot):
    slot = jnp.arange(NP, dtype=jnp.int32)
    tile = slot // PD
    rank = slot % PD
    tile_x = tile // (TY * TZ)
    tile_y = (tile // TZ) % TY
    tile_z = tile % TZ
    coord_x = jnp.arange(NX, dtype=jnp.int32)
    coord_y = jnp.arange(NY, dtype=jnp.int32)
    coord_z = jnp.arange(NZ, dtype=jnp.int32)
    keep_x = ((coord_x >= 1) & (coord_x <= NX - 2)).astype(jnp.float32)
    keep_y = ((coord_y >= 1) & (coord_y <= NY - 2)).astype(jnp.float32)
    keep_z = ((coord_z >= 1) & (coord_z <= NZ - 2)).astype(jnp.float32)
    keep_flat = (keep_x[:, None, None] * keep_y[None, :, None] * keep_z[None, None, :]).reshape(-1)

    def setup(which):
        centre = centers[which]
        local_x = centre // (CY * CZ)
        local_y = (centre // CZ) % CY
        local_z = centre % CZ
        node = ((tile_x * CX + local_x) * NY + tile_y * CY + local_y) * NZ + tile_z * CZ + local_z
        in_use = (rank < live_count[tile, which]).astype(jnp.float32)
        return node.astype(jnp.int32), in_use, cell_mass[which].reshape(-1)

    node_second, use_second, mass_second = setup(1)
    second = reverse_global(final_adjoint, fractions[1], node_second, deform[1], next_affine[1], mass_second, keep_flat, use_second)

    stay_target = jnp.where(prior_slot < PD, tile * PD + prior_slot, NP).astype(jnp.int32)
    carried = jnp.zeros((21, NP + 1), jnp.float32).at[:, stay_target].add(second)
    tiles = jnp.arange(TILES, dtype=jnp.int32)
    own_x = tiles // (TY * TZ)
    own_y = (tiles // TZ) % TY
    own_z = tiles % TZ
    offsets = jnp.asarray(neighbours)
    near_x = jnp.clip(own_x[:, None] + offsets[None, :, 0], 0, TX - 1)
    near_y = jnp.clip(own_y[:, None] + offsets[None, :, 1], 0, TY - 1)
    near_z = jnp.clip(own_z[:, None] + offsets[None, :, 2], 0, TZ - 1)
    near = ((near_x * TY + near_y) * TZ + near_z).astype(jnp.int32)
    positions = jnp.arange(MIG, dtype=jnp.int32)
    valid = positions[None, None] < receive_count[:, :, None]
    source = (tiles[:, None, None] * PD + receive_slot).astype(jnp.int32)
    opposite = (25 - jnp.arange(26, dtype=jnp.int32))
    target_slot = send_slot[near[:, :, None], opposite[None, :, None], positions[None, None, :]]
    target = jnp.where(valid, near[:, :, None] * PD + target_slot, NP).astype(jnp.int32)
    carried = carried.at[:, target.reshape(-1)].add(second[:, source.reshape(-1)])

    node_first, use_first, mass_first = setup(0)
    return reverse_global(carried[:, :NP], fractions[0], node_first, deform[0], next_affine[0], mass_first, keep_flat, use_first)
```

```python
import functools

import jax
import jax.numpy as jnp
from jax import lax
from jax.experimental import pallas as pl
from jax.experimental.pallas import tpu as pltpu
from jax.sharding import PartitionSpec as P

TIME_STEP = 0.2
APIC_SCALE = 4.0
STRESS_SCALE = 0.3
F32 = jnp.float32
BF16 = jnp.bfloat16
I32 = jnp.int32
AXES = ("gx", "gy", "gz")
VMEM = pl.BlockSpec(memory_space=pltpu.VMEM)
SMEM = pl.BlockSpec(memory_space=pltpu.SMEM)
CHUNKS = 8
ZROWS = 144


def contract(a, b, da, db, precision=None):
    return lax.dot_general(
        a, b, (((da,), (db,)), ((), ())), preferred_element_type=F32, precision=precision
    )


def nt(a, b):
    return contract(a, b, 1, 1)


def nn(a, b):
    return contract(a, b, 1, 0)


def split(x):
    hi = x.astype(BF16)
    return hi, (x - hi.astype(F32)).astype(BF16)


def rounded(x):
    hi = x.astype(BF16).astype(F32)
    return hi, x - hi


def spline(f):
    return 0.5 * (0.5 - f) * (0.5 - f), 0.75 - f * f, 0.5 * (0.5 + f) * (0.5 + f)


def iota(shape, axis):
    return lax.broadcasted_iota(I32, shape, axis)


def dense(ref, lead, rows):
    value = ref[lead] if lead is not None else ref[...]
    value = value.reshape(rows, CHUNKS, 128)
    return [value[i] for i in range(rows)]


def axis_tables(fx, cell_x, count):
    low, mid, high = spline(fx)
    plain, signed = [], []
    for plane in range(count):
        is_low, is_mid, is_high = cell_x == plane, cell_x + 1 == plane, cell_x + 2 == plane
        plain.append(jnp.where(is_low, low, jnp.where(is_mid, mid, jnp.where(is_high, high, 0.0))))
        signed.append(jnp.where(is_low, -low, jnp.where(is_high, high, 0.0)))
    return plain, signed


def y_tables(fy, cell_y, chunk):
    low, mid, high = (v[chunk : chunk + 1] for v in spline(fy))
    away = iota((8, 128), 0) - (cell_y[chunk : chunk + 1] + 1)
    plain = jnp.where(away == -1, low, jnp.where(away == 0, mid, jnp.where(away == 1, high, 0.0)))
    signed = jnp.where(away == -1, -low, jnp.where(away == 1, high, 0.0))
    return plain, signed


def build_z(fz, cell_z, w_hi, w_lo, d_hi, d_lo):
    low, mid, high = spline(fz)
    low_h, low_l = rounded(low)
    mid_h, mid_l = rounded(mid)
    high_h, high_l = rounded(high)
    to_low = jnp.where(cell_z == 0, 129, cell_z - 1)
    to_high = cell_z + 1
    inner = iota((128, 128), 0)
    edge = iota((16, 128), 0)
    edge = jnp.where(edge < 2, edge + 128, jnp.where(edge == 2, 0, jnp.where(edge == 3, 127, 999)))
    for chunk in range(CHUNKS):
        at = slice(chunk, chunk + 1)
        lanes = slice(chunk * 128, chunk * 128 + 128)
        for rows, index in ((slice(0, 128), inner), (slice(128, ZROWS), edge)):
            is_low, is_mid, is_high = index == to_low[at], index == cell_z[at], index == to_high[at]
            for plain, signed, (a, b, c) in (
                (w_hi, d_hi, (low_h, mid_h, high_h)),
                (w_lo, d_lo, (low_l, mid_l, high_l)),
            ):
                ends = jnp.where(is_high, c[at], 0.0)
                plain[rows, lanes] = jnp.where(
                    is_low, a[at], jnp.where(is_mid, b[at], ends)
                ).astype(BF16)
                signed[rows, lanes] = jnp.where(is_low, -a[at], ends).astype(BF16)


def cells_of(centre):
    return centre // 512, centre // 128 % 4, centre % 128


def transfer(adj, deform, affine):
    a_v, a_c, a_f = adj[0:3], adj[3:12], adj[12:21]
    b_f, b_c = [], []
    for i in range(3):
        for j in range(3):
            b_f.append(
                a_f[3 * i + j]
                + TIME_STEP * sum(affine[3 * m + i] * a_f[3 * m + j] for m in range(3))
            )
            b_c.append(
                a_c[3 * i + j]
                + TIME_STEP * sum(a_f[3 * i + m] * deform[3 * j + m] for m in range(3))
            )
    return a_v, b_c, b_f


def scatter_rows(a_v, b_c, frac, cell_x, cell_y, l0h, l0l, l2h, l2l):
    base, slope = [], []
    for c in range(3):
        base.append(a_v[c] - APIC_SCALE * sum(b_c[3 * c + j] * frac[j] for j in range(3)))
        slope.append([APIC_SCALE * b_c[3 * c + j] for j in range(3)])
    wx, wx1 = axis_tables(frac[0], cell_x, 6)
    for k in range(CHUNKS):
        at = slice(k, k + 1)
        lanes = slice(k * 128, k * 128 + 128)
        wy, wy1 = y_tables(frac[1], cell_y, k)
        for c in range(3):
            a = wy * base[c][at] + wy1 * slope[c][1][at]
            b = wy * slope[c][0][at]
            d = wy * slope[c][2][at]
            for pair in range(3):
                rows = slice(c * 48 + pair * 16, c * 48 + pair * 16 + 16)
                planes = (2 * pair, 2 * pair + 1)
                l0 = jnp.concatenate([wx[x][at] * a + wx1[x][at] * b for x in planes], axis=0)
                l2 = jnp.concatenate([wx[x][at] * d for x in planes], axis=0)
                l0h[rows, lanes], l0l[rows, lanes] = split(l0)
                l2h[rows, lanes], l2l[rows, lanes] = split(l2)


def scatter_sums(l0h, l0l, l2h, l2l, w_hi, w_lo, d_hi, d_lo):
    inner, edge = slice(0, 128), slice(128, ZROWS)
    terms = ((l0h, w_hi), (l0l, w_hi), (l0h, w_lo), (l2h, d_hi), (l2l, d_hi), (l2h, d_lo))
    core = sum(nt(a[...], b[inner]) for a, b in terms)
    ends = sum(nt(b[edge], a[...]) for a, b in terms)
    return core, ends


def write_planes(ends, width, hb, zu, zd):
    hb[...] = jnp.zeros(hb.shape, F32)
    zu[...] = jnp.zeros(zu.shape, F32)
    zd[...] = jnp.zeros(zd.shape, F32)
    hb[0:1, :width] = ends[0:1]
    hb[1:2, :width] = ends[1:2]
    zu[0:1, :width] = ends[0:1]
    zu[1:2, :width] = ends[3:4]
    zd[0:1, :width] = ends[1:2]
    zd[1:2, :width] = ends[2:3]


def first_kernel(
    live, adjoint, fractions, centers, deform, affine, mass,
    h, hb, zu, zd, bf_out, w_hi, w_lo, d_hi, d_lo,
    l0h, l0l, l2h, l2l,
):
    which = 1
    slots = iota((8, 128), 0) * 128 + iota((8, 128), 1)
    use = (slots < live[0, which]).astype(F32)
    adj = [v * use for v in dense(adjoint, None, 21)]
    frac = dense(fractions, which, 3)
    centre = centers[which : which + 1, :].reshape(CHUNKS, 128)
    cell_x, cell_y, cell_z = cells_of(centre)
    build_z(frac[2], cell_z, w_hi, w_lo, d_hi, d_lo)
    a_v, b_c, b_f = transfer(adj, dense(deform, which, 9), dense(affine, which, 9))
    for i in range(9):
        bf_out[i] = b_f[i]
    scatter_rows(a_v, b_c, frac, cell_x, cell_y, l0h, l0l, l2h, l2l)
    core, ends = scatter_sums(l0h, l0l, l2h, l2l, w_hi, w_lo, d_hi, d_lo)
    h[0:144] = core
    h[144:240] = jnp.zeros((96, 128), F32)
    for s in range(2):
        for x in range(4):
            row = 144 + s * 48 + (x + 1) * 8 + 1
            h[row : row + 4] = mass[s, x]
    lane, row = iota((16, 128), 1), iota((16, 128), 0)
    pick = (((row == 2) & (lane == 0)) | ((row == 3) & (lane == 127))).astype(F32)
    mass_ends = contract(pick, h[144:240], 1, 1, lax.Precision.HIGHEST)
    write_planes(jnp.concatenate([ends, mass_ends], axis=1), 240, hb, zu, zd)


def wide_rows(hb):
    return jnp.concatenate(
        [hb[0:1, :128], hb[0:1, 128:], hb[1:2, :128], hb[1:2, 128:], jnp.zeros((4, 128), F32)], axis=0
    )


def from_wide(rows):
    top = jnp.concatenate([rows[0:1], rows[1:2]], axis=1)
    low = jnp.concatenate([rows[2:3], rows[3:4]], axis=1)
    return jnp.concatenate([top, low, jnp.zeros((6, 256), F32)], axis=0)


def transposed(rows):
    return jnp.concatenate([rows, jnp.zeros((120, 256), F32)], axis=0).T


def z_kernel(comps, h, hb, from_low, from_high, h_out, hb_out, yu, yd):
    low, high = from_low[...], from_high[...]
    pad = jnp.zeros((6, 256), F32)
    halo = hb[...] + jnp.concatenate([high[1:2], low[1:2], pad], axis=0)
    hb_out[...] = halo
    wall = transposed(jnp.concatenate([low[0:1], high[0:1], pad], axis=0))
    lane = iota((8, 128), 1)
    row = iota((8, 128), 0)
    blocks = comps * 6
    up, down = None, None
    for q in range(blocks):
        rows = slice(q * 8, q * 8 + 8)
        tile = (
            h[rows]
            + jnp.where(lane == 0, wall[rows, 0:1], 0.0)
            + jnp.where(lane == 127, wall[rows, 1:2], 0.0)
        )
        h_out[rows] = tile
        place = 2 * (q % 4)
        chosen = (row >= place) & (row < place + 2)
        a = pltpu.roll(tile, (place - 4) % 8, 0) if place != 4 else tile
        b = pltpu.roll(tile, place, 0) if place else tile
        up = jnp.where(chosen, a, 0.0 if up is None else up)
        down = jnp.where(chosen, b, 0.0 if down is None else down)
        if q % 4 == 3 or q == blocks - 1:
            out = slice(q // 4 * 8, q // 4 * 8 + 8)
            yu[out] = up
            yd[out] = down
            up, down = None, None
    packed = (blocks + 3) // 4 * 8
    yu[packed : packed + 8] = wide_rows(halo)
    yd[packed : packed + 8] = wide_rows(halo)


def y_kernel(comps, h, hb, from_low, from_high, h_out, hb_out, xu, xd):
    row = iota((8, 128), 0)
    blocks = comps * 6
    packed = (blocks + 3) // 4 * 8
    for q in range(blocks):
        rows = slice(q * 8, q * 8 + 8)
        place = 2 * (q % 4)
        src = slice(q // 4 * 8, q // 4 * 8 + 8)
        a, b = from_low[src], from_high[src]
        a = pltpu.roll(a, (-place) % 8, 0) if place else a
        b = pltpu.roll(b, (4 - place) % 8, 0) if place != 4 else b
        tile = (
            h[rows] + jnp.where(row < 2, a, 0.0) + jnp.where((row >= 4) & (row < 6), b, 0.0)
        )
        h_out[rows] = tile
        c, x = q // 6, q % 6
        if x >= 4:
            xu[c * 16 + (x - 4) * 8 : c * 16 + (x - 4) * 8 + 8] = tile
        if x < 2:
            xd[c * 16 + x * 8 : c * 16 + x * 8 + 8] = tile
    place = iota((8, 256), 1) % 8
    a = pltpu.roll(from_wide(from_low[packed : packed + 8]), 252, 1)
    b = pltpu.roll(from_wide(from_high[packed : packed + 8]), 4, 1)
    halo = hb[...] + jnp.where(place < 2, a, 0.0) + jnp.where((place >= 4) & (place < 6), b, 0.0)
    hb_out[...] = halo
    xu[comps * 16 : comps * 16 + 8] = wide_rows(halo)
    xd[comps * 16 : comps * 16 + 8] = wide_rows(halo)


def x_fold(comps, h, hb, from_low, from_high, total):
    for c in range(comps):
        total[c * 48 : c * 48 + 16] = h[c * 48 : c * 48 + 16] + from_low[c * 16 : c * 16 + 16]
        total[c * 48 + 16 : c * 48 + 32] = h[c * 48 + 16 : c * 48 + 32]
        total[c * 48 + 32 : c * 48 + 48] = (
            h[c * 48 + 32 : c * 48 + 48] + from_high[c * 16 : c * 16 + 16]
        )
    plane = iota((8, 256), 1) % 48 // 8
    a = pltpu.roll(from_wide(from_low[comps * 16 : comps * 16 + 8]), 224, 1)
    b = pltpu.roll(from_wide(from_high[comps * 16 : comps * 16 + 8]), 32, 1)
    return hb[...] + jnp.where(plane < 2, a, 0.0) + jnp.where(plane >= 4, b, 0.0)


def node_values(spot, extents, total, halo, mass_at, mass_halo, g_hi, g_lo):
    first_x, first_y, first_z = spot[0], spot[1], spot[2]
    lane, row = iota((8, 128), 1), iota((8, 128), 0)
    node_z = first_z + lane
    node_y = first_y + row - 1
    keep_yz = (
        (node_z >= 1) & (node_z <= extents[2] - 2) & (node_y >= 1) & (node_y <= extents[1] - 2)
    )
    wide = iota((8, 256), 1)
    side = iota((8, 256), 0)
    halo_x = first_x + wide % 48 // 8 - 1
    halo_y = first_y + wide % 8 - 1
    halo_z = first_z + jnp.where(side == 0, 128, -1)
    keep = (
        (halo_x >= 1) & (halo_x <= extents[0] - 2)
        & (halo_y >= 1) & (halo_y <= extents[1] - 2)
        & (halo_z >= 1) & (halo_z <= extents[2] - 2)
        & (side < 2) & (wide < 144) & (wide % 8 < 6)
    )
    ends = jnp.where(keep, halo / jnp.where(keep, mass_halo, 1.0), 0.0)
    columns = transposed(ends)
    g_hi[:, 128:256], g_lo[:, 128:256] = split(columns[0:144])
    for x in range(6):
        node_x = first_x + x - 1
        keep_here = keep_yz & (row < 6) & (node_x >= 1) & (node_x <= extents[0] - 2)
        mass = jnp.where(keep_here, mass_at(x), 1.0)
        for c in range(3):
            rows = slice(c * 48 + x * 8, c * 48 + x * 8 + 8)
            total[rows] = jnp.where(keep_here, total[rows] / mass, 0.0)
    g_hi[:, 0:128], g_lo[:, 0:128] = split(total[0:144])


def gather(frac, cell_x, cell_y, g_hi, g_lo, w_hi, w_lo, d_hi, d_lo, s0, sz, rows12):
    a, b = g_hi[:, 0:ZROWS], g_lo[:, 0:ZROWS]
    s0[...] = nn(a, w_hi[...]) + nn(b, w_hi[...]) + nn(a, w_lo[...])
    sz[...] = nn(a, d_hi[...]) + nn(b, d_hi[...]) + nn(a, d_lo[...])
    wx, wx1 = axis_tables(frac[0], cell_x, 6)
    for k in range(CHUNKS):
        at = slice(k, k + 1)
        lanes = slice(k * 128, k * 128 + 128)
        wy, wy1 = y_tables(frac[1], cell_y, k)
        for c in range(3):
            plain = [s0[c * 48 + x * 8 : c * 48 + x * 8 + 8, lanes] for x in range(6)]
            slope = [sz[c * 48 + x * 8 : c * 48 + x * 8 + 8, lanes] for x in range(6)]
            r0 = sum(wx[x][at] * plain[x] for x in range(6))
            r1 = sum(wx1[x][at] * plain[x] for x in range(6))
            rz = sum(wx[x][at] * slope[x] for x in range(6))
            for i, v in enumerate((wy * r0, wy * r1, wy1 * r0, wy * rz)):
                rows12[c * 4 + i, at, :] = jnp.sum(v, axis=0, keepdims=True)


def particle(rows12, frac, b_f, deform, use):
    r_v = [rows12[c * 4] for c in range(3)]
    area = [rows12[c * 4 + 1 + j] - r_v[c] * frac[j] for c in range(3) for j in range(3)]
    stress = [-STRESS_SCALE * v for v in area]
    cof = []
    for i in range(3):
        for j in range(3):
            i1, i2, j1, j2 = (i + 1) % 3, (i + 2) % 3, (j + 1) % 3, (j + 2) % 3
            cof.append(
                deform[3 * i1 + j1] * deform[3 * i2 + j2] - deform[3 * i1 + j2] * deform[3 * i2 + j1]
            )
    det = sum(deform[j] * cof[j] for j in range(3))
    ratio = (stress[0] + stress[4] + stress[8]) / det
    out = r_v + area
    for i in range(3):
        for j in range(3):
            shear = sum((stress[3 * i + m] + stress[3 * m + i]) * deform[3 * m + j] for m in range(3))
            out.append(b_f[3 * i + j] + shear + ratio * cof[3 * i + j])
    return [v * use for v in out]


def gather_first_kernel(
    extents, live, spot, h, hb, from_low, from_high, fractions, centers, deform, bf,
    w_hi, w_lo, d_hi, d_lo, pick,
    second, zu, zd, mid, mass_core, mass_halo,
    total, g_hi, g_lo, s0, sz, rows12, buf, hot,
):
    which = 1
    halo = x_fold(5, h, hb, from_low, from_high, total)
    mass_core[...] = total[144:192]
    wide = iota((8, 256), 1)

    def spread(step):
        start = 144 + step * 48
        out = jnp.ones((8, 256), F32)
        for c in range(3):
            moved = pltpu.roll(halo, (c * 48 - start) % 256, 1)
            out = jnp.where((wide >= c * 48) & (wide < c * 48 + 48), moved, out)
        return out

    mass_halo[...] = spread(0)
    node_values(
        spot, extents, total, halo,
        lambda x: total[192 + x * 8 : 192 + x * 8 + 8], spread(1), g_hi, g_lo,
    )
    frac = dense(fractions, which, 3)
    cell_x, cell_y, _ = cells_of(centers[which : which + 1, :].reshape(CHUNKS, 128))
    gather(frac, cell_x, cell_y, g_hi, g_lo, w_hi, w_lo, d_hi, d_lo, s0, sz, rows12)
    slots = iota((8, 128), 0) * 128 + iota((8, 128), 1)
    use = (slots < live[0, which]).astype(F32)
    out = particle(rows12, frac, [bf[i] for i in range(9)], dense(deform, which, 9), use)
    for i in range(21):
        second[i] = out[i]
        buf[i * 8 : i * 8 + 8] = out[i]
    buf[168:176] = jnp.zeros((8, 128), F32)
    hi, lo = split(buf[...])
    low_row = iota((128, 128), 0)
    row = iota((8, 128), 0)
    for t in range(9):
        index = pick[t : t + 1]
        hot[...] = (low_row == index % 128).astype(F32).astype(BF16)
        got = nn(hi, hot[...]) + nn(lo, hot[...])
        chosen = (row == index // 128) & (index >= 0)
        got = got.reshape(22, 8, 128)[0:21]
        got = jnp.sum(jnp.where(chosen[None], got, 0.0), axis=1)
        dest, place = ((zd, t), (mid, t - 3), (zu, t - 6))[t // 3]
        dest[:, place * 128 : place * 128 + 128] = got


def pieces(groups, at, tiles):
    lane = iota((21, 128), 1)
    out = [jnp.zeros((21, 128), F32) for _ in range(tiles)]
    for i, group in enumerate(groups):
        place = 32 * (i % 4)
        moved = pltpu.roll(group, (place - at) % 128, 1) if place != at else group
        out[i // 4] = jnp.where((lane >= place) & (lane < place + 32), moved, out[i // 4])
    return out


def lane_tile(ref, i):
    return ref[:, i * 128 : i * 128 + 128]


def route_y_kernel(mid, from_low, from_high, yu, yd):
    for i, ref in enumerate((mid, from_low, from_high)):
        yd[:, i * 128 : i * 128 + 128] = lane_tile(ref, 0)
        yu[:, i * 128 : i * 128 + 128] = lane_tile(ref, 2)


def route_x_kernel(mid, z_low, z_high, y_low, y_high, xu, xd, final):
    groups = [lane_tile(mid, 1), lane_tile(z_low, 1), lane_tile(z_high, 1)]
    groups += [lane_tile(y_low, i) for i in range(3)]
    groups += [lane_tile(y_high, i) for i in range(3)]
    for ref, at in ((xd, 0), (xu, 64)):
        for i, tile in enumerate(pieces(groups, at, 3)):
            ref[:, i * 128 : i * 128 + 128] = tile
    for i, tile in enumerate(pieces(groups[1:], 32, 2)):
        final[:, i * 128 : i * 128 + 128] = tile


def second_kernel(
    live, second, final, x_low, x_high, prior, send, fractions, centers, deform, affine,
    h, hb, zu, zd, bf_out, w_hi, w_lo, d_hi, d_lo,
    lh, ll, hot, l0h, l0l, l2h, l2l,
):
    which = 0
    row = iota((8, 128), 0)
    low_row = iota((128, 128), 0)
    moved = [lane_tile(final, 0), lane_tile(final, 1)]
    moved += [lane_tile(x_low, i) for i in range(3)] + [lane_tile(x_high, i) for i in range(3)]
    for t in range(16):
        index = prior[t : t + 1] if t < 8 else send[t - 8 : t - 7]
        lanes = slice(t * 128, t * 128 + 128)
        hot[:, lanes] = (low_row == index % 128).astype(F32).astype(BF16)
        chosen = row == index // 128
        for pair in range(11):
            tiles = []
            for r in (2 * pair, 2 * pair + 1):
                if r > 20:
                    tiles.append(jnp.zeros((8, 128), F32))
                    continue
                value = second[r, t : t + 1, :] if t < 8 else moved[t - 8][r : r + 1]
                tiles.append(jnp.where(chosen, value, 0.0))
            hi, lo = split(jnp.concatenate(tiles, axis=0))
            lh[pair * 16 : pair * 16 + 16, lanes] = hi
            ll[pair * 16 : pair * 16 + 16, lanes] = lo
    carried = nt(lh[...], hot[...]) + nt(ll[...], hot[...])
    slots = iota((8, 128), 0) * 128 + iota((8, 128), 1)
    use = (slots < live[0, which]).astype(F32)
    adj = [carried[i * 8 : i * 8 + 8] * use for i in range(21)]
    frac = dense(fractions, which, 3)
    cell_x, cell_y, cell_z = cells_of(centers[which : which + 1, :].reshape(CHUNKS, 128))
    build_z(frac[2], cell_z, w_hi, w_lo, d_hi, d_lo)
    a_v, b_c, b_f = transfer(adj, dense(deform, which, 9), dense(affine, which, 9))
    for i in range(9):
        bf_out[i] = b_f[i]
    scatter_rows(a_v, b_c, frac, cell_x, cell_y, l0h, l0l, l2h, l2l)
    core, ends = scatter_sums(l0h, l0l, l2h, l2l, w_hi, w_lo, d_hi, d_lo)
    h[...] = core
    write_planes(ends, 144, hb, zu, zd)


def gather_second_kernel(
    extents, live, spot, h, hb, from_low, from_high, fractions, centers, deform, bf,
    w_hi, w_lo, d_hi, d_lo, mass_core, mass_halo,
    result,
    total, g_hi, g_lo, s0, sz, rows12, packed,
):
    which = 0
    halo = x_fold(3, h, hb, from_low, from_high, total)
    node_values(
        spot, extents, total, halo,
        lambda x: mass_core[x * 8 : x * 8 + 8], mass_halo[...], g_hi, g_lo,
    )
    frac = dense(fractions, which, 3)
    cell_x, cell_y, _ = cells_of(centers[which : which + 1, :].reshape(CHUNKS, 128))
    gather(frac, cell_x, cell_y, g_hi, g_lo, w_hi, w_lo, d_hi, d_lo, s0, sz, rows12)
    slots = iota((8, 128), 0) * 128 + iota((8, 128), 1)
    use = (slots < live[0, which]).astype(F32)
    out = particle(rows12, frac, [bf[i] for i in range(9)], dense(deform, which, 9), use)
    for i in range(21):
        packed[i] = out[i]
    for k in range(CHUNKS):
        result[:, k * 128 : k * 128 + 128] = packed[:, k, :]


def shape(*dims, dtype=F32):
    return jax.ShapeDtypeStruct(dims, dtype)


def call(kernel, name, specs, outs, scratch=()):
    return pl.pallas_call(
        kernel,
        name=name,
        in_specs=list(specs),
        out_specs=[VMEM] * len(outs),
        out_shape=list(outs),
        scratch_shapes=[pltpu.VMEM(s, d) for s, d in scratch],
        compiler_params=pltpu.CompilerParams(vmem_limit_bytes=40 * 1024 * 1024),
    )


def both_ways(up, down, axis):
    count = lax.axis_size(axis)
    low = lax.ppermute(up, axis, [(i, i + 1) for i in range(count - 1)])
    high = lax.ppermute(down, axis, [(i + 1, i) for i in range(count - 1)])
    return low, high


def body(
    fractions, centers, deform, next_affine, cell_mass, final_adjoint,
    live_count, send_slot, receive_slot, receive_count, prior_slot,
):
    spot = jnp.stack([lax.axis_index("gx") * 4, lax.axis_index("gy") * 4, lax.axis_index("gz") * 128])
    spot = spot.astype(I32)
    extents = (lax.axis_size("gx") * 4, lax.axis_size("gy") * 4, lax.axis_size("gz") * 128)

    def cube(rows, fill):
        middle = jnp.full((1, 32), fill, I32)
        return jnp.concatenate([rows[:13], middle, rows[13:]]).reshape(3, 3, 3, 32)

    order = jnp.arange(32, dtype=I32)[None]
    chosen = jnp.where(order < receive_count[0][:, None], receive_slot[0], -1)
    pick = jnp.transpose(cube(chosen, -1), (2, 1, 0, 3))
    pick = jnp.concatenate([pick, jnp.full((3, 3, 1, 32), -1, I32)], axis=2).reshape(9, 128)
    back = cube(send_slot[0], 0)[::-1, ::-1, ::-1]
    back = jnp.concatenate([back[:, 1:], back[:, :1]], axis=1)
    back = jnp.concatenate([back[:, :, 1:], back[:, :, :1]], axis=2).reshape(3, 9, 32)
    blank = jnp.zeros((3, 32), I32)
    send = jnp.concatenate([back[1, 1:], back[2], blank, back[0], blank]).reshape(8, 128)
    prior = prior_slot.reshape(8, 128)

    wide = shape(ZROWS, 1024, dtype=BF16)
    weights = [wide] * 4
    lrows = [((144, 1024), BF16)] * 4
    gscratch = [
        ((144, 256), BF16), ((144, 256), BF16),
        ((144, 1024), F32), ((144, 1024), F32), ((12, 8, 128), F32),
    ]

    def fold(comps, h, hb, zu, zd):
        low, high = both_ways(zu, zd, "gz")
        packed = (comps * 6 + 3) // 4 * 8 + 8
        h, hb, yu, yd = call(
            functools.partial(z_kernel, comps), f"fold_z{comps}", [VMEM] * 4,
            [shape(comps * 48, 128), shape(8, 256), shape(packed, 128), shape(packed, 128)],
        )(h, hb, low, high)
        low, high = both_ways(yu, yd, "gy")
        rows = comps * 16 + 8
        h, hb, xu, xd = call(
            functools.partial(y_kernel, comps), f"fold_y{comps}", [VMEM] * 4,
            [shape(comps * 48, 128), shape(8, 256), shape(rows, 128), shape(rows, 128)],
        )(h, hb, low, high)
        low, high = both_ways(xu, xd, "gx")
        return h, hb, low, high

    h, hb, zu, zd, bf, *w = call(
        first_kernel, "scatter_first", [SMEM] + [VMEM] * 6,
        [shape(240, 128), shape(8, 256), shape(2, 256), shape(2, 256), shape(9, 8, 128)] + weights,
        lrows,
    )(live_count, final_adjoint, fractions, centers, deform, next_affine, cell_mass)
    h, hb, low, high = fold(5, h, hb, zu, zd)
    second, zu, zd, mid, mass_core, mass_halo = call(
        functools.partial(gather_first_kernel, extents), "gather_first",
        [SMEM, SMEM] + [VMEM] * 13,
        [shape(21, 8, 128), shape(21, 384), shape(21, 384), shape(21, 384), shape(48, 128), shape(8, 256)],
        [((240, 128), F32)] + gscratch + [((176, 128), F32), ((128, 128), BF16)],
    )(live_count, spot, h, hb, low, high, fractions, centers, deform, bf, *w, pick)

    z_low, z_high = both_ways(zu, zd, "gz")
    yu, yd = call(route_y_kernel, "route_y", [VMEM] * 3, [shape(21, 384)] * 2)(mid, z_low, z_high)
    y_low, y_high = both_ways(yu, yd, "gy")
    xu, xd, final = call(
        route_x_kernel, "route_x", [VMEM] * 5, [shape(21, 384), shape(21, 384), shape(21, 256)]
    )(mid, z_low, z_high, y_low, y_high)
    x_low, x_high = both_ways(xu, xd, "gx")

    h, hb, zu, zd, bf, *w = call(
        second_kernel, "scatter_second", [SMEM] + [VMEM] * 10,
        [shape(144, 128), shape(8, 256), shape(2, 256), shape(2, 256), shape(9, 8, 128)] + weights,
        [((176, 2048), BF16)] * 2 + [((128, 2048), BF16)] + lrows,
    )(live_count, second, final, x_low, x_high, prior, send, fractions, centers, deform, next_affine)
    h, hb, low, high = fold(3, h, hb, zu, zd)
    (result,) = call(
        functools.partial(gather_second_kernel, extents), "gather_second",
        [SMEM, SMEM] + [VMEM] * 14,
        [shape(21, 1024)],
        [((144, 128), F32)] + gscratch + [((21, 8, 128), F32)],
    )(live_count, spot, h, hb, low, high, fractions, centers, deform, bf, *w, mass_core, mass_halo)
    return result


def solution(mesh):
    spread = AXES
    in_specs = (
        P(None, None, spread), P(None, spread), P(None, None, spread), P(None, None, spread),
        P(None, "gx", "gy", "gz"), P(None, spread), P(spread, None), P(spread, None, None),
        P(spread, None, None), P(spread, None), P(spread),
    )
    return jax.shard_map(
        body, mesh=mesh, in_specs=in_specs, out_specs=P(None, spread), check_vma=False
    )
```

```python
import functools

import jax
import jax.numpy as jnp
from jax import lax
from jax.experimental import pallas as pl
from jax.experimental.pallas import tpu as pltpu
from jax.sharding import PartitionSpec as P

TIME_STEP = 0.2
APIC_SCALE = 4.0
STRESS_SCALE = 0.3
F32 = jnp.float32
BF16 = jnp.bfloat16
I32 = jnp.int32
AXES = ("gx", "gy", "gz")
VMEM = pl.BlockSpec(memory_space=pltpu.VMEM)
SMEM = pl.BlockSpec(memory_space=pltpu.SMEM)
CHUNKS = 8
ZROWS = 144


def contract(a, b, da, db, precision=None):
    return lax.dot_general(
        a, b, (((da,), (db,)), ((), ())), preferred_element_type=F32, precision=precision
    )


def nt(a, b):
    return contract(a, b, 1, 1)


def nn(a, b):
    return contract(a, b, 1, 0)


def split(x):
    hi = x.astype(BF16)
    return hi, (x - hi.astype(F32)).astype(BF16)


def rounded(x):
    hi = x.astype(BF16).astype(F32)
    return hi, x - hi


def spline(f):
    return 0.5 * (0.5 - f) * (0.5 - f), 0.75 - f * f, 0.5 * (0.5 + f) * (0.5 + f)


def iota(shape, axis):
    return lax.broadcasted_iota(I32, shape, axis)


def dense(ref, lead, rows):
    value = ref[lead] if lead is not None else ref[...]
    value = value.reshape(rows, CHUNKS, 128)
    return [value[i] for i in range(rows)]


def axis_tables(fx, cell_x, count):
    low, mid, high = spline(fx)
    plain, signed = [], []
    for plane in range(count):
        is_low, is_mid, is_high = cell_x == plane, cell_x + 1 == plane, cell_x + 2 == plane
        plain.append(jnp.where(is_low, low, jnp.where(is_mid, mid, jnp.where(is_high, high, 0.0))))
        signed.append(jnp.where(is_low, -low, jnp.where(is_high, high, 0.0)))
    return plain, signed


def y_tables(fy, cell_y, chunk):
    low, mid, high = (v[chunk : chunk + 1] for v in spline(fy))
    away = iota((8, 128), 0) - (cell_y[chunk : chunk + 1] + 1)
    plain = jnp.where(away == -1, low, jnp.where(away == 0, mid, jnp.where(away == 1, high, 0.0)))
    signed = jnp.where(away == -1, -low, jnp.where(away == 1, high, 0.0))
    return plain, signed


def build_z(fz, cell_z, w_hi, w_lo, d_hi, d_lo, chunks=CHUNKS, edges_only=False):
    low, mid, high = spline(fz)
    low_h, low_l = rounded(low)
    mid_h, mid_l = rounded(mid)
    high_h, high_l = rounded(high)
    to_low = jnp.where(cell_z == 0, 129, cell_z - 1)
    to_high = cell_z + 1
    inner = iota((128, 128), 0)
    edge = iota((16, 128), 0)
    edge = jnp.where(edge < 2, edge + 128, jnp.where(edge == 2, 0, jnp.where(edge == 3, 127, 999)))
    parts = ((slice(0, 128), inner), (slice(128, ZROWS), edge))
    if edges_only:
        parts = ((slice(0, 16), edge),)
    for chunk in range(chunks):
        at = slice(chunk, chunk + 1)
        lanes = slice(chunk * 128, chunk * 128 + 128)
        for rows, index in parts:
            is_low, is_mid, is_high = index == to_low[at], index == cell_z[at], index == to_high[at]
            for plain, signed, (a, b, c) in (
                (w_hi, d_hi, (low_h, mid_h, high_h)),
                (w_lo, d_lo, (low_l, mid_l, high_l)),
            ):
                ends = jnp.where(is_high, c[at], 0.0)
                plain[rows, lanes] = jnp.where(
                    is_low, a[at], jnp.where(is_mid, b[at], ends)
                ).astype(BF16)
                signed[rows, lanes] = jnp.where(is_low, -a[at], ends).astype(BF16)


def cells_of(centre):
    return centre // 512, centre // 128 % 4, centre % 128


def to_grid(adj, deform):
    a_v, a_c, a_f = adj[0:3], adj[3:12], adj[12:21]
    b_c = [
        a_c[3 * i + j] + TIME_STEP * sum(a_f[3 * i + m] * deform[3 * j + m] for m in range(3))
        for i in range(3)
        for j in range(3)
    ]
    return a_v, b_c


def transfer(adj, deform, affine):
    a_v, b_c = to_grid(adj, deform)
    a_f = adj[12:21]
    b_f = [
        a_f[3 * i + j] + TIME_STEP * sum(affine[3 * m + i] * a_f[3 * m + j] for m in range(3))
        for i in range(3)
        for j in range(3)
    ]
    return a_v, b_c, b_f


def scatter_rows(a_v, b_c, frac, cell_x, cell_y, l0h, l0l, l2h, l2l, chunks=CHUNKS):
    base, slope = [], []
    for c in range(3):
        base.append(a_v[c] - APIC_SCALE * sum(b_c[3 * c + j] * frac[j] for j in range(3)))
        slope.append([APIC_SCALE * b_c[3 * c + j] for j in range(3)])
    wx, wx1 = axis_tables(frac[0], cell_x, 6)
    for k in range(chunks):
        at = slice(k, k + 1)
        lanes = slice(k * 128, k * 128 + 128)
        wy, wy1 = y_tables(frac[1], cell_y, k)
        for c in range(3):
            a = wy * base[c][at] + wy1 * slope[c][1][at]
            b = wy * slope[c][0][at]
            d = wy * slope[c][2][at]
            for pair in range(3):
                rows = slice(c * 48 + pair * 16, c * 48 + pair * 16 + 16)
                planes = (2 * pair, 2 * pair + 1)
                l0 = jnp.concatenate([wx[x][at] * a + wx1[x][at] * b for x in planes], axis=0)
                l2 = jnp.concatenate([wx[x][at] * d for x in planes], axis=0)
                l0h[rows, lanes], l0l[rows, lanes] = split(l0)
                l2h[rows, lanes], l2l[rows, lanes] = split(l2)


def paired(l, w):
    l0h, l0l, l2h, l2l = l
    w_hi, w_lo, d_hi, d_lo = w
    return ((l0h, w_hi), (l0l, w_hi), (l0h, w_lo), (l2h, d_hi), (l2l, d_hi), (l2h, d_lo))


def core_sums(l, w):
    return sum(nt(a[...], b[0:128]) for a, b in paired(l, w))


def edge_sums(l, w, rows=slice(128, ZROWS), lanes=slice(0, 1024)):
    return sum(nt(b[rows, lanes], a[:, lanes]) for a, b in paired(l, w))


def put_planes(ref, at, first, second):
    width = first.shape[1]
    ref[at : at + 1, :width] = first
    ref[at + 1 : at + 2, :width] = second


def static_rows(table, send, start, hot, dest):
    hi, lo = split(table[...])
    low_row, row = iota((128, 128), 0), iota((8, 128), 0)
    for t in range(3):
        index = send[start + t : start + t + 1]
        hot[...] = (low_row == index % 128).astype(F32).astype(BF16)
        got = (nn(hi, hot[...]) + nn(lo, hot[...])).reshape(14, 8, 128)
        chosen = row == index // 128
        dest[0:14, t * 128 : t * 128 + 128] = jnp.sum(jnp.where(chosen[None], got, 0.0), axis=1)


def first_kernel(
    live, adjoint, fractions, centers, deform, affine, mass, send,
    h, hb, zu, zd, bf_out, w_hi, w_lo, d_hi, d_lo,
    l0h, l0l, l2h, l2l, table, hot,
):
    table[104:112] = jnp.zeros((8, 128), F32)
    early = dense(fractions, 0, 3) + [centers[0:1, :].reshape(CHUNKS, 128).astype(F32)]
    for i, tile in enumerate(early + dense(deform, 0, 9)):
        table[i * 8 : i * 8 + 8] = tile
    zu[...] = jnp.zeros(zu.shape, F32)
    zd[...] = jnp.zeros(zd.shape, F32)
    static_rows(table, send, 2, hot, zd)
    static_rows(table, send, 5, hot, zu)
    which = 1
    slots = iota((8, 128), 0) * 128 + iota((8, 128), 1)
    use = (slots < live[0, which]).astype(F32)
    adj = [v * use for v in dense(adjoint, None, 21)]
    frac = dense(fractions, which, 3)
    centre = centers[which : which + 1, :].reshape(CHUNKS, 128)
    cell_x, cell_y, cell_z = cells_of(centre)
    w = (w_hi, w_lo, d_hi, d_lo)
    l = (l0h, l0l, l2h, l2l)
    build_z(frac[2], cell_z, *w)
    a_v, b_c, b_f = transfer(adj, dense(deform, which, 9), dense(affine, which, 9))
    for i in range(9):
        bf_out[i] = b_f[i]
    scatter_rows(a_v, b_c, frac, cell_x, cell_y, *l)
    h[0:144] = core_sums(l, w)
    h[144:240] = jnp.zeros((96, 128), F32)
    for s in range(2):
        for x in range(4):
            row = 144 + s * 48 + (x + 1) * 8 + 1
            h[row : row + 4] = mass[s, x]
    lane, row = iota((16, 128), 1), iota((16, 128), 0)
    pick = (((row == 2) & (lane == 0)) | ((row == 3) & (lane == 127))).astype(F32)
    mass_ends = contract(pick, h[144:240], 1, 1, lax.Precision.HIGHEST)
    ends = jnp.concatenate([edge_sums(l, w), mass_ends], axis=1)
    hb[...] = jnp.zeros(hb.shape, F32)
    put_planes(hb, 0, ends[0:1], ends[1:2])
    put_planes(zu, 13, ends[0:1], ends[3:4])
    put_planes(zd, 13, ends[1:2], ends[2:3])


def wide_rows(hb):
    return jnp.concatenate(
        [hb[0:1, :128], hb[0:1, 128:], hb[1:2, :128], hb[1:2, 128:], jnp.zeros((4, 128), F32)], axis=0
    )


def from_wide(rows):
    top = jnp.concatenate([rows[0:1], rows[1:2]], axis=1)
    low = jnp.concatenate([rows[2:3], rows[3:4]], axis=1)
    return jnp.concatenate([top, low, jnp.zeros((6, 256), F32)], axis=0)


def transposed(rows):
    return jnp.concatenate([rows, jnp.zeros((120, 256), F32)], axis=0).T


def z_kernel(comps, h, hb, from_low, from_high, h_out, hb_out, yu, yd):
    z_fold(
        comps, h, hb[...], from_low[13:15, 0:256], from_high[13:15, 0:256], h_out, hb_out, yu, yd
    )


def z_fold(comps, h, halo, low, high, h_out, hb_out, yu, yd):
    pad = jnp.zeros((6, 256), F32)
    halo = halo + jnp.concatenate([high[1:2], low[1:2], pad], axis=0)
    hb_out[...] = halo
    wall = transposed(jnp.concatenate([low[0:1], high[0:1], pad], axis=0))
    lane = iota((8, 128), 1)
    row = iota((8, 128), 0)
    blocks = comps * 6
    up, down = None, None
    for q in range(blocks):
        rows = slice(q * 8, q * 8 + 8)
        tile = (
            h[rows]
            + jnp.where(lane == 0, wall[rows, 0:1], 0.0)
            + jnp.where(lane == 127, wall[rows, 1:2], 0.0)
        )
        h_out[rows] = tile
        place = 2 * (q % 4)
        chosen = (row >= place) & (row < place + 2)
        a = pltpu.roll(tile, (place - 4) % 8, 0) if place != 4 else tile
        b = pltpu.roll(tile, place, 0) if place else tile
        up = jnp.where(chosen, a, 0.0 if up is None else up)
        down = jnp.where(chosen, b, 0.0 if down is None else down)
        if q % 4 == 3 or q == blocks - 1:
            out = slice(q // 4 * 8, q // 4 * 8 + 8)
            yu[out] = up
            yd[out] = down
            up, down = None, None
    packed = (blocks + 3) // 4 * 8
    yu[packed : packed + 8] = wide_rows(halo)
    yd[packed : packed + 8] = wide_rows(halo)


def y_kernel(comps, h, hb, from_low, from_high, h_out, hb_out, xu, xd):
    row = iota((8, 128), 0)
    blocks = comps * 6
    packed = (blocks + 3) // 4 * 8
    for q in range(blocks):
        rows = slice(q * 8, q * 8 + 8)
        place = 2 * (q % 4)
        src = slice(q // 4 * 8, q // 4 * 8 + 8)
        a, b = from_low[src], from_high[src]
        a = pltpu.roll(a, (-place) % 8, 0) if place else a
        b = pltpu.roll(b, (4 - place) % 8, 0) if place != 4 else b
        tile = (
            h[rows] + jnp.where(row < 2, a, 0.0) + jnp.where((row >= 4) & (row < 6), b, 0.0)
        )
        h_out[rows] = tile
        c, x = q // 6, q % 6
        if x >= 4:
            xu[c * 16 + (x - 4) * 8 : c * 16 + (x - 4) * 8 + 8] = tile
        if x < 2:
            xd[c * 16 + x * 8 : c * 16 + x * 8 + 8] = tile
    place = iota((8, 256), 1) % 8
    a = pltpu.roll(from_wide(from_low[packed : packed + 8]), 252, 1)
    b = pltpu.roll(from_wide(from_high[packed : packed + 8]), 4, 1)
    halo = hb[...] + jnp.where(place < 2, a, 0.0) + jnp.where((place >= 4) & (place < 6), b, 0.0)
    hb_out[...] = halo
    xu[comps * 16 : comps * 16 + 8] = wide_rows(halo)
    xd[comps * 16 : comps * 16 + 8] = wide_rows(halo)


def x_fold(comps, h, hb, from_low, from_high, total):
    for c in range(comps):
        total[c * 48 : c * 48 + 16] = h[c * 48 : c * 48 + 16] + from_low[c * 16 : c * 16 + 16]
        total[c * 48 + 16 : c * 48 + 32] = h[c * 48 + 16 : c * 48 + 32]
        total[c * 48 + 32 : c * 48 + 48] = (
            h[c * 48 + 32 : c * 48 + 48] + from_high[c * 16 : c * 16 + 16]
        )
    plane = iota((8, 256), 1) % 48 // 8
    a = pltpu.roll(from_wide(from_low[comps * 16 : comps * 16 + 8]), 224, 1)
    b = pltpu.roll(from_wide(from_high[comps * 16 : comps * 16 + 8]), 32, 1)
    return hb[...] + jnp.where(plane < 2, a, 0.0) + jnp.where(plane >= 4, b, 0.0)


def node_values(spot, extents, total, halo, mass_at, mass_halo, g_hi, g_lo):
    first_x, first_y, first_z = spot[0], spot[1], spot[2]
    lane, row = iota((8, 128), 1), iota((8, 128), 0)
    node_z = first_z + lane
    node_y = first_y + row - 1
    keep_yz = (
        (node_z >= 1) & (node_z <= extents[2] - 2) & (node_y >= 1) & (node_y <= extents[1] - 2)
    )
    wide = iota((8, 256), 1)
    side = iota((8, 256), 0)
    halo_x = first_x + wide % 48 // 8 - 1
    halo_y = first_y + wide % 8 - 1
    halo_z = first_z + jnp.where(side == 0, 128, -1)
    keep = (
        (halo_x >= 1) & (halo_x <= extents[0] - 2)
        & (halo_y >= 1) & (halo_y <= extents[1] - 2)
        & (halo_z >= 1) & (halo_z <= extents[2] - 2)
        & (side < 2) & (wide < 144) & (wide % 8 < 6)
    )
    ends = jnp.where(keep, halo / jnp.where(keep, mass_halo, 1.0), 0.0)
    columns = transposed(ends)
    g_hi[:, 128:256], g_lo[:, 128:256] = split(columns[0:144])
    for x in range(6):
        node_x = first_x + x - 1
        keep_here = keep_yz & (row < 6) & (node_x >= 1) & (node_x <= extents[0] - 2)
        mass = jnp.where(keep_here, mass_at(x), 1.0)
        for c in range(3):
            rows = slice(c * 48 + x * 8, c * 48 + x * 8 + 8)
            total[rows] = jnp.where(keep_here, total[rows] / mass, 0.0)
    g_hi[:, 0:128], g_lo[:, 0:128] = split(total[0:144])


def gather(frac, cell_x, cell_y, g_hi, g_lo, w_hi, w_lo, d_hi, d_lo, s0, sz, rows12):
    a, b = g_hi[:, 0:ZROWS], g_lo[:, 0:ZROWS]
    s0[...] = nn(a, w_hi[...]) + nn(b, w_hi[...]) + nn(a, w_lo[...])
    sz[...] = nn(a, d_hi[...]) + nn(b, d_hi[...]) + nn(a, d_lo[...])
    wx, wx1 = axis_tables(frac[0], cell_x, 6)
    for k in range(CHUNKS):
        at = slice(k, k + 1)
        lanes = slice(k * 128, k * 128 + 128)
        wy, wy1 = y_tables(frac[1], cell_y, k)
        for c in range(3):
            plain = [s0[c * 48 + x * 8 : c * 48 + x * 8 + 8, lanes] for x in range(6)]
            slope = [sz[c * 48 + x * 8 : c * 48 + x * 8 + 8, lanes] for x in range(6)]
            r0 = sum(wx[x][at] * plain[x] for x in range(6))
            r1 = sum(wx1[x][at] * plain[x] for x in range(6))
            rz = sum(wx[x][at] * slope[x] for x in range(6))
            for i, v in enumerate((wy * r0, wy * r1, wy1 * r0, wy * rz)):
                rows12[c * 4 + i, at, :] = jnp.sum(v, axis=0, keepdims=True)


def particle(rows12, frac, b_f, deform, use):
    r_v = [rows12[c * 4] for c in range(3)]
    area = [rows12[c * 4 + 1 + j] - r_v[c] * frac[j] for c in range(3) for j in range(3)]
    stress = [-STRESS_SCALE * v for v in area]
    cof = []
    for i in range(3):
        for j in range(3):
            i1, i2, j1, j2 = (i + 1) % 3, (i + 2) % 3, (j + 1) % 3, (j + 2) % 3
            cof.append(
                deform[3 * i1 + j1] * deform[3 * i2 + j2] - deform[3 * i1 + j2] * deform[3 * i2 + j1]
            )
    det = sum(deform[j] * cof[j] for j in range(3))
    ratio = (stress[0] + stress[4] + stress[8]) / det
    out = r_v + area
    for i in range(3):
        for j in range(3):
            shear = sum((stress[3 * i + m] + stress[3 * m + i]) * deform[3 * m + j] for m in range(3))
            out.append(b_f[3 * i + j] + shear + ratio * cof[3 * i + j])
    return [v * use for v in out]


def gather_first_kernel(
    extents, live, spot, h, hb, from_low, from_high, fractions, centers, deform, bf,
    w_hi, w_lo, d_hi, d_lo, pick,
    second, xu, xd, mid, mass_core, mass_halo,
    total, g_hi, g_lo, s0, sz, rows12, buf, hot,
):
    which = 1
    halo = x_fold(5, h, hb, from_low, from_high, total)
    mass_core[...] = total[144:192]
    wide = iota((8, 256), 1)

    def spread(step):
        start = 144 + step * 48
        out = jnp.ones((8, 256), F32)
        for c in range(3):
            moved = pltpu.roll(halo, (c * 48 - start) % 256, 1)
            out = jnp.where((wide >= c * 48) & (wide < c * 48 + 48), moved, out)
        return out

    mass_halo[...] = spread(0)
    node_values(
        spot, extents, total, halo,
        lambda x: total[192 + x * 8 : 192 + x * 8 + 8], spread(1), g_hi, g_lo,
    )
    frac = dense(fractions, which, 3)
    cell_x, cell_y, _ = cells_of(centers[which : which + 1, :].reshape(CHUNKS, 128))
    gather(frac, cell_x, cell_y, g_hi, g_lo, w_hi, w_lo, d_hi, d_lo, s0, sz, rows12)
    slots = iota((8, 128), 0) * 128 + iota((8, 128), 1)
    use = (slots < live[0, which]).astype(F32)
    out = particle(rows12, frac, [bf[i] for i in range(9)], dense(deform, which, 9), use)
    for i in range(21):
        second[i] = out[i]
        buf[i * 8 : i * 8 + 8] = out[i]
    buf[168:176] = jnp.zeros((8, 128), F32)
    hi, lo = split(buf[...])
    low_row = iota((128, 128), 0)
    row = iota((8, 128), 0)
    for t in range(9):
        index = pick[t : t + 1]
        hot[...] = (low_row == index % 128).astype(F32).astype(BF16)
        got = nn(hi, hot[...]) + nn(lo, hot[...])
        chosen = (row == index // 128) & (index >= 0)
        got = got.reshape(22, 8, 128)[0:21]
        got = jnp.sum(jnp.where(chosen[None], got, 0.0), axis=1)
        dest, place = ((xd, t), (mid, t - 3), (xu, t - 6))[t // 3]
        dest[:, place * 128 : place * 128 + 128] = got


def pieces(groups, at, tiles):
    lane = iota((21, 128), 1)
    out = [jnp.zeros((21, 128), F32) for _ in range(tiles)]
    for i, group in enumerate(groups):
        place = 32 * (i % 4)
        moved = pltpu.roll(group, (place - at) % 128, 1) if place != at else group
        out[i // 4] = jnp.where((lane >= place) & (lane < place + 32), moved, out[i // 4])
    return out


def lane_tile(ref, i):
    return ref[:, i * 128 : i * 128 + 128]


def route_y_kernel(mid, from_low, from_high, yu, yd):
    for i, ref in enumerate((mid, from_low, from_high)):
        yd[:, i * 128 : i * 128 + 128] = lane_tile(ref, 0)
        yu[:, i * 128 : i * 128 + 128] = lane_tile(ref, 2)


def carry(tiles, indices, lh, ll, hot):
    row, low_row = iota((8, 128), 0), iota((128, 128), 0)
    for t, (values, index) in enumerate(zip(tiles, indices)):
        lanes = slice(t * 128, t * 128 + 128)
        hot[:, lanes] = (low_row == index % 128).astype(F32).astype(BF16)
        chosen = row == index // 128
        for pair in range(11):
            both = []
            for r in (2 * pair, 2 * pair + 1):
                blank = jnp.zeros((8, 128), F32)
                both.append(blank if r > 20 else jnp.where(chosen, values(r), 0.0))
            rows = slice(pair * 16, pair * 16 + 16)
            lh[rows, lanes], ll[rows, lanes] = split(jnp.concatenate(both, axis=0))
    return nt(lh[...], hot[...]) + nt(ll[...], hot[...])


def weights_kernel(fractions, centers, w_hi, w_lo, d_hi, d_lo):
    _, _, cell_z = cells_of(centers[0:1, :].reshape(CHUNKS, 128))
    build_z(dense(fractions, 0, 3)[2], cell_z, w_hi, w_lo, d_hi, d_lo)


def near_kernel(
    live, mid, x_low, x_high, y_low, y_high, second, prior, send,
    static_low, static_high, fractions, centers, deform, w_hi, w_lo, d_hi, d_lo,
    zu, zd, up2, dn2, own_low, own_high, carried,
    lh, ll, hot, l0h, l0l, l2h, l2l, moved, static, e0, e1, e2, e3,
):
    groups = [lane_tile(mid, 1), lane_tile(x_low, 1), lane_tile(x_high, 1)]
    groups += [lane_tile(y_low, i) for i in range(3)]
    groups += [lane_tile(y_high, i) for i in range(3)]
    final = pieces(groups[1:], 32, 2)
    moved[...] = jnp.zeros(moved.shape, F32)
    static[...] = jnp.zeros(static.shape, F32)
    zu[...] = jnp.zeros(zu.shape, F32)
    zd[...] = jnp.zeros(zd.shape, F32)
    for ref, at, first, known in ((zu, 64, 0, static_high), (zd, 0, 3, static_low)):
        for i, tile in enumerate(pieces(groups, at, 3)):
            ref[0:21, i * 128 : i * 128 + 128] = tile
            moved[:, first + i, :] = tile
            static[:, first + i, :] = known[0:14, i * 128 : i * 128 + 128]
    l = (l0h, l0l, l2h, l2l)
    e = (e0, e1, e2, e3)

    place = [static[i] for i in range(3)]
    cell_x, cell_y, cell_z = cells_of((static[3] + 0.5).astype(I32))
    build_z(place[2], cell_z, *e, chunks=6, edges_only=True)
    a_v, b_c = to_grid([moved[i] for i in range(21)], [static[4 + i] for i in range(9)])
    scatter_rows(a_v, b_c, place, cell_x, cell_y, *l, chunks=6)
    upward = edge_sums(l, e, slice(0, 16), slice(0, 384))
    downward = edge_sums(l, e, slice(0, 16), slice(384, 768))
    for ref in (up2, dn2, own_low, own_high):
        ref[...] = jnp.zeros(ref.shape, F32)
    put_planes(up2, 0, upward[0:1], upward[3:4])
    put_planes(own_high, 0, upward[1:2], upward[2:3])
    put_planes(own_low, 0, downward[0:1], downward[3:4])
    put_planes(dn2, 0, downward[1:2], downward[2:3])

    tiles = [lambda r, t=t: second[r, t : t + 1, :] for t in range(8)]
    tiles += [lambda r, t=t: final[t][r : r + 1] for t in range(2)]
    indices = [prior[t : t + 1] for t in range(8)] + [send[t : t + 1] for t in range(2)]
    total = carry(tiles, indices, lh, ll, hot)
    slots = iota((8, 128), 0) * 128 + iota((8, 128), 1)
    use = (slots < live[0, 0]).astype(F32)
    adj = [total[i * 8 : i * 8 + 8] * use for i in range(21)]
    for i in range(21):
        carried[i] = adj[i]
    frac = dense(fractions, 0, 3)
    cell_x, cell_y, _ = cells_of(centers[0:1, :].reshape(CHUNKS, 128))
    a_v, b_c = to_grid(adj, dense(deform, 0, 9))
    scatter_rows(a_v, b_c, frac, cell_x, cell_y, *l)
    ends = edge_sums(l, (w_hi, w_lo, d_hi, d_lo))
    put_planes(zu, 21, ends[0:1], ends[3:4])
    put_planes(zd, 21, ends[1:2], ends[2:3])


def second_kernel(
    live, carried, z_low, z_high, low2, high2, own_low, own_high, send,
    fractions, centers, deform, affine, w_hi, w_lo, d_hi, d_lo,
    h_out, hb_out, yu, yd, bf_out,
    lh, ll, hot, l0h, l0l, l2h, l2l, h,
):
    tiles = [lambda r, t=t: z_low[r : r + 1, t * 128 : t * 128 + 128] for t in range(3)]
    tiles += [lambda r, t=t: z_high[r : r + 1, t * 128 : t * 128 + 128] for t in range(3)]
    total = carry(tiles, [send[t : t + 1] for t in range(2, 8)], lh, ll, hot)
    slots = iota((8, 128), 0) * 128 + iota((8, 128), 1)
    use = (slots < live[0, 0]).astype(F32)
    adj = [(carried[i] + total[i * 8 : i * 8 + 8]) * use for i in range(21)]
    frac = dense(fractions, 0, 3)
    cell_x, cell_y, _ = cells_of(centers[0:1, :].reshape(CHUNKS, 128))
    a_v, b_c, b_f = transfer(adj, dense(deform, 0, 9), dense(affine, 0, 9))
    for i in range(9):
        bf_out[i] = b_f[i]
    l = (l0h, l0l, l2h, l2l)
    w = (w_hi, w_lo, d_hi, d_lo)
    scatter_rows(a_v, b_c, frac, cell_x, cell_y, *l)
    h[...] = core_sums(l, w)
    ends = jnp.concatenate([edge_sums(l, w)[0:8], jnp.zeros((8, 112), F32)], axis=1)
    halo = jnp.where(iota((8, 256), 0) < 2, ends, 0.0)
    low = z_low[21:23, 0:256] + low2[0:2] + own_low[0:2]
    high = z_high[21:23, 0:256] + high2[0:2] + own_high[0:2]
    z_fold(3, h, halo, low, high, h_out, hb_out, yu, yd)


def gather_second_kernel(
    extents, live, spot, h, hb, from_low, from_high, fractions, centers, deform, bf,
    w_hi, w_lo, d_hi, d_lo, mass_core, mass_halo,
    result,
    total, g_hi, g_lo, s0, sz, rows12, packed,
):
    which = 0
    halo = x_fold(3, h, hb, from_low, from_high, total)
    node_values(
        spot, extents, total, halo,
        lambda x: mass_core[x * 8 : x * 8 + 8], mass_halo[...], g_hi, g_lo,
    )
    frac = dense(fractions, which, 3)
    cell_x, cell_y, _ = cells_of(centers[which : which + 1, :].reshape(CHUNKS, 128))
    gather(frac, cell_x, cell_y, g_hi, g_lo, w_hi, w_lo, d_hi, d_lo, s0, sz, rows12)
    slots = iota((8, 128), 0) * 128 + iota((8, 128), 1)
    use = (slots < live[0, which]).astype(F32)
    out = particle(rows12, frac, [bf[i] for i in range(9)], dense(deform, which, 9), use)
    for i in range(21):
        packed[i] = out[i]
    for k in range(CHUNKS):
        result[:, k * 128 : k * 128 + 128] = packed[:, k, :]


def shape(*dims, dtype=F32):
    return jax.ShapeDtypeStruct(dims, dtype)


def call(kernel, name, specs, outs, scratch=()):
    return pl.pallas_call(
        kernel,
        name=name,
        in_specs=list(specs),
        out_specs=[VMEM] * len(outs),
        out_shape=list(outs),
        scratch_shapes=[pltpu.VMEM(s, d) for s, d in scratch],
        compiler_params=pltpu.CompilerParams(vmem_limit_bytes=40 * 1024 * 1024),
    )


def both_ways(up, down, axis, step=1):
    count = lax.axis_size(axis)
    low = lax.ppermute(up, axis, [(i, i + step) for i in range(count - step)])
    high = lax.ppermute(down, axis, [(i + step, i) for i in range(count - step)])
    return low, high


def body(
    fractions, centers, deform, next_affine, cell_mass, final_adjoint,
    live_count, send_slot, receive_slot, receive_count, prior_slot,
):
    spot = jnp.stack([lax.axis_index("gx") * 4, lax.axis_index("gy") * 4, lax.axis_index("gz") * 128])
    spot = spot.astype(I32)
    extents = (lax.axis_size("gx") * 4, lax.axis_size("gy") * 4, lax.axis_size("gz") * 128)

    def cube(rows, fill):
        middle = jnp.full((1, 32), fill, I32)
        return jnp.concatenate([rows[:13], middle, rows[13:]]).reshape(3, 3, 3, 32)

    order = jnp.arange(32, dtype=I32)[None]
    chosen = jnp.where(order < receive_count[0][:, None], receive_slot[0], -1)
    pick = cube(chosen, -1)
    pick = jnp.concatenate([pick, jnp.full((3, 3, 1, 32), -1, I32)], axis=2).reshape(9, 128)
    back = jnp.transpose(cube(send_slot[0], 0)[::-1, ::-1, ::-1], (2, 1, 0, 3))
    back = jnp.concatenate([back[:, 1:], back[:, :1]], axis=1)
    back = jnp.concatenate([back[:, :, 1:], back[:, :, :1]], axis=2).reshape(3, 9, 32)
    blank = jnp.zeros((3, 32), I32)
    send = jnp.concatenate([back[1, 1:], back[2], blank, back[0], blank]).reshape(8, 128)
    prior = prior_slot.reshape(8, 128)

    wide = shape(ZROWS, 1024, dtype=BF16)
    weights = [wide] * 4
    lrows = [((144, 1024), BF16)] * 4
    gscratch = [
        ((144, 256), BF16), ((144, 256), BF16),
        ((144, 1024), F32), ((144, 1024), F32), ((12, 8, 128), F32),
    ]

    def fold(comps, h, hb, yu, yd):
        low, high = both_ways(yu, yd, "gy")
        rows = comps * 16 + 8
        h, hb, xu, xd = call(
            functools.partial(y_kernel, comps), f"fold_y{comps}", [VMEM] * 4,
            [shape(comps * 48, 128), shape(8, 256), shape(rows, 128), shape(rows, 128)],
        )(h, hb, low, high)
        low, high = both_ways(xu, xd, "gx")
        return h, hb, low, high

    h, hb, zu, zd, bf, *w = call(
        first_kernel, "scatter_first", [SMEM] + [VMEM] * 7,
        [shape(240, 128), shape(8, 256), shape(16, 384), shape(16, 384), shape(9, 8, 128)] + weights,
        lrows + [((112, 128), F32), ((128, 128), BF16)],
    )(live_count, final_adjoint, fractions, centers, deform, next_affine, cell_mass, send)
    static_low, static_high = both_ways(zu, zd, "gz")
    h, hb, yu, yd = call(
        functools.partial(z_kernel, 5), "fold_z5", [VMEM] * 4,
        [shape(240, 128), shape(8, 256), shape(72, 128), shape(72, 128)],
    )(h, hb, static_low, static_high)
    h, hb, low, high = fold(5, h, hb, yu, yd)
    second, xu, xd, mid, mass_core, mass_halo = call(
        functools.partial(gather_first_kernel, extents), "gather_first",
        [SMEM, SMEM] + [VMEM] * 13,
        [shape(21, 8, 128), shape(21, 384), shape(21, 384), shape(21, 384), shape(48, 128), shape(8, 256)],
        [((240, 128), F32)] + gscratch + [((176, 128), F32), ((128, 128), BF16)],
    )(live_count, spot, h, hb, low, high, fractions, centers, deform, bf, *w, pick)

    w = call(weights_kernel, "weights_second", [VMEM] * 2, weights)(fractions, centers)
    x_low, x_high = both_ways(xu, xd, "gx")
    yu, yd = call(route_y_kernel, "route_y", [VMEM] * 3, [shape(21, 384)] * 2)(mid, x_low, x_high)
    y_low, y_high = both_ways(yu, yd, "gy")
    zu, zd, up2, dn2, own_low, own_high, carried = call(
        near_kernel, "scatter_near", [SMEM] + [VMEM] * 17,
        [shape(24, 384)] * 2 + [shape(2, 256)] * 4 + [shape(21, 8, 128)],
        [((176, 1280), BF16)] * 2 + [((128, 1280), BF16)] + lrows
        + [((21, 8, 128), F32), ((14, 8, 128), F32)] + [((16, 768), BF16)] * 4,
    )(
        live_count, mid, x_low, x_high, y_low, y_high, second, prior, send,
        static_low, static_high, fractions, centers, deform, *w,
    )
    z_low, z_high = both_ways(zu, zd, "gz")
    low2, high2 = both_ways(up2, dn2, "gz", 2)
    h, hb, yu, yd, bf = call(
        second_kernel, "scatter_second", [SMEM] + [VMEM] * 16,
        [shape(144, 128), shape(8, 256), shape(48, 128), shape(48, 128), shape(9, 8, 128)],
        [((176, 768), BF16)] * 2 + [((128, 768), BF16)] + lrows + [((144, 128), F32)],
    )(
        live_count, carried, z_low, z_high, low2, high2, own_low, own_high, send,
        fractions, centers, deform, next_affine, *w,
    )
    h, hb, low, high = fold(3, h, hb, yu, yd)
    (result,) = call(
        functools.partial(gather_second_kernel, extents), "gather_second",
        [SMEM, SMEM] + [VMEM] * 14,
        [shape(21, 1024)],
        [((144, 128), F32)] + gscratch + [((21, 8, 128), F32)],
    )(live_count, spot, h, hb, low, high, fractions, centers, deform, bf, *w, mass_core, mass_halo)
    return result


def solution(mesh):
    spread = AXES
    in_specs = (
        P(None, None, spread), P(None, spread), P(None, None, spread), P(None, None, spread),
        P(None, "gx", "gy", "gz"), P(None, spread), P(spread, None), P(spread, None, None),
        P(spread, None, None), P(spread, None), P(spread),
    )
    return jax.shard_map(
        body, mesh=mesh, in_specs=in_specs, out_specs=P(None, spread), check_vma=False
    )
```

```python
import functools

import jax
import jax.numpy as jnp
from jax import lax
from jax.experimental import pallas as pl
from jax.experimental.pallas import tpu as pltpu
from jax.sharding import PartitionSpec as P

TIME_STEP = 0.2
APIC_SCALE = 4.0
STRESS_SCALE = 0.3
F32 = jnp.float32
BF16 = jnp.bfloat16
I32 = jnp.int32
AXES = ("gx", "gy", "gz")
VMEM = pl.BlockSpec(memory_space=pltpu.VMEM)
SMEM = pl.BlockSpec(memory_space=pltpu.SMEM)
CHUNKS = 8
ZROWS = 144


def contract(a, b, da, db, precision=None):
    return lax.dot_general(
        a, b, (((da,), (db,)), ((), ())), preferred_element_type=F32, precision=precision
    )


def nt(a, b):
    return contract(a, b, 1, 1)


def nn(a, b):
    return contract(a, b, 1, 0)


def split(x):
    hi = x.astype(BF16)
    return hi, (x - hi.astype(F32)).astype(BF16)


def rounded(x):
    hi = x.astype(BF16).astype(F32)
    return hi, x - hi


def spline(f):
    return 0.5 * (0.5 - f) * (0.5 - f), 0.75 - f * f, 0.5 * (0.5 + f) * (0.5 + f)


def iota(shape, axis):
    return lax.broadcasted_iota(I32, shape, axis)


def dense(ref, step, rows):
    value = ref[:, step, :] if step is not None else ref[...]
    value = value.reshape(rows, CHUNKS, 128)
    return [value[i] for i in range(rows)]


def axis_tables(fx, cell_x, count):
    low, mid, high = spline(fx)
    plain, signed = [], []
    for plane in range(count):
        is_low, is_mid, is_high = cell_x == plane, cell_x + 1 == plane, cell_x + 2 == plane
        plain.append(jnp.where(is_low, low, jnp.where(is_mid, mid, jnp.where(is_high, high, 0.0))))
        signed.append(jnp.where(is_low, -low, jnp.where(is_high, high, 0.0)))
    return plain, signed


def y_tables(fy, cell_y, chunk):
    low, mid, high = (v[chunk : chunk + 1] for v in spline(fy))
    away = iota((8, 128), 0) - (cell_y[chunk : chunk + 1] + 1)
    plain = jnp.where(away == -1, low, jnp.where(away == 0, mid, jnp.where(away == 1, high, 0.0)))
    signed = jnp.where(away == -1, -low, jnp.where(away == 1, high, 0.0))
    return plain, signed


def build_z(fz, cell_z, w_hi, w_lo, d_hi, d_lo, chunks=CHUNKS, edges_only=False):
    low, mid, high = spline(fz)
    low_h, low_l = rounded(low)
    mid_h, mid_l = rounded(mid)
    high_h, high_l = rounded(high)
    to_low = jnp.where(cell_z == 0, 129, cell_z - 1)
    to_high = cell_z + 1
    inner = iota((128, 128), 0)
    edge = iota((16, 128), 0)
    edge = jnp.where(edge < 2, edge + 128, jnp.where(edge == 2, 0, jnp.where(edge == 3, 127, 999)))
    parts = ((slice(0, 128), inner), (slice(128, ZROWS), edge))
    if edges_only:
        parts = ((slice(0, 16), edge),)
    for chunk in range(chunks):
        at = slice(chunk, chunk + 1)
        lanes = slice(chunk * 128, chunk * 128 + 128)
        for rows, index in parts:
            is_low, is_mid, is_high = index == to_low[at], index == cell_z[at], index == to_high[at]
            for plain, signed, (a, b, c) in (
                (w_hi, d_hi, (low_h, mid_h, high_h)),
                (w_lo, d_lo, (low_l, mid_l, high_l)),
            ):
                ends = jnp.where(is_high, c[at], 0.0)
                plain[rows, lanes] = jnp.where(
                    is_low, a[at], jnp.where(is_mid, b[at], ends)
                ).astype(BF16)
                signed[rows, lanes] = jnp.where(is_low, -a[at], ends).astype(BF16)


def lower_first(spot):
    return spot[1] // 4 % 2 == 0


def by_side(first, one, other):
    return jnp.where(first, one, other)


STEPS = (0, 1, -1)


def offset_row(offset):
    place = (offset[0] + 1) * 9 + (offset[1] + 1) * 3 + offset[2] + 1
    return place - (place > 13)


def fill_send(slots, send):
    inward = [(x, y, 0) for y in STEPS for x in STEPS][1:]
    order = inward + [(x, y, 1) for y in STEPS for x in STEPS] + [None] * 3
    order += [(x, y, -1) for y in STEPS for x in STEPS]
    send[...] = jnp.zeros(send.shape, I32)
    for n, offset in enumerate(order):
        if offset is not None:
            lane = n % 4 * 32
            send[n // 4 : n // 4 + 1, lane : lane + 32] = slots[25 - offset_row(offset)]


def pick_kernel(counts, slots, pick):
    pick[...] = jnp.full(pick.shape, -1, I32)
    order = iota((1, 32), 1)
    for x in (-1, 0, 1):
        for y in (-1, 0, 1):
            for z in (-1, 0, 1):
                if (x, y, z) != (0, 0, 0):
                    n, row, lane = offset_row((x, y, z)), (x + 1) * 3 + y + 1, (z + 1) * 32
                    pick[row : row + 1, lane : lane + 32] = jnp.where(
                        order < counts[0, n], slots[n], -1
                    )


def cells_of(centre):
    return centre // 512, centre // 128 % 4, centre % 128


def to_grid(adj, deform):
    a_v, a_c, a_f = adj[0:3], adj[3:12], adj[12:21]
    b_c = [
        a_c[3 * i + j] + TIME_STEP * sum(a_f[3 * i + m] * deform[3 * j + m] for m in range(3))
        for i in range(3)
        for j in range(3)
    ]
    return a_v, b_c


def transfer(adj, deform, affine):
    a_v, b_c = to_grid(adj, deform)
    a_f = adj[12:21]
    b_f = [
        a_f[3 * i + j] + TIME_STEP * sum(affine[3 * m + i] * a_f[3 * m + j] for m in range(3))
        for i in range(3)
        for j in range(3)
    ]
    return a_v, b_c, b_f


def scatter_rows(a_v, b_c, frac, cell_x, cell_y, l0h, l0l, l2h, l2l, chunks=CHUNKS):
    base, slope = [], []
    for c in range(3):
        base.append(a_v[c] - APIC_SCALE * sum(b_c[3 * c + j] * frac[j] for j in range(3)))
        slope.append([APIC_SCALE * b_c[3 * c + j] for j in range(3)])
    wx, wx1 = axis_tables(frac[0], cell_x, 6)
    for k in range(chunks):
        at = slice(k, k + 1)
        lanes = slice(k * 128, k * 128 + 128)
        wy, wy1 = y_tables(frac[1], cell_y, k)
        for c in range(3):
            a = wy * base[c][at] + wy1 * slope[c][1][at]
            b = wy * slope[c][0][at]
            d = wy * slope[c][2][at]
            for pair in range(3):
                rows = slice(c * 48 + pair * 16, c * 48 + pair * 16 + 16)
                planes = (2 * pair, 2 * pair + 1)
                l0 = jnp.concatenate([wx[x][at] * a + wx1[x][at] * b for x in planes], axis=0)
                l2 = jnp.concatenate([wx[x][at] * d for x in planes], axis=0)
                l0h[rows, lanes], l0l[rows, lanes] = split(l0)
                l2h[rows, lanes], l2l[rows, lanes] = split(l2)


def paired(l, w):
    l0h, l0l, l2h, l2l = l
    w_hi, w_lo, d_hi, d_lo = w
    return ((l0h, w_hi), (l0l, w_hi), (l0h, w_lo), (l2h, d_hi), (l2l, d_hi), (l2h, d_lo))


def core_sums(l, w):
    return sum(nt(a[...], b[0:128]) for a, b in paired(l, w))


def edge_sums(l, w, rows=slice(128, ZROWS), lanes=slice(0, 1024)):
    return sum(nt(b[rows, lanes], a[:, lanes]) for a, b in paired(l, w))


def put_planes(ref, at, first, second):
    width = first.shape[1]
    ref[at : at + 1, :width] = first
    ref[at + 1 : at + 2, :width] = second


def static_rows(table, send, start, hot, dest):
    hi, lo = split(table[...])
    low_row, row = iota((128, 128), 0), iota((8, 128), 0)
    for t in range(3):
        index = send[start + t : start + t + 1]
        hot[...] = (low_row == index % 128).astype(F32).astype(BF16)
        got = (nn(hi, hot[...]) + nn(lo, hot[...])).reshape(14, 8, 128)
        chosen = row == index // 128
        dest[0:14, t * 128 : t * 128 + 128] = jnp.sum(jnp.where(chosen[None], got, 0.0), axis=1)


def first_kernel(
    live, adjoint, fractions, centers, deform, affine, mass, slots_back,
    h, hb, zu, zd, bf_out, w_hi, w_lo, d_hi, d_lo, send,
    l0h, l0l, l2h, l2l, table, hot,
):
    fill_send(slots_back, send)
    table[104:112] = jnp.zeros((8, 128), F32)
    early = dense(fractions, 0, 3) + [centers[0:1, :].reshape(CHUNKS, 128).astype(F32)]
    for i, tile in enumerate(early + dense(deform, 0, 9)):
        table[i * 8 : i * 8 + 8] = tile
    zu[...] = jnp.zeros(zu.shape, F32)
    zd[...] = jnp.zeros(zd.shape, F32)
    static_rows(table, send, 2, hot, zd)
    static_rows(table, send, 5, hot, zu)
    which = 1
    slots = iota((8, 128), 0) * 128 + iota((8, 128), 1)
    use = (slots < live[0, which]).astype(F32)
    adj = [v * use for v in dense(adjoint, None, 21)]
    frac = dense(fractions, which, 3)
    centre = centers[which : which + 1, :].reshape(CHUNKS, 128)
    cell_x, cell_y, cell_z = cells_of(centre)
    w = (w_hi, w_lo, d_hi, d_lo)
    l = (l0h, l0l, l2h, l2l)
    build_z(frac[2], cell_z, *w)
    a_v, b_c, b_f = transfer(adj, dense(deform, which, 9), dense(affine, which, 9))
    for i in range(9):
        bf_out[i] = b_f[i]
    scatter_rows(a_v, b_c, frac, cell_x, cell_y, *l)
    h[0:144] = core_sums(l, w)
    h[144:240] = jnp.zeros((96, 128), F32)
    for s in range(2):
        for x in range(4):
            row = 144 + s * 48 + (x + 1) * 8 + 1
            h[row : row + 4] = mass[s, x]
    lane, row = iota((16, 128), 1), iota((16, 128), 0)
    pick = (((row == 2) & (lane == 0)) | ((row == 3) & (lane == 127))).astype(F32)
    mass_ends = contract(pick, h[144:240], 1, 1, lax.Precision.HIGHEST)
    ends = jnp.concatenate([edge_sums(l, w), mass_ends], axis=1)
    hb[...] = jnp.zeros(hb.shape, F32)
    put_planes(hb, 0, ends[0:1], ends[1:2])
    put_planes(zu, 13, ends[0:1], ends[3:4])
    put_planes(zd, 13, ends[1:2], ends[2:3])


def wide_rows(hb):
    return jnp.concatenate(
        [hb[0:1, :128], hb[0:1, 128:], hb[1:2, :128], hb[1:2, 128:], jnp.zeros((4, 128), F32)], axis=0
    )


def from_wide(rows):
    top = jnp.concatenate([rows[0:1], rows[1:2]], axis=1)
    low = jnp.concatenate([rows[2:3], rows[3:4]], axis=1)
    return jnp.concatenate([top, low, jnp.zeros((6, 256), F32)], axis=0)


def transposed(rows):
    return jnp.concatenate([rows, jnp.zeros((120, 256), F32)], axis=0).T


def z_kernel(comps, spot, h, hb, from_low, from_high, h_out, hb_out, ya, yb):
    low, high = from_low[13:15, 0:256], from_high[13:15, 0:256]
    z_fold(comps, lower_first(spot), h, hb[...], low, high, h_out, hb_out, ya, yb)


def z_fold(comps, first, h, halo, low, high, h_out, hb_out, ya, yb):
    pad = jnp.zeros((6, 256), F32)
    halo = halo + jnp.concatenate([high[1:2], low[1:2], pad], axis=0)
    hb_out[...] = halo
    wall = transposed(jnp.concatenate([low[0:1], high[0:1], pad], axis=0))
    lane = iota((8, 128), 1)
    row = iota((8, 128), 0)
    blocks = comps * 6
    up, down = None, None
    for q in range(blocks):
        rows = slice(q * 8, q * 8 + 8)
        tile = (
            h[rows]
            + jnp.where(lane == 0, wall[rows, 0:1], 0.0)
            + jnp.where(lane == 127, wall[rows, 1:2], 0.0)
        )
        h_out[rows] = tile
        place = 2 * (q % 4)
        chosen = (row >= place) & (row < place + 2)
        a = pltpu.roll(tile, (place - 4) % 8, 0) if place != 4 else tile
        b = pltpu.roll(tile, place, 0) if place else tile
        up = jnp.where(chosen, a, 0.0 if up is None else up)
        down = jnp.where(chosen, b, 0.0 if down is None else down)
        if q % 4 == 3 or q == blocks - 1:
            out = slice(q // 4 * 8, q // 4 * 8 + 8)
            ya[out] = by_side(first, up, down)
            yb[out] = by_side(first, down, up)
            up, down = None, None
    packed = (blocks + 3) // 4 * 8
    ya[packed : packed + 8] = wide_rows(halo)
    yb[packed : packed + 8] = wide_rows(halo)


def y_kernel(comps, spot, h, hb, ra, rb, h_out, hb_out, xu, xd):
    first = lower_first(spot)
    row = iota((8, 128), 0)
    blocks = comps * 6
    packed = (blocks + 3) // 4 * 8
    for q in range(blocks):
        rows = slice(q * 8, q * 8 + 8)
        place = 2 * (q % 4)
        src = slice(q // 4 * 8, q // 4 * 8 + 8)
        a, b = by_side(first, rb[src], ra[src]), by_side(first, ra[src], rb[src])
        a = pltpu.roll(a, (-place) % 8, 0) if place else a
        b = pltpu.roll(b, (4 - place) % 8, 0) if place != 4 else b
        tile = (
            h[rows] + jnp.where(row < 2, a, 0.0) + jnp.where((row >= 4) & (row < 6), b, 0.0)
        )
        h_out[rows] = tile
        c, x = q // 6, q % 6
        if x >= 4:
            xu[c * 16 + (x - 4) * 8 : c * 16 + (x - 4) * 8 + 8] = tile
        if x < 2:
            xd[c * 16 + x * 8 : c * 16 + x * 8 + 8] = tile
    place = iota((8, 256), 1) % 8
    a, b = ra[packed : packed + 8], rb[packed : packed + 8]
    a, b = by_side(first, b, a), by_side(first, a, b)
    a = pltpu.roll(from_wide(a), 252, 1)
    b = pltpu.roll(from_wide(b), 4, 1)
    halo = hb[...] + jnp.where(place < 2, a, 0.0) + jnp.where((place >= 4) & (place < 6), b, 0.0)
    hb_out[...] = halo
    xu[comps * 16 : comps * 16 + 8] = wide_rows(halo)
    xd[comps * 16 : comps * 16 + 8] = wide_rows(halo)


def x_fold(comps, h, hb, from_low, from_high, total):
    for c in range(comps):
        total[c * 48 : c * 48 + 16] = h[c * 48 : c * 48 + 16] + from_low[c * 16 : c * 16 + 16]
        total[c * 48 + 16 : c * 48 + 32] = h[c * 48 + 16 : c * 48 + 32]
        total[c * 48 + 32 : c * 48 + 48] = (
            h[c * 48 + 32 : c * 48 + 48] + from_high[c * 16 : c * 16 + 16]
        )
    plane = iota((8, 256), 1) % 48 // 8
    a = pltpu.roll(from_wide(from_low[comps * 16 : comps * 16 + 8]), 224, 1)
    b = pltpu.roll(from_wide(from_high[comps * 16 : comps * 16 + 8]), 32, 1)
    return hb[...] + jnp.where(plane < 2, a, 0.0) + jnp.where(plane >= 4, b, 0.0)


def node_values(spot, extents, total, halo, mass_at, mass_halo, g_hi, g_lo):
    first_x, first_y, first_z = spot[0], spot[1], spot[2]
    lane, row = iota((8, 128), 1), iota((8, 128), 0)
    node_z = first_z + lane
    node_y = first_y + row - 1
    keep_yz = (
        (node_z >= 1) & (node_z <= extents[2] - 2) & (node_y >= 1) & (node_y <= extents[1] - 2)
    )
    wide = iota((8, 256), 1)
    side = iota((8, 256), 0)
    halo_x = first_x + wide % 48 // 8 - 1
    halo_y = first_y + wide % 8 - 1
    halo_z = first_z + jnp.where(side == 0, 128, -1)
    keep = (
        (halo_x >= 1) & (halo_x <= extents[0] - 2)
        & (halo_y >= 1) & (halo_y <= extents[1] - 2)
        & (halo_z >= 1) & (halo_z <= extents[2] - 2)
        & (side < 2) & (wide < 144) & (wide % 8 < 6)
    )
    ends = jnp.where(keep, halo / jnp.where(keep, mass_halo, 1.0), 0.0)
    columns = transposed(ends)
    g_hi[:, 128:256], g_lo[:, 128:256] = split(columns[0:144])
    for x in range(6):
        node_x = first_x + x - 1
        keep_here = keep_yz & (row < 6) & (node_x >= 1) & (node_x <= extents[0] - 2)
        mass = jnp.where(keep_here, mass_at(x), 1.0)
        for c in range(3):
            rows = slice(c * 48 + x * 8, c * 48 + x * 8 + 8)
            total[rows] = jnp.where(keep_here, total[rows] / mass, 0.0)
    g_hi[:, 0:128], g_lo[:, 0:128] = split(total[0:144])


def gather(frac, cell_x, cell_y, g_hi, g_lo, w_hi, w_lo, d_hi, d_lo, s0, sz, rows12):
    a, b = g_hi[:, 0:ZROWS], g_lo[:, 0:ZROWS]
    s0[...] = nn(a, w_hi[...]) + nn(b, w_hi[...]) + nn(a, w_lo[...])
    sz[...] = nn(a, d_hi[...]) + nn(b, d_hi[...]) + nn(a, d_lo[...])
    wx, wx1 = axis_tables(frac[0], cell_x, 6)
    for k in range(CHUNKS):
        at = slice(k, k + 1)
        lanes = slice(k * 128, k * 128 + 128)
        wy, wy1 = y_tables(frac[1], cell_y, k)
        for c in range(3):
            plain = [s0[c * 48 + x * 8 : c * 48 + x * 8 + 8, lanes] for x in range(6)]
            slope = [sz[c * 48 + x * 8 : c * 48 + x * 8 + 8, lanes] for x in range(6)]
            r0 = sum(wx[x][at] * plain[x] for x in range(6))
            r1 = sum(wx1[x][at] * plain[x] for x in range(6))
            rz = sum(wx[x][at] * slope[x] for x in range(6))
            for i, v in enumerate((wy * r0, wy * r1, wy1 * r0, wy * rz)):
                rows12[c * 4 + i, at, :] = jnp.sum(v, axis=0, keepdims=True)


def particle(rows12, frac, b_f, deform, use):
    r_v = [rows12[c * 4] for c in range(3)]
    area = [rows12[c * 4 + 1 + j] - r_v[c] * frac[j] for c in range(3) for j in range(3)]
    stress = [-STRESS_SCALE * v for v in area]
    cof = []
    for i in range(3):
        for j in range(3):
            i1, i2, j1, j2 = (i + 1) % 3, (i + 2) % 3, (j + 1) % 3, (j + 2) % 3
            cof.append(
                deform[3 * i1 + j1] * deform[3 * i2 + j2] - deform[3 * i1 + j2] * deform[3 * i2 + j1]
            )
    det = sum(deform[j] * cof[j] for j in range(3))
    ratio = (stress[0] + stress[4] + stress[8]) / det
    out = r_v + area
    for i in range(3):
        for j in range(3):
            shear = sum((stress[3 * i + m] + stress[3 * m + i]) * deform[3 * m + j] for m in range(3))
            out.append(b_f[3 * i + j] + shear + ratio * cof[3 * i + j])
    return [v * use for v in out]


def gather_first_kernel(
    extents, live, spot, h, hb, from_low, from_high, fractions, centers, deform, bf,
    w_hi, w_lo, d_hi, d_lo, pick,
    second, xu, xd, mid, mass_core, mass_halo,
    total, g_hi, g_lo, s0, sz, rows12, buf, hot,
):
    which = 1
    halo = x_fold(5, h, hb, from_low, from_high, total)
    mass_core[...] = total[144:192]
    wide = iota((8, 256), 1)

    def spread(step):
        start = 144 + step * 48
        out = jnp.ones((8, 256), F32)
        for c in range(3):
            moved = pltpu.roll(halo, (c * 48 - start) % 256, 1)
            out = jnp.where((wide >= c * 48) & (wide < c * 48 + 48), moved, out)
        return out

    mass_halo[...] = spread(0)
    node_values(
        spot, extents, total, halo,
        lambda x: total[192 + x * 8 : 192 + x * 8 + 8], spread(1), g_hi, g_lo,
    )
    frac = dense(fractions, which, 3)
    cell_x, cell_y, _ = cells_of(centers[which : which + 1, :].reshape(CHUNKS, 128))
    gather(frac, cell_x, cell_y, g_hi, g_lo, w_hi, w_lo, d_hi, d_lo, s0, sz, rows12)
    slots = iota((8, 128), 0) * 128 + iota((8, 128), 1)
    use = (slots < live[0, which]).astype(F32)
    out = particle(rows12, frac, [bf[i] for i in range(9)], dense(deform, which, 9), use)
    for i in range(21):
        second[i] = out[i]
        buf[i * 8 : i * 8 + 8] = out[i]
    buf[168:176] = jnp.zeros((8, 128), F32)
    hi, lo = split(buf[...])
    low_row = iota((128, 128), 0)
    row = iota((8, 128), 0)
    for t in range(9):
        index = pick[t : t + 1]
        hot[...] = (low_row == index % 128).astype(F32).astype(BF16)
        got = nn(hi, hot[...]) + nn(lo, hot[...])
        chosen = (row == index // 128) & (index >= 0)
        got = got.reshape(22, 8, 128)[0:21]
        got = jnp.sum(jnp.where(chosen[None], got, 0.0), axis=1)
        dest, place = ((xd, t), (mid, t - 3), (xu, t - 6))[t // 3]
        dest[:, place * 128 : place * 128 + 128] = got


def pieces(groups, at, tiles):
    lane = iota((21, 128), 1)
    out = [jnp.zeros((21, 128), F32) for _ in range(tiles)]
    for i, group in enumerate(groups):
        place = 32 * (i % 4)
        moved = pltpu.roll(group, (place - at) % 128, 1) if place != at else group
        out[i // 4] = jnp.where((lane >= place) & (lane < place + 32), moved, out[i // 4])
    return out


def lane_tile(ref, i):
    return ref[:, i * 128 : i * 128 + 128]


def route_y_kernel(spot, mid, from_low, from_high, ya, yb):
    first = lower_first(spot)
    for i, ref in enumerate((mid, from_low, from_high)):
        down, up = lane_tile(ref, 0), lane_tile(ref, 2)
        ya[:, i * 128 : i * 128 + 128] = by_side(first, up, down)
        yb[:, i * 128 : i * 128 + 128] = by_side(first, down, up)


def carry(tiles, indices, lh, ll, hot):
    row, low_row = iota((8, 128), 0), iota((128, 128), 0)
    for t, (values, index) in enumerate(zip(tiles, indices)):
        lanes = slice(t * 128, t * 128 + 128)
        hot[:, lanes] = (low_row == index % 128).astype(F32).astype(BF16)
        chosen = row == index // 128
        for pair in range(11):
            both = []
            for r in (2 * pair, 2 * pair + 1):
                blank = jnp.zeros((8, 128), F32)
                both.append(blank if r > 20 else jnp.where(chosen, values(r), 0.0))
            rows = slice(pair * 16, pair * 16 + 16)
            lh[rows, lanes], ll[rows, lanes] = split(jnp.concatenate(both, axis=0))
    return nt(lh[...], hot[...]) + nt(ll[...], hot[...])


def weights_kernel(fractions, centers, w_hi, w_lo, d_hi, d_lo):
    _, _, cell_z = cells_of(centers[0:1, :].reshape(CHUNKS, 128))
    build_z(dense(fractions, 0, 3)[2], cell_z, w_hi, w_lo, d_hi, d_lo)


def stay_kernel(second, prior, stayed, lh, ll, hot):
    tiles = [lambda r, t=t: second[r, t : t + 1, :] for t in range(8)]
    total = carry(tiles, [prior[t : t + 1] for t in range(8)], lh, ll, hot)
    for i in range(21):
        stayed[i] = total[i * 8 : i * 8 + 8]


def near_kernel(
    live, spot, mid, x_low, x_high, ra, rb, stayed, send,
    static_low, static_high, fractions, centers, deform, w_hi, w_lo, d_hi, d_lo,
    zu, zd, up2, dn2, own_low, own_high, carried,
    lh, ll, hot, l0h, l0l, l2h, l2l, moved, static, e0, e1, e2, e3,
):
    groups = [lane_tile(mid, 1), lane_tile(x_low, 1), lane_tile(x_high, 1)]
    first = lower_first(spot)
    groups += [by_side(first, lane_tile(rb, i), lane_tile(ra, i)) for i in range(3)]
    groups += [by_side(first, lane_tile(ra, i), lane_tile(rb, i)) for i in range(3)]
    final = pieces(groups[1:], 32, 2)
    moved[...] = jnp.zeros(moved.shape, F32)
    static[...] = jnp.zeros(static.shape, F32)
    zu[...] = jnp.zeros(zu.shape, F32)
    zd[...] = jnp.zeros(zd.shape, F32)
    for ref, at, first, known in ((zu, 64, 0, static_high), (zd, 0, 3, static_low)):
        for i, tile in enumerate(pieces(groups, at, 3)):
            ref[0:21, i * 128 : i * 128 + 128] = tile
            moved[:, first + i, :] = tile
            static[:, first + i, :] = known[0:14, i * 128 : i * 128 + 128]
    l = (l0h, l0l, l2h, l2l)
    e = (e0, e1, e2, e3)

    place = [static[i] for i in range(3)]
    cell_x, cell_y, cell_z = cells_of((static[3] + 0.5).astype(I32))
    build_z(place[2], cell_z, *e, chunks=6, edges_only=True)
    a_v, b_c = to_grid([moved[i] for i in range(21)], [static[4 + i] for i in range(9)])
    scatter_rows(a_v, b_c, place, cell_x, cell_y, *l, chunks=6)
    upward = edge_sums(l, e, slice(0, 16), slice(0, 384))
    downward = edge_sums(l, e, slice(0, 16), slice(384, 768))
    for ref in (up2, dn2, own_low, own_high):
        ref[...] = jnp.zeros(ref.shape, F32)
    put_planes(up2, 0, upward[0:1], upward[3:4])
    put_planes(own_high, 0, upward[1:2], upward[2:3])
    put_planes(own_low, 0, downward[0:1], downward[3:4])
    put_planes(dn2, 0, downward[1:2], downward[2:3])

    tiles = [lambda r, t=t: final[t][r : r + 1] for t in range(2)]
    total = carry(tiles, [send[t : t + 1] for t in range(2)], lh, ll, hot)
    slots = iota((8, 128), 0) * 128 + iota((8, 128), 1)
    use = (slots < live[0, 0]).astype(F32)
    adj = [(stayed[i] + total[i * 8 : i * 8 + 8]) * use for i in range(21)]
    for i in range(21):
        carried[i] = adj[i]
    frac = dense(fractions, 0, 3)
    cell_x, cell_y, _ = cells_of(centers[0:1, :].reshape(CHUNKS, 128))
    a_v, b_c = to_grid(adj, dense(deform, 0, 9))
    scatter_rows(a_v, b_c, frac, cell_x, cell_y, *l)
    ends = edge_sums(l, (w_hi, w_lo, d_hi, d_lo))
    put_planes(zu, 21, ends[0:1], ends[3:4])
    put_planes(zd, 21, ends[1:2], ends[2:3])


def second_kernel(
    live, spot, carried, z_low, z_high, low2, high2, own_low, own_high, send,
    fractions, centers, deform, affine, w_hi, w_lo, d_hi, d_lo,
    h_out, hb_out, ya, yb, bf_out,
    lh, ll, hot, l0h, l0l, l2h, l2l, h,
):
    tiles = [lambda r, t=t: z_low[r : r + 1, t * 128 : t * 128 + 128] for t in range(3)]
    tiles += [lambda r, t=t: z_high[r : r + 1, t * 128 : t * 128 + 128] for t in range(3)]
    total = carry(tiles, [send[t : t + 1] for t in range(2, 8)], lh, ll, hot)
    slots = iota((8, 128), 0) * 128 + iota((8, 128), 1)
    use = (slots < live[0, 0]).astype(F32)
    adj = [(carried[i] + total[i * 8 : i * 8 + 8]) * use for i in range(21)]
    frac = dense(fractions, 0, 3)
    cell_x, cell_y, _ = cells_of(centers[0:1, :].reshape(CHUNKS, 128))
    a_v, b_c, b_f = transfer(adj, dense(deform, 0, 9), dense(affine, 0, 9))
    for i in range(9):
        bf_out[i] = b_f[i]
    l = (l0h, l0l, l2h, l2l)
    w = (w_hi, w_lo, d_hi, d_lo)
    scatter_rows(a_v, b_c, frac, cell_x, cell_y, *l)
    h[...] = core_sums(l, w)
    ends = jnp.concatenate([edge_sums(l, w)[0:8], jnp.zeros((8, 112), F32)], axis=1)
    halo = jnp.where(iota((8, 256), 0) < 2, ends, 0.0)
    low = z_low[21:23, 0:256] + low2[0:2] + own_low[0:2]
    high = z_high[21:23, 0:256] + high2[0:2] + own_high[0:2]
    z_fold(3, lower_first(spot), h, halo, low, high, h_out, hb_out, ya, yb)


def gather_second_kernel(
    extents, live, spot, h, hb, from_low, from_high, fractions, centers, deform, bf,
    w_hi, w_lo, d_hi, d_lo, mass_core, mass_halo,
    result,
    total, g_hi, g_lo, s0, sz, rows12, packed,
):
    which = 0
    halo = x_fold(3, h, hb, from_low, from_high, total)
    node_values(
        spot, extents, total, halo,
        lambda x: mass_core[x * 8 : x * 8 + 8], mass_halo[...], g_hi, g_lo,
    )
    frac = dense(fractions, which, 3)
    cell_x, cell_y, _ = cells_of(centers[which : which + 1, :].reshape(CHUNKS, 128))
    gather(frac, cell_x, cell_y, g_hi, g_lo, w_hi, w_lo, d_hi, d_lo, s0, sz, rows12)
    slots = iota((8, 128), 0) * 128 + iota((8, 128), 1)
    use = (slots < live[0, which]).astype(F32)
    out = particle(rows12, frac, [bf[i] for i in range(9)], dense(deform, which, 9), use)
    for i in range(21):
        packed[i] = out[i]
    for k in range(CHUNKS):
        result[:, k * 128 : k * 128 + 128] = packed[:, k, :]


def shape(*dims, dtype=F32):
    return jax.ShapeDtypeStruct(dims, dtype)


def call(kernel, name, specs, outs, scratch=()):
    return pl.pallas_call(
        kernel,
        name=name,
        in_specs=list(specs),
        out_specs=[VMEM] * len(outs),
        out_shape=list(outs),
        scratch_shapes=[pltpu.VMEM(s, d) for s, d in scratch],
        compiler_params=pltpu.CompilerParams(vmem_limit_bytes=40 * 1024 * 1024),
    )


def both_ways(up, down, axis, step=1):
    count = lax.axis_size(axis)
    low = lax.ppermute(up, axis, [(i, i + step) for i in range(count - step)])
    high = lax.ppermute(down, axis, [(i + step, i) for i in range(count - step)])
    return low, high


def both_pairs(first, second, axis):
    count = lax.axis_size(axis)
    a = [(i, i ^ 1) for i in range(count) if i ^ 1 < count]
    b = [p for i in range(1, count - 1, 2) for p in ((i, i + 1), (i + 1, i))]
    ra = lax.ppermute(first, axis, a)
    rb = lax.ppermute(second, axis, b) if b else jnp.zeros_like(second)
    return ra, rb


def body(
    fractions, centers, deform, next_affine, cell_mass, final_adjoint,
    live_count, send_slot, receive_slot, receive_count, prior_slot,
):
    spot = jnp.stack([lax.axis_index("gx") * 4, lax.axis_index("gy") * 4, lax.axis_index("gz") * 128])
    spot = spot.astype(I32)
    extents = (lax.axis_size("gx") * 4, lax.axis_size("gy") * 4, lax.axis_size("gz") * 128)

    fractions, deform, next_affine = (
        jnp.transpose(v, (1, 0, 2)) for v in (fractions, deform, next_affine)
    )
    slots_back = jnp.transpose(send_slot, (1, 0, 2))
    slots_out = jnp.transpose(receive_slot, (1, 0, 2))
    prior = prior_slot.reshape(8, 128)

    wide = shape(ZROWS, 1024, dtype=BF16)
    weights = [wide] * 4
    lrows = [((144, 1024), BF16)] * 4
    gscratch = [
        ((144, 256), BF16), ((144, 256), BF16),
        ((144, 1024), F32), ((144, 1024), F32), ((12, 8, 128), F32),
    ]

    def fold(comps, h, hb, ya, yb):
        ra, rb = both_pairs(ya, yb, "gy")
        rows = comps * 16 + 8
        h, hb, xu, xd = call(
            functools.partial(y_kernel, comps), f"fold_y{comps}", [SMEM] + [VMEM] * 4,
            [shape(comps * 48, 128), shape(8, 256), shape(rows, 128), shape(rows, 128)],
        )(spot, h, hb, ra, rb)
        low, high = both_ways(xu, xd, "gx")
        return h, hb, low, high

    h, hb, zu, zd, bf, *w, send = call(
        first_kernel, "scatter_first", [SMEM] + [VMEM] * 7,
        [shape(240, 128), shape(8, 256), shape(16, 384), shape(16, 384), shape(9, 8, 128)]
        + weights + [shape(8, 128, dtype=I32)],
        lrows + [((112, 128), F32), ((128, 128), BF16)],
    )(live_count, final_adjoint, fractions, centers, deform, next_affine, cell_mass, slots_back)
    static_low, static_high = both_ways(zu, zd, "gz")
    (pick,) = call(pick_kernel, "fill_pick", [SMEM, VMEM], [shape(9, 128, dtype=I32)])(
        receive_count, slots_out
    )
    h, hb, ya, yb = call(
        functools.partial(z_kernel, 5), "fold_z5", [SMEM] + [VMEM] * 4,
        [shape(240, 128), shape(8, 256), shape(72, 128), shape(72, 128)],
    )(spot, h, hb, static_low, static_high)
    h, hb, low, high = fold(5, h, hb, ya, yb)
    second, xu, xd, mid, mass_core, mass_halo = call(
        functools.partial(gather_first_kernel, extents), "gather_first",
        [SMEM, SMEM] + [VMEM] * 13,
        [shape(21, 8, 128), shape(21, 384), shape(21, 384), shape(21, 384), shape(48, 128), shape(8, 256)],
        [((240, 128), F32)] + gscratch + [((176, 128), F32), ((128, 128), BF16)],
    )(live_count, spot, h, hb, low, high, fractions, centers, deform, bf, *w, pick)

    w = call(weights_kernel, "weights_second", [VMEM] * 2, weights)(fractions, centers)
    x_low, x_high = both_ways(xu, xd, "gx")
    (stayed,) = call(
        stay_kernel, "stay", [VMEM] * 2, [shape(21, 8, 128)],
        [((176, 1024), BF16)] * 2 + [((128, 1024), BF16)],
    )(second, prior)
    ya, yb = call(route_y_kernel, "route_y", [SMEM] + [VMEM] * 3, [shape(21, 384)] * 2)(
        spot, mid, x_low, x_high
    )
    ra, rb = both_pairs(ya, yb, "gy")
    zu, zd, up2, dn2, own_low, own_high, carried = call(
        near_kernel, "scatter_near", [SMEM] * 2 + [VMEM] * 16,
        [shape(24, 384)] * 2 + [shape(2, 256)] * 4 + [shape(21, 8, 128)],
        [((176, 256), BF16)] * 2 + [((128, 256), BF16)] + lrows
        + [((21, 8, 128), F32), ((14, 8, 128), F32)] + [((16, 768), BF16)] * 4,
    )(
        live_count, spot, mid, x_low, x_high, ra, rb, stayed, send,
        static_low, static_high, fractions, centers, deform, *w,
    )
    z_low, z_high = both_ways(zu, zd, "gz")
    low2, high2 = both_ways(up2, dn2, "gz", 2)
    h, hb, ya, yb, bf = call(
        second_kernel, "scatter_second", [SMEM] * 2 + [VMEM] * 16,
        [shape(144, 128), shape(8, 256), shape(48, 128), shape(48, 128), shape(9, 8, 128)],
        [((176, 768), BF16)] * 2 + [((128, 768), BF16)] + lrows + [((144, 128), F32)],
    )(
        live_count, spot, carried, z_low, z_high, low2, high2, own_low, own_high, send,
        fractions, centers, deform, next_affine, *w,
    )
    h, hb, low, high = fold(3, h, hb, ya, yb)
    (result,) = call(
        functools.partial(gather_second_kernel, extents), "gather_second",
        [SMEM, SMEM] + [VMEM] * 14,
        [shape(21, 1024)],
        [((144, 128), F32)] + gscratch + [((21, 8, 128), F32)],
    )(live_count, spot, h, hb, low, high, fractions, centers, deform, bf, *w, mass_core, mass_halo)
    return result


def solution(mesh):
    spread = AXES
    in_specs = (
        P(None, None, spread), P(None, spread), P(None, None, spread), P(None, None, spread),
        P(None, "gx", "gy", "gz"), P(None, spread), P(spread, None), P(spread, None, None),
        P(spread, None, None), P(spread, None), P(spread),
    )
    return jax.shard_map(
        body, mesh=mesh, in_specs=in_specs, out_specs=P(None, spread), check_vma=False
    )
```

```python
import functools

import jax
import jax.numpy as jnp
from jax import lax
from jax.experimental import pallas as pl
from jax.experimental.pallas import tpu as pltpu
from jax.sharding import PartitionSpec as P

TIME_STEP = 0.2
APIC_SCALE = 4.0
STRESS_SCALE = 0.3
F32 = jnp.float32
BF16 = jnp.bfloat16
I32 = jnp.int32
AXES = ("gx", "gy", "gz")
VMEM = pl.BlockSpec(memory_space=pltpu.VMEM)
HBM = pl.BlockSpec(memory_space=pltpu.HBM)
CHUNKS = 8
ZROWS = 144


def contract(a, b, da, db, precision=None):
    return lax.dot_general(
        a, b, (((da,), (db,)), ((), ())), preferred_element_type=F32, precision=precision
    )


def nt(a, b):
    return contract(a, b, 1, 1)


def nn(a, b):
    return contract(a, b, 1, 0)


def split(x):
    hi = x.astype(BF16)
    return hi, (x - hi.astype(F32)).astype(BF16)


def rounded(x):
    hi = x.astype(BF16).astype(F32)
    return hi, x - hi


def spline(f):
    return 0.5 * (0.5 - f) * (0.5 - f), 0.75 - f * f, 0.5 * (0.5 + f) * (0.5 + f)


def iota(shape, axis):
    return lax.broadcasted_iota(I32, shape, axis)


def dense(ref, step, rows):
    value = ref[:, step, :] if step is not None else ref[...]
    value = value.reshape(rows, CHUNKS, 128)
    return [value[i] for i in range(rows)]


def axis_tables(fx, cell_x, count):
    low, mid, high = spline(fx)
    plain, signed = [], []
    for plane in range(count):
        is_low, is_mid, is_high = cell_x == plane, cell_x + 1 == plane, cell_x + 2 == plane
        plain.append(jnp.where(is_low, low, jnp.where(is_mid, mid, jnp.where(is_high, high, 0.0))))
        signed.append(jnp.where(is_low, -low, jnp.where(is_high, high, 0.0)))
    return plain, signed


def y_tables(fy, cell_y, chunk):
    low, mid, high = (v[chunk : chunk + 1] for v in spline(fy))
    away = iota((8, 128), 0) - (cell_y[chunk : chunk + 1] + 1)
    plain = jnp.where(away == -1, low, jnp.where(away == 0, mid, jnp.where(away == 1, high, 0.0)))
    signed = jnp.where(away == -1, -low, jnp.where(away == 1, high, 0.0))
    return plain, signed


def build_z(fz, cell_z, w_hi, w_lo, d_hi, d_lo, chunks=CHUNKS, edges_only=False):
    low, mid, high = spline(fz)
    low_h, low_l = rounded(low)
    mid_h, mid_l = rounded(mid)
    high_h, high_l = rounded(high)
    to_low = jnp.where(cell_z == 0, 129, cell_z - 1)
    to_high = cell_z + 1
    inner = iota((128, 128), 0)
    edge = iota((16, 128), 0)
    edge = jnp.where(edge < 2, edge + 128, jnp.where(edge == 2, 0, jnp.where(edge == 3, 127, 999)))
    parts = ((slice(0, 128), inner), (slice(128, ZROWS), edge))
    if edges_only:
        parts = ((slice(0, 16), edge),)
    for chunk in range(chunks):
        at = slice(chunk, chunk + 1)
        lanes = slice(chunk * 128, chunk * 128 + 128)
        for rows, index in parts:
            is_low, is_mid, is_high = index == to_low[at], index == cell_z[at], index == to_high[at]
            for plain, signed, (a, b, c) in (
                (w_hi, d_hi, (low_h, mid_h, high_h)),
                (w_lo, d_lo, (low_l, mid_l, high_l)),
            ):
                ends = jnp.where(is_high, c[at], 0.0)
                plain[rows, lanes] = jnp.where(
                    is_low, a[at], jnp.where(is_mid, b[at], ends)
                ).astype(BF16)
                signed[rows, lanes] = jnp.where(is_low, -a[at], ends).astype(BF16)


def row_of(info, i, rows=8):
    return jnp.broadcast_to(info[i : i + 1, :], (rows, 128))


def by_side(info, one, other):
    return jnp.where(row_of(info, 3, one.shape[0]) == 0, one, other)


def in_use(live, step):
    slots = iota((8, 128), 0) * 128 + iota((8, 128), 1)
    return (slots < jnp.broadcast_to(live[0:1, step : step + 1], (8, 128))).astype(F32)


STEPS = (0, 1, -1)


def offset_row(offset):
    place = (offset[0] + 1) * 9 + (offset[1] + 1) * 3 + offset[2] + 1
    return place - (place > 13)


def fill_send(slots, send):
    inward = [(x, y, 0) for y in STEPS for x in STEPS][1:]
    order = inward + [(x, y, 1) for y in STEPS for x in STEPS] + [None] * 3
    order += [(x, y, -1) for y in STEPS for x in STEPS]
    send[...] = jnp.zeros(send.shape, I32)
    for n, offset in enumerate(order):
        if offset is not None:
            lane = n % 4 * 32
            send[n // 4 : n // 4 + 1, lane : lane + 32] = slots[25 - offset_row(offset)]


def pick_kernel(counts, slots, pick):
    pick[...] = jnp.full(pick.shape, -1, I32)
    order = iota((1, 32), 1)
    for x in (-1, 0, 1):
        for y in (-1, 0, 1):
            for z in (-1, 0, 1):
                if (x, y, z) != (0, 0, 0):
                    n, row, lane = offset_row((x, y, z)), (x + 1) * 3 + y + 1, (z + 1) * 32
                    pick[row : row + 1, lane : lane + 32] = jnp.where(
                        order < jnp.broadcast_to(counts[0:1, n : n + 1], (1, 32)), slots[n], -1
                    )


def cells_of(centre):
    return centre // 512, centre // 128 % 4, centre % 128


def to_grid(adj, deform):
    a_v, a_c, a_f = adj[0:3], adj[3:12], adj[12:21]
    b_c = [
        a_c[3 * i + j] + TIME_STEP * sum(a_f[3 * i + m] * deform[3 * j + m] for m in range(3))
        for i in range(3)
        for j in range(3)
    ]
    return a_v, b_c


def transfer(adj, deform, affine):
    a_v, b_c = to_grid(adj, deform)
    a_f = adj[12:21]
    b_f = [
        a_f[3 * i + j] + TIME_STEP * sum(affine[3 * m + i] * a_f[3 * m + j] for m in range(3))
        for i in range(3)
        for j in range(3)
    ]
    return a_v, b_c, b_f


def scatter_rows(a_v, b_c, frac, cell_x, cell_y, l0h, l0l, l2h, l2l, chunks=CHUNKS):
    base, slope = [], []
    for c in range(3):
        base.append(a_v[c] - APIC_SCALE * sum(b_c[3 * c + j] * frac[j] for j in range(3)))
        slope.append([APIC_SCALE * b_c[3 * c + j] for j in range(3)])
    wx, wx1 = axis_tables(frac[0], cell_x, 6)
    for k in range(chunks):
        at = slice(k, k + 1)
        lanes = slice(k * 128, k * 128 + 128)
        wy, wy1 = y_tables(frac[1], cell_y, k)
        for c in range(3):
            a = wy * base[c][at] + wy1 * slope[c][1][at]
            b = wy * slope[c][0][at]
            d = wy * slope[c][2][at]
            for pair in range(3):
                rows = slice(c * 48 + pair * 16, c * 48 + pair * 16 + 16)
                planes = (2 * pair, 2 * pair + 1)
                l0 = jnp.concatenate([wx[x][at] * a + wx1[x][at] * b for x in planes], axis=0)
                l2 = jnp.concatenate([wx[x][at] * d for x in planes], axis=0)
                l0h[rows, lanes], l0l[rows, lanes] = split(l0)
                l2h[rows, lanes], l2l[rows, lanes] = split(l2)


def paired(l, w):
    l0h, l0l, l2h, l2l = l
    w_hi, w_lo, d_hi, d_lo = w
    return ((l0h, w_hi), (l0l, w_hi), (l0h, w_lo), (l2h, d_hi), (l2l, d_hi), (l2h, d_lo))


def core_sums(l, w):
    return sum(nt(a[...], b[0:128]) for a, b in paired(l, w))


def edge_sums(l, w, rows=slice(128, ZROWS), lanes=slice(0, 1024)):
    return sum(nt(b[rows, lanes], a[:, lanes]) for a, b in paired(l, w))


def put_planes(ref, at, first, second):
    width = first.shape[1]
    ref[at : at + 1, :width] = first
    ref[at + 1 : at + 2, :width] = second


def static_rows(table, send, start, hot, dest):
    hi, lo = split(table[...])
    low_row, row = iota((128, 128), 0), iota((8, 128), 0)
    for t in range(3):
        index = send[start + t : start + t + 1]
        hot[...] = (low_row == index % 128).astype(F32).astype(BF16)
        got = (nn(hi, hot[...]) + nn(lo, hot[...])).reshape(14, 8, 128)
        chosen = row == index // 128
        dest[0:14, t * 128 : t * 128 + 128] = jnp.sum(jnp.where(chosen[None], got, 0.0), axis=1)


def first_kernel(
    live_at, adjoint_at, fractions_at, centers_at, deform_at, affine_at, mass_at, slots_at,
    h, hb, zu, zd, bf_out, w_hi, w_lo, d_hi, d_lo, send,
    l0h, l0l, l2h, l2l, table, hot,
    live, adjoint, fractions, centers, deform, affine, mass, slots_back, arrived,
):
    sources = (slots_at, fractions_at, centers_at, deform_at, live_at, adjoint_at, affine_at, mass_at)
    places = (slots_back, fractions, centers, deform, live, adjoint, affine, mass)
    copies = [
        pltpu.make_async_copy(a, b, arrived.at[i]) for i, (a, b) in enumerate(zip(sources, places))
    ]
    for copy in copies:
        copy.start()
    w = (w_hi, w_lo, d_hi, d_lo)
    l = (l0h, l0l, l2h, l2l)
    for copy in copies[:3]:
        copy.wait()
    fill_send(slots_back, send)
    which = 1
    frac = dense(fractions, which, 3)
    centre = centers[which : which + 1, :].reshape(CHUNKS, 128)
    cell_x, cell_y, cell_z = cells_of(centre)
    build_z(frac[2], cell_z, *w)
    for copy in copies[3:]:
        copy.wait()
    table[104:112] = jnp.zeros((8, 128), F32)
    early = dense(fractions, 0, 3) + [centers[0:1, :].reshape(CHUNKS, 128).astype(F32)]
    for i, tile in enumerate(early + dense(deform, 0, 9)):
        table[i * 8 : i * 8 + 8] = tile
    zu[...] = jnp.zeros(zu.shape, F32)
    zd[...] = jnp.zeros(zd.shape, F32)
    static_rows(table, send, 2, hot, zd)
    static_rows(table, send, 5, hot, zu)
    use = in_use(live, which)
    adj = [v * use for v in dense(adjoint, None, 21)]
    a_v, b_c, b_f = transfer(adj, dense(deform, which, 9), dense(affine, which, 9))
    for i in range(9):
        bf_out[i] = b_f[i]
    scatter_rows(a_v, b_c, frac, cell_x, cell_y, *l)
    h[0:144] = core_sums(l, w)
    h[144:240] = jnp.zeros((96, 128), F32)
    for s in range(2):
        for x in range(4):
            row = 144 + s * 48 + (x + 1) * 8 + 1
            h[row : row + 4] = mass[s, x]
    lane, row = iota((16, 128), 1), iota((16, 128), 0)
    pick = (((row == 2) & (lane == 0)) | ((row == 3) & (lane == 127))).astype(F32)
    mass_ends = contract(pick, h[144:240], 1, 1, lax.Precision.HIGHEST)
    ends = jnp.concatenate([edge_sums(l, w), mass_ends], axis=1)
    hb[...] = jnp.zeros(hb.shape, F32)
    put_planes(hb, 0, ends[0:1], ends[1:2])
    put_planes(zu, 13, ends[0:1], ends[3:4])
    put_planes(zd, 13, ends[1:2], ends[2:3])


def wide_rows(hb):
    return jnp.concatenate(
        [hb[0:1, :128], hb[0:1, 128:], hb[1:2, :128], hb[1:2, 128:], jnp.zeros((4, 128), F32)], axis=0
    )


def from_wide(rows):
    top = jnp.concatenate([rows[0:1], rows[1:2]], axis=1)
    low = jnp.concatenate([rows[2:3], rows[3:4]], axis=1)
    return jnp.concatenate([top, low, jnp.zeros((6, 256), F32)], axis=0)


def transposed(rows):
    return jnp.concatenate([rows, jnp.zeros((120, 256), F32)], axis=0).T


def z_kernel(comps, spot, h, hb, from_low, from_high, h_out, hb_out, ya, yb):
    low, high = from_low[13:15, 0:256], from_high[13:15, 0:256]
    z_fold(comps, spot, h, hb[...], low, high, h_out, hb_out, ya, yb)


def z_fold(comps, first, h, halo, low, high, h_out, hb_out, ya, yb):
    pad = jnp.zeros((6, 256), F32)
    halo = halo + jnp.concatenate([high[1:2], low[1:2], pad], axis=0)
    hb_out[...] = halo
    wall = transposed(jnp.concatenate([low[0:1], high[0:1], pad], axis=0))
    lane = iota((8, 128), 1)
    row = iota((8, 128), 0)
    blocks = comps * 6
    up, down = None, None
    for q in range(blocks):
        rows = slice(q * 8, q * 8 + 8)
        tile = (
            h[rows]
            + jnp.where(lane == 0, wall[rows, 0:1], 0.0)
            + jnp.where(lane == 127, wall[rows, 1:2], 0.0)
        )
        h_out[rows] = tile
        place = 2 * (q % 4)
        chosen = (row >= place) & (row < place + 2)
        a = pltpu.roll(tile, (place - 4) % 8, 0) if place != 4 else tile
        b = pltpu.roll(tile, place, 0) if place else tile
        up = jnp.where(chosen, a, 0.0 if up is None else up)
        down = jnp.where(chosen, b, 0.0 if down is None else down)
        if q % 4 == 3 or q == blocks - 1:
            out = slice(q // 4 * 8, q // 4 * 8 + 8)
            ya[out] = by_side(first, up, down)
            yb[out] = by_side(first, down, up)
            up, down = None, None
    packed = (blocks + 3) // 4 * 8
    ya[packed : packed + 8] = wide_rows(halo)
    yb[packed : packed + 8] = wide_rows(halo)


def y_kernel(comps, spot, h, hb, ra, rb, h_out, hb_out, xu, xd):
    first = spot
    row = iota((8, 128), 0)
    blocks = comps * 6
    packed = (blocks + 3) // 4 * 8
    for q in range(blocks):
        rows = slice(q * 8, q * 8 + 8)
        place = 2 * (q % 4)
        src = slice(q // 4 * 8, q // 4 * 8 + 8)
        a, b = by_side(first, rb[src], ra[src]), by_side(first, ra[src], rb[src])
        a = pltpu.roll(a, (-place) % 8, 0) if place else a
        b = pltpu.roll(b, (4 - place) % 8, 0) if place != 4 else b
        tile = (
            h[rows] + jnp.where(row < 2, a, 0.0) + jnp.where((row >= 4) & (row < 6), b, 0.0)
        )
        h_out[rows] = tile
        c, x = q // 6, q % 6
        if x >= 4:
            xu[c * 16 + (x - 4) * 8 : c * 16 + (x - 4) * 8 + 8] = tile
        if x < 2:
            xd[c * 16 + x * 8 : c * 16 + x * 8 + 8] = tile
    place = iota((8, 256), 1) % 8
    a, b = ra[packed : packed + 8], rb[packed : packed + 8]
    a, b = by_side(first, b, a), by_side(first, a, b)
    a = pltpu.roll(from_wide(a), 252, 1)
    b = pltpu.roll(from_wide(b), 4, 1)
    halo = hb[...] + jnp.where(place < 2, a, 0.0) + jnp.where((place >= 4) & (place < 6), b, 0.0)
    hb_out[...] = halo
    xu[comps * 16 : comps * 16 + 8] = wide_rows(halo)
    xd[comps * 16 : comps * 16 + 8] = wide_rows(halo)


def x_fold(comps, h, hb, from_low, from_high, total):
    for c in range(comps):
        total[c * 48 : c * 48 + 16] = h[c * 48 : c * 48 + 16] + from_low[c * 16 : c * 16 + 16]
        total[c * 48 + 16 : c * 48 + 32] = h[c * 48 + 16 : c * 48 + 32]
        total[c * 48 + 32 : c * 48 + 48] = (
            h[c * 48 + 32 : c * 48 + 48] + from_high[c * 16 : c * 16 + 16]
        )
    plane = iota((8, 256), 1) % 48 // 8
    a = pltpu.roll(from_wide(from_low[comps * 16 : comps * 16 + 8]), 224, 1)
    b = pltpu.roll(from_wide(from_high[comps * 16 : comps * 16 + 8]), 32, 1)
    return hb[...] + jnp.where(plane < 2, a, 0.0) + jnp.where(plane >= 4, b, 0.0)


def node_values(spot, extents, total, halo, mass_at, mass_halo, g_hi, g_lo):
    first_x, first_y, first_z = (row_of(spot, i) for i in range(3))
    far_x, far_y, far_z = (jnp.concatenate([v, v], axis=1) for v in (first_x, first_y, first_z))
    lane, row = iota((8, 128), 1), iota((8, 128), 0)
    node_z = first_z + lane
    node_y = first_y + row - 1
    keep_yz = (
        (node_z >= 1) & (node_z <= extents[2] - 2) & (node_y >= 1) & (node_y <= extents[1] - 2)
    )
    wide = iota((8, 256), 1)
    side = iota((8, 256), 0)
    halo_x = far_x + wide % 48 // 8 - 1
    halo_y = far_y + wide % 8 - 1
    halo_z = far_z + jnp.where(side == 0, 128, -1)
    keep = (
        (halo_x >= 1) & (halo_x <= extents[0] - 2)
        & (halo_y >= 1) & (halo_y <= extents[1] - 2)
        & (halo_z >= 1) & (halo_z <= extents[2] - 2)
        & (side < 2) & (wide < 144) & (wide % 8 < 6)
    )
    ends = jnp.where(keep, halo / jnp.where(keep, mass_halo, 1.0), 0.0)
    columns = transposed(ends)
    g_hi[:, 128:256], g_lo[:, 128:256] = split(columns[0:144])
    for x in range(6):
        node_x = first_x + x - 1
        keep_here = keep_yz & (row < 6) & (node_x >= 1) & (node_x <= extents[0] - 2)
        mass = jnp.where(keep_here, mass_at(x), 1.0)
        for c in range(3):
            rows = slice(c * 48 + x * 8, c * 48 + x * 8 + 8)
            total[rows] = jnp.where(keep_here, total[rows] / mass, 0.0)
    g_hi[:, 0:128], g_lo[:, 0:128] = split(total[0:144])


def gather(frac, cell_x, cell_y, g_hi, g_lo, w_hi, w_lo, d_hi, d_lo, s0, sz, rows12):
    a, b = g_hi[:, 0:ZROWS], g_lo[:, 0:ZROWS]
    s0[...] = nn(a, w_hi[...]) + nn(b, w_hi[...]) + nn(a, w_lo[...])
    sz[...] = nn(a, d_hi[...]) + nn(b, d_hi[...]) + nn(a, d_lo[...])
    wx, wx1 = axis_tables(frac[0], cell_x, 6)
    for k in range(CHUNKS):
        at = slice(k, k + 1)
        lanes = slice(k * 128, k * 128 + 128)
        wy, wy1 = y_tables(frac[1], cell_y, k)
        for c in range(3):
            plain = [s0[c * 48 + x * 8 : c * 48 + x * 8 + 8, lanes] for x in range(6)]
            slope = [sz[c * 48 + x * 8 : c * 48 + x * 8 + 8, lanes] for x in range(6)]
            r0 = sum(wx[x][at] * plain[x] for x in range(6))
            r1 = sum(wx1[x][at] * plain[x] for x in range(6))
            rz = sum(wx[x][at] * slope[x] for x in range(6))
            for i, v in enumerate((wy * r0, wy * r1, wy1 * r0, wy * rz)):
                rows12[c * 4 + i, at, :] = jnp.sum(v, axis=0, keepdims=True)


def particle(rows12, frac, b_f, deform, use):
    r_v = [rows12[c * 4] for c in range(3)]
    area = [rows12[c * 4 + 1 + j] - r_v[c] * frac[j] for c in range(3) for j in range(3)]
    stress = [-STRESS_SCALE * v for v in area]
    cof = []
    for i in range(3):
        for j in range(3):
            i1, i2, j1, j2 = (i + 1) % 3, (i + 2) % 3, (j + 1) % 3, (j + 2) % 3
            cof.append(
                deform[3 * i1 + j1] * deform[3 * i2 + j2] - deform[3 * i1 + j2] * deform[3 * i2 + j1]
            )
    det = sum(deform[j] * cof[j] for j in range(3))
    ratio = (stress[0] + stress[4] + stress[8]) / det
    out = r_v + area
    for i in range(3):
        for j in range(3):
            shear = sum((stress[3 * i + m] + stress[3 * m + i]) * deform[3 * m + j] for m in range(3))
            out.append(b_f[3 * i + j] + shear + ratio * cof[3 * i + j])
    return [v * use for v in out]


def gather_first_kernel(
    extents, live, spot, h, hb, from_low, from_high, fractions, centers, deform, bf,
    w_hi, w_lo, d_hi, d_lo, pick,
    second, xu, xd, mid, mass_core, mass_halo,
    total, g_hi, g_lo, s0, sz, rows12, buf, hot,
):
    which = 1
    halo = x_fold(5, h, hb, from_low, from_high, total)
    mass_core[...] = total[144:192]
    wide = iota((8, 256), 1)

    def spread(step):
        start = 144 + step * 48
        out = jnp.ones((8, 256), F32)
        for c in range(3):
            moved = pltpu.roll(halo, (c * 48 - start) % 256, 1)
            out = jnp.where((wide >= c * 48) & (wide < c * 48 + 48), moved, out)
        return out

    mass_halo[...] = spread(0)
    node_values(
        spot, extents, total, halo,
        lambda x: total[192 + x * 8 : 192 + x * 8 + 8], spread(1), g_hi, g_lo,
    )
    frac = dense(fractions, which, 3)
    cell_x, cell_y, _ = cells_of(centers[which : which + 1, :].reshape(CHUNKS, 128))
    gather(frac, cell_x, cell_y, g_hi, g_lo, w_hi, w_lo, d_hi, d_lo, s0, sz, rows12)
    use = in_use(live, which)
    out = particle(rows12, frac, [bf[i] for i in range(9)], dense(deform, which, 9), use)
    for i in range(21):
        second[i] = out[i]
        buf[i * 8 : i * 8 + 8] = out[i]
    buf[168:176] = jnp.zeros((8, 128), F32)
    hi, lo = split(buf[...])
    low_row = iota((128, 128), 0)
    row = iota((8, 128), 0)
    for t in range(9):
        index = pick[t : t + 1]
        hot[...] = (low_row == index % 128).astype(F32).astype(BF16)
        got = nn(hi, hot[...]) + nn(lo, hot[...])
        chosen = (row == index // 128) & (index >= 0)
        got = got.reshape(22, 8, 128)[0:21]
        got = jnp.sum(jnp.where(chosen[None], got, 0.0), axis=1)
        dest, place = ((xd, t), (mid, t - 3), (xu, t - 6))[t // 3]
        dest[:, place * 128 : place * 128 + 128] = got


def pieces(groups, at, tiles):
    lane = iota((21, 128), 1)
    out = [jnp.zeros((21, 128), F32) for _ in range(tiles)]
    for i, group in enumerate(groups):
        place = 32 * (i % 4)
        moved = pltpu.roll(group, (place - at) % 128, 1) if place != at else group
        out[i // 4] = jnp.where((lane >= place) & (lane < place + 32), moved, out[i // 4])
    return out


def lane_tile(ref, i):
    return ref[:, i * 128 : i * 128 + 128]


def route_y_kernel(spot, mid, from_low, from_high, ya, yb):
    first = spot
    for i, ref in enumerate((mid, from_low, from_high)):
        down, up = lane_tile(ref, 0), lane_tile(ref, 2)
        ya[:, i * 128 : i * 128 + 128] = by_side(first, up, down)
        yb[:, i * 128 : i * 128 + 128] = by_side(first, down, up)


def carry(tiles, indices, lh, ll, hot):
    row, low_row = iota((8, 128), 0), iota((128, 128), 0)
    for t, (values, index) in enumerate(zip(tiles, indices)):
        lanes = slice(t * 128, t * 128 + 128)
        hot[:, lanes] = (low_row == index % 128).astype(F32).astype(BF16)
        chosen = row == index // 128
        for pair in range(11):
            both = []
            for r in (2 * pair, 2 * pair + 1):
                blank = jnp.zeros((8, 128), F32)
                both.append(blank if r > 20 else jnp.where(chosen, values(r), 0.0))
            rows = slice(pair * 16, pair * 16 + 16)
            lh[rows, lanes], ll[rows, lanes] = split(jnp.concatenate(both, axis=0))
    return nt(lh[...], hot[...]) + nt(ll[...], hot[...])


def weights_kernel(fractions, centers, w_hi, w_lo, d_hi, d_lo):
    _, _, cell_z = cells_of(centers[0:1, :].reshape(CHUNKS, 128))
    build_z(dense(fractions, 0, 3)[2], cell_z, w_hi, w_lo, d_hi, d_lo)


def stay_kernel(second, prior, stayed, lh, ll, hot):
    tiles = [lambda r, t=t: second[r, t : t + 1, :] for t in range(8)]
    total = carry(tiles, [prior[t : t + 1] for t in range(8)], lh, ll, hot)
    for i in range(21):
        stayed[i] = total[i * 8 : i * 8 + 8]


def near_kernel(
    live, spot, mid, x_low, x_high, ra, rb, stayed, send,
    static_low, static_high, fractions, centers, deform, w_hi, w_lo, d_hi, d_lo,
    zu, zd, up2, dn2, own_low, own_high, carried,
    lh, ll, hot, l0h, l0l, l2h, l2l, moved, static, e0, e1, e2, e3,
):
    groups = [lane_tile(mid, 1), lane_tile(x_low, 1), lane_tile(x_high, 1)]
    first = spot
    groups += [by_side(first, lane_tile(rb, i), lane_tile(ra, i)) for i in range(3)]
    groups += [by_side(first, lane_tile(ra, i), lane_tile(rb, i)) for i in range(3)]
    final = pieces(groups[1:], 32, 2)
    moved[...] = jnp.zeros(moved.shape, F32)
    static[...] = jnp.zeros(static.shape, F32)
    zu[...] = jnp.zeros(zu.shape, F32)
    zd[...] = jnp.zeros(zd.shape, F32)
    for ref, at, first, known in ((zu, 64, 0, static_high), (zd, 0, 3, static_low)):
        for i, tile in enumerate(pieces(groups, at, 3)):
            ref[0:21, i * 128 : i * 128 + 128] = tile
            moved[:, first + i, :] = tile
            static[:, first + i, :] = known[0:14, i * 128 : i * 128 + 128]
    l = (l0h, l0l, l2h, l2l)
    e = (e0, e1, e2, e3)

    place = [static[i] for i in range(3)]
    cell_x, cell_y, cell_z = cells_of((static[3] + 0.5).astype(I32))
    build_z(place[2], cell_z, *e, chunks=6, edges_only=True)
    a_v, b_c = to_grid([moved[i] for i in range(21)], [static[4 + i] for i in range(9)])
    scatter_rows(a_v, b_c, place, cell_x, cell_y, *l, chunks=6)
    upward = edge_sums(l, e, slice(0, 16), slice(0, 384))
    downward = edge_sums(l, e, slice(0, 16), slice(384, 768))
    for ref in (up2, dn2, own_low, own_high):
        ref[...] = jnp.zeros(ref.shape, F32)
    put_planes(up2, 0, upward[0:1], upward[3:4])
    put_planes(own_high, 0, upward[1:2], upward[2:3])
    put_planes(own_low, 0, downward[0:1], downward[3:4])
    put_planes(dn2, 0, downward[1:2], downward[2:3])

    tiles = [lambda r, t=t: final[t][r : r + 1] for t in range(2)]
    total = carry(tiles, [send[t : t + 1] for t in range(2)], lh, ll, hot)
    use = in_use(live, 0)
    adj = [(stayed[i] + total[i * 8 : i * 8 + 8]) * use for i in range(21)]
    for i in range(21):
        carried[i] = adj[i]
    frac = dense(fractions, 0, 3)
    cell_x, cell_y, _ = cells_of(centers[0:1, :].reshape(CHUNKS, 128))
    a_v, b_c = to_grid(adj, dense(deform, 0, 9))
    scatter_rows(a_v, b_c, frac, cell_x, cell_y, *l)
    ends = edge_sums(l, (w_hi, w_lo, d_hi, d_lo))
    put_planes(zu, 21, ends[0:1], ends[3:4])
    put_planes(zd, 21, ends[1:2], ends[2:3])


def second_kernel(
    live, spot, carried, z_low, z_high, low2, high2, own_low, own_high, send,
    fractions, centers, deform, affine, w_hi, w_lo, d_hi, d_lo,
    h_out, hb_out, ya, yb, bf_out,
    lh, ll, hot, l0h, l0l, l2h, l2l, h,
):
    tiles = [lambda r, t=t: z_low[r : r + 1, t * 128 : t * 128 + 128] for t in range(3)]
    tiles += [lambda r, t=t: z_high[r : r + 1, t * 128 : t * 128 + 128] for t in range(3)]
    total = carry(tiles, [send[t : t + 1] for t in range(2, 8)], lh, ll, hot)
    use = in_use(live, 0)
    adj = [(carried[i] + total[i * 8 : i * 8 + 8]) * use for i in range(21)]
    frac = dense(fractions, 0, 3)
    cell_x, cell_y, _ = cells_of(centers[0:1, :].reshape(CHUNKS, 128))
    a_v, b_c, b_f = transfer(adj, dense(deform, 0, 9), dense(affine, 0, 9))
    for i in range(9):
        bf_out[i] = b_f[i]
    l = (l0h, l0l, l2h, l2l)
    w = (w_hi, w_lo, d_hi, d_lo)
    scatter_rows(a_v, b_c, frac, cell_x, cell_y, *l)
    h[...] = core_sums(l, w)
    ends = jnp.concatenate([edge_sums(l, w)[0:8], jnp.zeros((8, 112), F32)], axis=1)
    halo = jnp.where(iota((8, 256), 0) < 2, ends, 0.0)
    low = z_low[21:23, 0:256] + low2[0:2] + own_low[0:2]
    high = z_high[21:23, 0:256] + high2[0:2] + own_high[0:2]
    z_fold(3, spot, h, halo, low, high, h_out, hb_out, ya, yb)


def gather_second_kernel(
    extents, live, spot, h, hb, from_low, from_high, fractions, centers, deform, bf,
    w_hi, w_lo, d_hi, d_lo, mass_core, mass_halo,
    result,
    total, g_hi, g_lo, s0, sz, rows12, packed,
):
    which = 0
    halo = x_fold(3, h, hb, from_low, from_high, total)
    node_values(
        spot, extents, total, halo,
        lambda x: mass_core[x * 8 : x * 8 + 8], mass_halo[...], g_hi, g_lo,
    )
    frac = dense(fractions, which, 3)
    cell_x, cell_y, _ = cells_of(centers[which : which + 1, :].reshape(CHUNKS, 128))
    gather(frac, cell_x, cell_y, g_hi, g_lo, w_hi, w_lo, d_hi, d_lo, s0, sz, rows12)
    use = in_use(live, which)
    out = particle(rows12, frac, [bf[i] for i in range(9)], dense(deform, which, 9), use)
    for i in range(21):
        packed[i] = out[i]
    for k in range(CHUNKS):
        result[:, k * 128 : k * 128 + 128] = packed[:, k, :]


def shape(*dims, dtype=F32):
    return jax.ShapeDtypeStruct(dims, dtype)


def call(kernel, name, specs, outs, scratch=()):
    return pl.pallas_call(
        kernel,
        name=name,
        in_specs=list(specs),
        out_specs=[VMEM] * len(outs),
        out_shape=list(outs),
        scratch_shapes=[pltpu.VMEM(*v) if isinstance(v, tuple) else v for v in scratch],
        compiler_params=pltpu.CompilerParams(vmem_limit_bytes=40 * 1024 * 1024),
    )


def both_ways(up, down, axis, step=1):
    count = lax.axis_size(axis)
    low = lax.ppermute(up, axis, [(i, i + step) for i in range(count - step)])
    high = lax.ppermute(down, axis, [(i + step, i) for i in range(count - step)])
    return low, high


def both_pairs(first, second, axis):
    count = lax.axis_size(axis)
    a = [(i, i ^ 1) for i in range(count) if i ^ 1 < count]
    b = [p for i in range(1, count - 1, 2) for p in ((i, i + 1), (i + 1, i))]
    ra = lax.ppermute(first, axis, a)
    rb = lax.ppermute(second, axis, b) if b else jnp.zeros_like(second)
    return ra, rb


def body(
    fractions, centers, deform, next_affine, cell_mass, final_adjoint,
    live_count, send_slot, receive_slot, receive_count, prior_slot,
):
    at_y = lax.axis_index("gy")
    spot = [lax.axis_index("gx") * 4, at_y * 4, lax.axis_index("gz") * 128, at_y % 2]
    spot = jnp.stack(spot + [jnp.zeros_like(at_y)] * 4).astype(I32)
    spot = jnp.broadcast_to(spot[:, None], (8, 128))
    extents = (lax.axis_size("gx") * 4, lax.axis_size("gy") * 4, lax.axis_size("gz") * 128)

    fractions, deform, next_affine = (
        jnp.transpose(v, (1, 0, 2)) for v in (fractions, deform, next_affine)
    )
    slots_back = jnp.transpose(send_slot, (1, 0, 2))
    slots_out = jnp.transpose(receive_slot, (1, 0, 2))
    prior = prior_slot.reshape(8, 128)

    wide = shape(ZROWS, 1024, dtype=BF16)
    weights = [wide] * 4
    lrows = [((144, 1024), BF16)] * 4
    gscratch = [
        ((144, 256), BF16), ((144, 256), BF16),
        ((144, 1024), F32), ((144, 1024), F32), ((12, 8, 128), F32),
    ]

    def fold(comps, h, hb, ya, yb):
        ra, rb = both_pairs(ya, yb, "gy")
        rows = comps * 16 + 8
        h, hb, xu, xd = call(
            functools.partial(y_kernel, comps), f"fold_y{comps}", [VMEM] + [VMEM] * 4,
            [shape(comps * 48, 128), shape(8, 256), shape(rows, 128), shape(rows, 128)],
        )(spot, h, hb, ra, rb)
        low, high = both_ways(xu, xd, "gx")
        return h, hb, low, high

    firsts = (
        live_count, final_adjoint, fractions, centers, deform, next_affine, cell_mass, slots_back
    )
    h, hb, zu, zd, bf, *w, send = call(
        first_kernel, "scatter_first", [HBM] * 8,
        [shape(240, 128), shape(8, 256), shape(16, 384), shape(16, 384), shape(9, 8, 128)]
        + weights + [shape(8, 128, dtype=I32)],
        lrows + [((112, 128), F32), ((128, 128), BF16)]
        + [(v.shape, v.dtype) for v in firsts] + [pltpu.SemaphoreType.DMA((8,))],
    )(*(pltpu.with_memory_space_constraint(v, pltpu.HBM) for v in firsts))
    static_low, static_high = both_ways(zu, zd, "gz")
    (pick,) = call(pick_kernel, "fill_pick", [VMEM, VMEM], [shape(9, 128, dtype=I32)])(
        receive_count, slots_out
    )
    h, hb, ya, yb = call(
        functools.partial(z_kernel, 5), "fold_z5", [VMEM] + [VMEM] * 4,
        [shape(240, 128), shape(8, 256), shape(72, 128), shape(72, 128)],
    )(spot, h, hb, static_low, static_high)
    h, hb, low, high = fold(5, h, hb, ya, yb)
    second, xu, xd, mid, mass_core, mass_halo = call(
        functools.partial(gather_first_kernel, extents), "gather_first",
        [VMEM, VMEM] + [VMEM] * 13,
        [shape(21, 8, 128), shape(21, 384), shape(21, 384), shape(21, 384), shape(48, 128), shape(8, 256)],
        [((240, 128), F32)] + gscratch + [((176, 128), F32), ((128, 128), BF16)],
    )(live_count, spot, h, hb, low, high, fractions, centers, deform, bf, *w, pick)

    w = call(weights_kernel, "weights_second", [VMEM] * 2, weights)(fractions, centers)
    x_low, x_high = both_ways(xu, xd, "gx")
    (stayed,) = call(
        stay_kernel, "stay", [VMEM] * 2, [shape(21, 8, 128)],
        [((176, 1024), BF16)] * 2 + [((128, 1024), BF16)],
    )(second, prior)
    ya, yb = call(route_y_kernel, "route_y", [VMEM] + [VMEM] * 3, [shape(21, 384)] * 2)(
        spot, mid, x_low, x_high
    )
    ra, rb = both_pairs(ya, yb, "gy")
    zu, zd, up2, dn2, own_low, own_high, carried = call(
        near_kernel, "scatter_near", [VMEM] * 2 + [VMEM] * 16,
        [shape(24, 384)] * 2 + [shape(2, 256)] * 4 + [shape(21, 8, 128)],
        [((176, 256), BF16)] * 2 + [((128, 256), BF16)] + lrows
        + [((21, 8, 128), F32), ((14, 8, 128), F32)] + [((16, 768), BF16)] * 4,
    )(
        live_count, spot, mid, x_low, x_high, ra, rb, stayed, send,
        static_low, static_high, fractions, centers, deform, *w,
    )
    z_low, z_high = both_ways(zu, zd, "gz")
    low2, high2 = both_ways(up2, dn2, "gz", 2)
    h, hb, ya, yb, bf = call(
        second_kernel, "scatter_second", [VMEM] * 2 + [VMEM] * 16,
        [shape(144, 128), shape(8, 256), shape(48, 128), shape(48, 128), shape(9, 8, 128)],
        [((176, 768), BF16)] * 2 + [((128, 768), BF16)] + lrows + [((144, 128), F32)],
    )(
        live_count, spot, carried, z_low, z_high, low2, high2, own_low, own_high, send,
        fractions, centers, deform, next_affine, *w,
    )
    h, hb, low, high = fold(3, h, hb, ya, yb)
    (result,) = call(
        functools.partial(gather_second_kernel, extents), "gather_second",
        [VMEM, VMEM] + [VMEM] * 14,
        [shape(21, 1024)],
        [((144, 128), F32)] + gscratch + [((21, 8, 128), F32)],
    )(live_count, spot, h, hb, low, high, fractions, centers, deform, bf, *w, mass_core, mass_halo)
    return result


def solution(mesh):
    spread = AXES
    in_specs = (
        P(None, None, spread), P(None, spread), P(None, None, spread), P(None, None, spread),
        P(None, "gx", "gy", "gz"), P(None, spread), P(spread, None), P(spread, None, None),
        P(spread, None, None), P(spread, None), P(spread),
    )
    return jax.shard_map(
        body, mesh=mesh, in_specs=in_specs, out_specs=P(None, spread), check_vma=False
    )
```

```python
import functools

import jax
import jax.numpy as jnp
from jax import lax
from jax.experimental import pallas as pl
from jax.experimental.pallas import tpu as pltpu
from jax.sharding import PartitionSpec as P

TIME_STEP = 0.2
APIC_SCALE = 4.0
STRESS_SCALE = 0.3
F32 = jnp.float32
BF16 = jnp.bfloat16
I32 = jnp.int32
AXES = ("gx", "gy", "gz")
VMEM = pl.BlockSpec(memory_space=pltpu.VMEM)
HBM = pl.BlockSpec(memory_space=pltpu.HBM)
CHUNKS = 8
ZROWS = 144


def contract(a, b, da, db, precision=None):
    return lax.dot_general(
        a, b, (((da,), (db,)), ((), ())), preferred_element_type=F32, precision=precision
    )


def nt(a, b):
    return contract(a, b, 1, 1)


def nn(a, b):
    return contract(a, b, 1, 0)


def split(x):
    hi = x.astype(BF16)
    return hi, (x - hi.astype(F32)).astype(BF16)


def rounded(x):
    hi = x.astype(BF16).astype(F32)
    return hi, x - hi


def spline(f):
    return 0.5 * (0.5 - f) * (0.5 - f), 0.75 - f * f, 0.5 * (0.5 + f) * (0.5 + f)


def iota(shape, axis):
    return lax.broadcasted_iota(I32, shape, axis)


def dense(ref, step, rows):
    value = ref[:, step, :] if step is not None else ref[...]
    value = value.reshape(rows, CHUNKS, 128)
    return [value[i] for i in range(rows)]


def axis_tables(fx, cell_x, count):
    low, mid, high = spline(fx)
    plain, signed = [], []
    for plane in range(count):
        is_low, is_mid, is_high = cell_x == plane, cell_x + 1 == plane, cell_x + 2 == plane
        plain.append(jnp.where(is_low, low, jnp.where(is_mid, mid, jnp.where(is_high, high, 0.0))))
        signed.append(jnp.where(is_low, -low, jnp.where(is_high, high, 0.0)))
    return plain, signed


def y_tables(fy, cell_y, chunk):
    low, mid, high = (v[chunk : chunk + 1] for v in spline(fy))
    away = iota((8, 128), 0) - (cell_y[chunk : chunk + 1] + 1)
    plain = jnp.where(away == -1, low, jnp.where(away == 0, mid, jnp.where(away == 1, high, 0.0)))
    signed = jnp.where(away == -1, -low, jnp.where(away == 1, high, 0.0))
    return plain, signed


def build_z(fz, cell_z, w_hi, w_lo, d_hi, d_lo, chunks=CHUNKS, edges_only=False):
    low, mid, high = spline(fz)
    low_h, low_l = rounded(low)
    mid_h, mid_l = rounded(mid)
    high_h, high_l = rounded(high)
    to_low = jnp.where(cell_z == 0, 129, cell_z - 1)
    to_high = cell_z + 1
    inner = iota((128, 128), 0)
    edge = iota((16, 128), 0)
    edge = jnp.where(edge < 2, edge + 128, jnp.where(edge == 2, 0, jnp.where(edge == 3, 127, 999)))
    parts = ((slice(0, 128), inner), (slice(128, ZROWS), edge))
    if edges_only:
        parts = ((slice(0, 16), edge),)
    for chunk in range(chunks):
        at = slice(chunk, chunk + 1)
        lanes = slice(chunk * 128, chunk * 128 + 128)
        for rows, index in parts:
            is_low, is_mid, is_high = index == to_low[at], index == cell_z[at], index == to_high[at]
            for plain, signed, (a, b, c) in (
                (w_hi, d_hi, (low_h, mid_h, high_h)),
                (w_lo, d_lo, (low_l, mid_l, high_l)),
            ):
                ends = jnp.where(is_high, c[at], 0.0)
                plain[rows, lanes] = jnp.where(
                    is_low, a[at], jnp.where(is_mid, b[at], ends)
                ).astype(BF16)
                signed[rows, lanes] = jnp.where(is_low, -a[at], ends).astype(BF16)


def row_of(info, i, rows=8):
    return jnp.broadcast_to(info[i : i + 1, :], (rows, 128))


def by_side(info, one, other, axis_row=3):
    return jnp.where(row_of(info, axis_row, one.shape[0]) == 0, one, other)


def by_z_side(info, one, other):
    tiles = [
        by_side(info, lane_tile(one, t), lane_tile(other, t), 4) for t in range(one.shape[1] // 128)
    ]
    return jnp.concatenate(tiles, axis=1)


def fields(ref):
    tiles = [ref[i * 8 : i * 8 + 8] for i in range(13)]
    return tiles[0:3], cells_of((tiles[3] + 0.5).astype(I32)), tiles[4:13]


def in_use(live, step):
    slots = iota((8, 128), 0) * 128 + iota((8, 128), 1)
    return (slots < jnp.broadcast_to(live[0:1, step : step + 1], (8, 128))).astype(F32)


STEPS = (0, 1, -1)


def offset_row(offset):
    place = (offset[0] + 1) * 9 + (offset[1] + 1) * 3 + offset[2] + 1
    return place - (place > 13)


def fill_send(slots, send):
    inward = [(x, y, 0) for y in STEPS for x in STEPS][1:]
    order = inward + [(x, y, 1) for y in STEPS for x in STEPS] + [None] * 3
    order += [(x, y, -1) for y in STEPS for x in STEPS]
    send[...] = jnp.zeros(send.shape, I32)
    for n, offset in enumerate(order):
        if offset is not None:
            lane = n % 4 * 32
            send[n // 4 : n // 4 + 1, lane : lane + 32] = slots[25 - offset_row(offset)]


def pick_kernel(counts, slots, pick):
    pick[...] = jnp.full(pick.shape, -1, I32)
    order = iota((1, 32), 1)
    for x in (-1, 0, 1):
        for y in (-1, 0, 1):
            for z in (-1, 0, 1):
                if (x, y, z) != (0, 0, 0):
                    n, row, lane = offset_row((x, y, z)), (x + 1) * 3 + y + 1, (z + 1) * 32
                    pick[row : row + 1, lane : lane + 32] = jnp.where(
                        order < jnp.broadcast_to(counts[0:1, n : n + 1], (1, 32)), slots[n], -1
                    )


def cells_of(centre):
    return centre // 512, centre // 128 % 4, centre % 128


def to_grid(adj, deform):
    a_v, a_c, a_f = adj[0:3], adj[3:12], adj[12:21]
    b_c = [
        a_c[3 * i + j] + TIME_STEP * sum(a_f[3 * i + m] * deform[3 * j + m] for m in range(3))
        for i in range(3)
        for j in range(3)
    ]
    return a_v, b_c


def transfer(adj, deform, affine):
    a_v, b_c = to_grid(adj, deform)
    a_f = adj[12:21]
    b_f = [
        a_f[3 * i + j] + TIME_STEP * sum(affine[3 * m + i] * a_f[3 * m + j] for m in range(3))
        for i in range(3)
        for j in range(3)
    ]
    return a_v, b_c, b_f


def scatter_rows(a_v, b_c, frac, cell_x, cell_y, l0h, l0l, l2h, l2l, chunks=CHUNKS):
    base, slope = [], []
    for c in range(3):
        base.append(a_v[c] - APIC_SCALE * sum(b_c[3 * c + j] * frac[j] for j in range(3)))
        slope.append([APIC_SCALE * b_c[3 * c + j] for j in range(3)])
    wx, wx1 = axis_tables(frac[0], cell_x, 6)
    for k in range(chunks):
        at = slice(k, k + 1)
        lanes = slice(k * 128, k * 128 + 128)
        wy, wy1 = y_tables(frac[1], cell_y, k)
        for c in range(3):
            a = wy * base[c][at] + wy1 * slope[c][1][at]
            b = wy * slope[c][0][at]
            d = wy * slope[c][2][at]
            for pair in range(3):
                rows = slice(c * 48 + pair * 16, c * 48 + pair * 16 + 16)
                planes = (2 * pair, 2 * pair + 1)
                l0 = jnp.concatenate([wx[x][at] * a + wx1[x][at] * b for x in planes], axis=0)
                l2 = jnp.concatenate([wx[x][at] * d for x in planes], axis=0)
                l0h[rows, lanes], l0l[rows, lanes] = split(l0)
                l2h[rows, lanes], l2l[rows, lanes] = split(l2)


def paired(l, w):
    l0h, l0l, l2h, l2l = l
    w_hi, w_lo, d_hi, d_lo = w
    return ((l0h, w_hi), (l0l, w_hi), (l0h, w_lo), (l2h, d_hi), (l2l, d_hi), (l2h, d_lo))


def core_sums(l, w):
    return sum(nt(a[...], b[0:128]) for a, b in paired(l, w))


def edge_sums(l, w, rows=slice(128, ZROWS), lanes=slice(0, 1024)):
    return sum(nt(b[rows, lanes], a[:, lanes]) for a, b in paired(l, w))


def put_planes(ref, at, first, second):
    width = first.shape[1]
    ref[at : at + 1, :width] = first
    ref[at + 1 : at + 2, :width] = second


def static_rows(table, send, rows, hot, put):
    hi, lo = split(table[...])
    low_row, row = iota((128, 128), 0), iota((8, 128), 0)
    for t, n in enumerate(rows):
        index = send[n : n + 1]
        hot[...] = (low_row == index % 128).astype(F32).astype(BF16)
        got = (nn(hi, hot[...]) + nn(lo, hot[...])).reshape(14, 8, 128)
        chosen = row == index // 128
        put(t, jnp.sum(jnp.where(chosen[None], got, 0.0), axis=1))


def first_kernel(
    spot, live_at, adjoint_at, fractions_at, centers_at, deform_at, affine_at, mass_at, slots_at,
    h, hb, both, bf_out, w_hi, w_lo, d_hi, d_lo, send, now, early,
    l0h, l0l, l2h, l2l, hot, zu, zd,
    live, adjoint, fractions, centers, deform, affine, mass, slots_back, arrived,
):
    sources = (slots_at, fractions_at, centers_at, deform_at, live_at, adjoint_at, affine_at, mass_at)
    places = (slots_back, fractions, centers, deform, live, adjoint, affine, mass)
    copies = [
        pltpu.make_async_copy(a, b, arrived.at[i]) for i, (a, b) in enumerate(zip(sources, places))
    ]
    for copy in copies:
        copy.start()
    w = (w_hi, w_lo, d_hi, d_lo)
    l = (l0h, l0l, l2h, l2l)
    zu[...] = jnp.zeros(zu.shape, F32)
    zd[...] = jnp.zeros(zd.shape, F32)
    for copy in copies[:3]:
        copy.wait()
    fill_send(slots_back, send)
    frac = dense(fractions, 1, 3)
    centre = centers[1:2, :].reshape(CHUNKS, 128)
    cell_x, cell_y, cell_z = cells_of(centre)
    build_z(frac[2], cell_z, *w)
    for copy in copies[3:]:
        copy.wait()
    deform_now = dense(deform, 1, 9)
    for i, tile in enumerate(frac + [centre.astype(F32)] + deform_now):
        now[i * 8 : i * 8 + 8] = tile
    early[104:112] = jnp.zeros((8, 128), F32)
    known = dense(fractions, 0, 3) + [centers[0:1, :].reshape(CHUNKS, 128).astype(F32)]
    for i, tile in enumerate(known + dense(deform, 0, 9)):
        early[i * 8 : i * 8 + 8] = tile

    def put(t, got):
        dest = (zd, zu)[t // 3]
        dest[0:14, t % 3 * 128 : t % 3 * 128 + 128] = got

    static_rows(early, send, range(2, 8), hot, put)
    use = in_use(live, 1)
    adj = [v * use for v in dense(adjoint, None, 21)]
    a_v, b_c, b_f = transfer(adj, deform_now, dense(affine, 1, 9))
    for i in range(9):
        bf_out[i] = b_f[i]
    scatter_rows(a_v, b_c, frac, cell_x, cell_y, *l)
    h[0:144] = core_sums(l, w)
    h[144:240] = jnp.zeros((96, 128), F32)
    for s in range(2):
        for x in range(4):
            row = 144 + s * 48 + (x + 1) * 8 + 1
            h[row : row + 4] = mass[s, x]
    lane, row = iota((16, 128), 1), iota((16, 128), 0)
    pick = (((row == 2) & (lane == 0)) | ((row == 3) & (lane == 127))).astype(F32)
    mass_ends = contract(pick, h[144:240], 1, 1, lax.Precision.HIGHEST)
    ends = jnp.concatenate([edge_sums(l, w), mass_ends], axis=1)
    hb[...] = jnp.zeros(hb.shape, F32)
    put_planes(hb, 0, ends[0:1], ends[1:2])
    put_planes(zu, 13, ends[0:1], ends[3:4])
    put_planes(zd, 13, ends[1:2], ends[2:3])
    both[0:16] = by_z_side(spot, zu, zd)
    both[16:32] = by_z_side(spot, zd, zu)


def wide_rows(hb):
    return jnp.concatenate(
        [hb[0:1, :128], hb[0:1, 128:], hb[1:2, :128], hb[1:2, 128:], jnp.zeros((4, 128), F32)], axis=0
    )


def from_wide(rows):
    top = jnp.concatenate([rows[0:1], rows[1:2]], axis=1)
    low = jnp.concatenate([rows[2:3], rows[3:4]], axis=1)
    return jnp.concatenate([top, low, jnp.zeros((6, 256), F32)], axis=0)


def transposed(rows):
    return jnp.concatenate([rows, jnp.zeros((120, 256), F32)], axis=0).T


def z_kernel(comps, spot, h, hb, both, far, h_out, hb_out, ya, yb):
    direct, relayed = both[13:15, 0:256], far[13:15, 0:256]
    low, high = by_z_side(spot, relayed, direct), by_z_side(spot, direct, relayed)
    z_fold(comps, spot, h, hb[...], low, high, h_out, hb_out, ya, yb)


def z_fold(comps, first, h, halo, low, high, h_out, hb_out, ya, yb):
    pad = jnp.zeros((6, 256), F32)
    halo = halo + jnp.concatenate([high[1:2], low[1:2], pad], axis=0)
    hb_out[...] = halo
    wall = transposed(jnp.concatenate([low[0:1], high[0:1], pad], axis=0))
    lane = iota((8, 128), 1)
    row = iota((8, 128), 0)
    blocks = comps * 6
    up, down = None, None
    for q in range(blocks):
        rows = slice(q * 8, q * 8 + 8)
        tile = (
            h[rows]
            + jnp.where(lane == 0, wall[rows, 0:1], 0.0)
            + jnp.where(lane == 127, wall[rows, 1:2], 0.0)
        )
        h_out[rows] = tile
        place = 2 * (q % 4)
        chosen = (row >= place) & (row < place + 2)
        a = pltpu.roll(tile, (place - 4) % 8, 0) if place != 4 else tile
        b = pltpu.roll(tile, place, 0) if place else tile
        up = jnp.where(chosen, a, 0.0 if up is None else up)
        down = jnp.where(chosen, b, 0.0 if down is None else down)
        if q % 4 == 3 or q == blocks - 1:
            out = slice(q // 4 * 8, q // 4 * 8 + 8)
            ya[out] = by_side(first, up, down)
            yb[out] = by_side(first, down, up)
            up, down = None, None
    packed = (blocks + 3) // 4 * 8
    ya[packed : packed + 8] = wide_rows(halo)
    yb[packed : packed + 8] = wide_rows(halo)


def y_kernel(comps, spot, h, hb, ra, rb, h_out, hb_out, xu, xd):
    first = spot
    row = iota((8, 128), 0)
    blocks = comps * 6
    packed = (blocks + 3) // 4 * 8
    for q in range(blocks):
        rows = slice(q * 8, q * 8 + 8)
        place = 2 * (q % 4)
        src = slice(q // 4 * 8, q // 4 * 8 + 8)
        a, b = by_side(first, rb[src], ra[src]), by_side(first, ra[src], rb[src])
        a = pltpu.roll(a, (-place) % 8, 0) if place else a
        b = pltpu.roll(b, (4 - place) % 8, 0) if place != 4 else b
        tile = (
            h[rows] + jnp.where(row < 2, a, 0.0) + jnp.where((row >= 4) & (row < 6), b, 0.0)
        )
        h_out[rows] = tile
        c, x = q // 6, q % 6
        if x >= 4:
            xu[c * 16 + (x - 4) * 8 : c * 16 + (x - 4) * 8 + 8] = tile
        if x < 2:
            xd[c * 16 + x * 8 : c * 16 + x * 8 + 8] = tile
    place = iota((8, 256), 1) % 8
    a, b = ra[packed : packed + 8], rb[packed : packed + 8]
    a, b = by_side(first, b, a), by_side(first, a, b)
    a = pltpu.roll(from_wide(a), 252, 1)
    b = pltpu.roll(from_wide(b), 4, 1)
    halo = hb[...] + jnp.where(place < 2, a, 0.0) + jnp.where((place >= 4) & (place < 6), b, 0.0)
    hb_out[...] = halo
    xu[comps * 16 : comps * 16 + 8] = wide_rows(halo)
    xd[comps * 16 : comps * 16 + 8] = wide_rows(halo)


def x_fold(comps, h, hb, from_low, from_high, total):
    for c in range(comps):
        total[c * 48 : c * 48 + 16] = h[c * 48 : c * 48 + 16] + from_low[c * 16 : c * 16 + 16]
        total[c * 48 + 16 : c * 48 + 32] = h[c * 48 + 16 : c * 48 + 32]
        total[c * 48 + 32 : c * 48 + 48] = (
            h[c * 48 + 32 : c * 48 + 48] + from_high[c * 16 : c * 16 + 16]
        )
    plane = iota((8, 256), 1) % 48 // 8
    a = pltpu.roll(from_wide(from_low[comps * 16 : comps * 16 + 8]), 224, 1)
    b = pltpu.roll(from_wide(from_high[comps * 16 : comps * 16 + 8]), 32, 1)
    return hb[...] + jnp.where(plane < 2, a, 0.0) + jnp.where(plane >= 4, b, 0.0)


def node_values(spot, extents, total, halo, mass_at, mass_halo, g_hi, g_lo):
    first_x, first_y, first_z = (row_of(spot, i) for i in range(3))
    far_x, far_y, far_z = (jnp.concatenate([v, v], axis=1) for v in (first_x, first_y, first_z))
    lane, row = iota((8, 128), 1), iota((8, 128), 0)
    node_z = first_z + lane
    node_y = first_y + row - 1
    keep_yz = (
        (node_z >= 1) & (node_z <= extents[2] - 2) & (node_y >= 1) & (node_y <= extents[1] - 2)
    )
    wide = iota((8, 256), 1)
    side = iota((8, 256), 0)
    halo_x = far_x + wide % 48 // 8 - 1
    halo_y = far_y + wide % 8 - 1
    halo_z = far_z + jnp.where(side == 0, 128, -1)
    keep = (
        (halo_x >= 1) & (halo_x <= extents[0] - 2)
        & (halo_y >= 1) & (halo_y <= extents[1] - 2)
        & (halo_z >= 1) & (halo_z <= extents[2] - 2)
        & (side < 2) & (wide < 144) & (wide % 8 < 6)
    )
    ends = jnp.where(keep, halo / jnp.where(keep, mass_halo, 1.0), 0.0)
    columns = transposed(ends)
    g_hi[:, 128:256], g_lo[:, 128:256] = split(columns[0:144])
    for x in range(6):
        node_x = first_x + x - 1
        keep_here = keep_yz & (row < 6) & (node_x >= 1) & (node_x <= extents[0] - 2)
        mass = jnp.where(keep_here, mass_at(x), 1.0)
        for c in range(3):
            rows = slice(c * 48 + x * 8, c * 48 + x * 8 + 8)
            total[rows] = jnp.where(keep_here, total[rows] / mass, 0.0)
    g_hi[:, 0:128], g_lo[:, 0:128] = split(total[0:144])


def gather(frac, cell_x, cell_y, g_hi, g_lo, w_hi, w_lo, d_hi, d_lo, s0, sz, rows12):
    a, b = g_hi[:, 0:ZROWS], g_lo[:, 0:ZROWS]
    s0[...] = nn(a, w_hi[...]) + nn(b, w_hi[...]) + nn(a, w_lo[...])
    sz[...] = nn(a, d_hi[...]) + nn(b, d_hi[...]) + nn(a, d_lo[...])
    wx, wx1 = axis_tables(frac[0], cell_x, 6)
    for k in range(CHUNKS):
        at = slice(k, k + 1)
        lanes = slice(k * 128, k * 128 + 128)
        wy, wy1 = y_tables(frac[1], cell_y, k)
        for c in range(3):
            plain = [s0[c * 48 + x * 8 : c * 48 + x * 8 + 8, lanes] for x in range(6)]
            slope = [sz[c * 48 + x * 8 : c * 48 + x * 8 + 8, lanes] for x in range(6)]
            r0 = sum(wx[x][at] * plain[x] for x in range(6))
            r1 = sum(wx1[x][at] * plain[x] for x in range(6))
            rz = sum(wx[x][at] * slope[x] for x in range(6))
            for i, v in enumerate((wy * r0, wy * r1, wy1 * r0, wy * rz)):
                rows12[c * 4 + i, at, :] = jnp.sum(v, axis=0, keepdims=True)


def particle(rows12, frac, b_f, deform, use):
    r_v = [rows12[c * 4] for c in range(3)]
    area = [rows12[c * 4 + 1 + j] - r_v[c] * frac[j] for c in range(3) for j in range(3)]
    stress = [-STRESS_SCALE * v for v in area]
    cof = []
    for i in range(3):
        for j in range(3):
            i1, i2, j1, j2 = (i + 1) % 3, (i + 2) % 3, (j + 1) % 3, (j + 2) % 3
            cof.append(
                deform[3 * i1 + j1] * deform[3 * i2 + j2] - deform[3 * i1 + j2] * deform[3 * i2 + j1]
            )
    det = sum(deform[j] * cof[j] for j in range(3))
    ratio = (stress[0] + stress[4] + stress[8]) / det
    out = r_v + area
    for i in range(3):
        for j in range(3):
            shear = sum((stress[3 * i + m] + stress[3 * m + i]) * deform[3 * m + j] for m in range(3))
            out.append(b_f[3 * i + j] + shear + ratio * cof[3 * i + j])
    return [v * use for v in out]


def gather_first_kernel(
    extents, live, spot, h, hb, from_low, from_high, now, bf, w_hi, w_lo, d_hi, d_lo, pick,
    second, xu, xd, mid, mass_core, mass_halo,
    total, g_hi, g_lo, s0, sz, rows12, buf, hot,
):
    which = 1
    halo = x_fold(5, h, hb, from_low, from_high, total)
    mass_core[...] = total[144:192]
    wide = iota((8, 256), 1)

    def spread(step):
        start = 144 + step * 48
        out = jnp.ones((8, 256), F32)
        for c in range(3):
            moved = pltpu.roll(halo, (c * 48 - start) % 256, 1)
            out = jnp.where((wide >= c * 48) & (wide < c * 48 + 48), moved, out)
        return out

    mass_halo[...] = spread(0)
    node_values(
        spot, extents, total, halo,
        lambda x: total[192 + x * 8 : 192 + x * 8 + 8], spread(1), g_hi, g_lo,
    )
    frac, (cell_x, cell_y, _), deform = fields(now)
    gather(frac, cell_x, cell_y, g_hi, g_lo, w_hi, w_lo, d_hi, d_lo, s0, sz, rows12)
    use = in_use(live, which)
    out = particle(rows12, frac, [bf[i] for i in range(9)], deform, use)
    for i in range(21):
        second[i] = out[i]
        buf[i * 8 : i * 8 + 8] = out[i]
    buf[168:176] = jnp.zeros((8, 128), F32)
    hi, lo = split(buf[...])
    low_row = iota((128, 128), 0)
    row = iota((8, 128), 0)
    for t in range(9):
        index = pick[t : t + 1]
        hot[...] = (low_row == index % 128).astype(F32).astype(BF16)
        got = nn(hi, hot[...]) + nn(lo, hot[...])
        chosen = (row == index // 128) & (index >= 0)
        got = got.reshape(22, 8, 128)[0:21]
        got = jnp.sum(jnp.where(chosen[None], got, 0.0), axis=1)
        dest, place = ((xd, t), (mid, t - 3), (xu, t - 6))[t // 3]
        dest[:, place * 128 : place * 128 + 128] = got


def pieces(groups, at, tiles):
    lane = iota((21, 128), 1)
    out = [jnp.zeros((21, 128), F32) for _ in range(tiles)]
    for i, group in enumerate(groups):
        place = 32 * (i % 4)
        moved = pltpu.roll(group, (place - at) % 128, 1) if place != at else group
        out[i // 4] = jnp.where((lane >= place) & (lane < place + 32), moved, out[i // 4])
    return out


def lane_tile(ref, i):
    return ref[:, i * 128 : i * 128 + 128]


def route_y_kernel(spot, mid, from_low, from_high, ya, yb):
    first = spot
    for i, ref in enumerate((mid, from_low, from_high)):
        down, up = lane_tile(ref, 0), lane_tile(ref, 2)
        ya[:, i * 128 : i * 128 + 128] = by_side(first, up, down)
        yb[:, i * 128 : i * 128 + 128] = by_side(first, down, up)


def carry(tiles, indices, lh, ll, hot, count=21):
    row, low_row = iota((8, 128), 0), iota((128, 128), 0)
    for t, (values, index) in enumerate(zip(tiles, indices)):
        lanes = slice(t * 128, t * 128 + 128)
        hot[:, lanes] = (low_row == index % 128).astype(F32).astype(BF16)
        chosen = row == index // 128
        for pair in range((count + 1) // 2):
            both = []
            for r in (2 * pair, 2 * pair + 1):
                blank = jnp.zeros((8, 128), F32)
                both.append(blank if r >= count else jnp.where(chosen, values(r), 0.0))
            rows = slice(pair * 16, pair * 16 + 16)
            lh[rows, lanes], ll[rows, lanes] = split(jnp.concatenate(both, axis=0))
    return nt(lh[...], hot[...]) + nt(ll[...], hot[...])


def weights_kernel(early, send, w_hi, w_lo, d_hi, d_lo, a_hi, a_lo, b_hi, b_lo, arrive, hot):
    frac, cells, _ = fields(early)
    build_z(frac[2], cells[2], w_hi, w_lo, d_hi, d_lo)

    def put(t, got):
        arrive[:, t, :] = got

    static_rows(early, send, (2, 3, 4, 5, 6, 7, 0, 1), hot, put)
    _, _, cell_z = cells_of((arrive[3] + 0.5).astype(I32))
    build_z(arrive[2], cell_z, a_hi, a_lo, b_hi, b_lo)


def stay_kernel(
    live, second, prior, early, w_hi, w_lo, d_hi, d_lo,
    stayed, core, ends,
    lh, ll, hot, l0h, l0l, l2h, l2l,
):
    tiles = [lambda r, t=t: second[r, t : t + 1, :] for t in range(8)]
    total = carry(tiles, [prior[t : t + 1] for t in range(8)], lh, ll, hot)
    use = in_use(live, 0)
    adj = [total[i * 8 : i * 8 + 8] * use for i in range(21)]
    for i in range(21):
        stayed[i] = adj[i]
    frac, (cell_x, cell_y, _), deform = fields(early)
    a_v, b_c = to_grid(adj, deform)
    l, w = (l0h, l0l, l2h, l2l), (w_hi, w_lo, d_hi, d_lo)
    scatter_rows(a_v, b_c, frac, cell_x, cell_y, *l)
    core[...] = core_sums(l, w)
    ends[...] = edge_sums(l, w)


def near_kernel(
    spot, mid, x_low, x_high, ra, rb, both, far, arrive, ends_stay,
    zu, zd, up2, dn2, own_low, own_high, final,
    l0h, l0l, l2h, l2l, moved, static, e0, e1, e2, e3,
):
    groups = [lane_tile(mid, 1), lane_tile(x_low, 1), lane_tile(x_high, 1)]
    groups += [by_side(spot, lane_tile(rb, i), lane_tile(ra, i)) for i in range(3)]
    groups += [by_side(spot, lane_tile(ra, i), lane_tile(rb, i)) for i in range(3)]
    zu[...] = jnp.zeros(zu.shape, F32)
    zd[...] = jnp.zeros(zd.shape, F32)
    direct, relayed = both[0:16], far[...]
    static_low = by_z_side(spot, relayed, direct)
    static_high = by_z_side(spot, direct, relayed)
    for ref, at, first, known in ((zu, 64, 0, static_high), (zd, 0, 3, static_low)):
        for i, tile in enumerate(pieces(groups, at, 3)):
            ref[0:21, i * 128 : i * 128 + 128] = tile
            moved[:, first + i, :] = tile
            static[:, first + i, :] = lane_tile(known, i)[0:14]
    for i, tile in enumerate(pieces(groups[1:], 32, 2)):
        final[:, i * 128 : i * 128 + 128] = tile
        moved[:, 6 + i, :] = tile
        static[:, 6 + i, :] = arrive[:, 6 + i, :]
    l = (l0h, l0l, l2h, l2l)
    e = (e0, e1, e2, e3)
    place = [static[i] for i in range(3)]
    cell_x, cell_y, cell_z = cells_of((static[3] + 0.5).astype(I32))
    build_z(place[2], cell_z, *e, edges_only=True)
    a_v, b_c = to_grid([moved[i] for i in range(21)], [static[4 + i] for i in range(9)])
    scatter_rows(a_v, b_c, place, cell_x, cell_y, *l)
    upward = edge_sums(l, e, slice(0, 16), slice(0, 384))
    downward = edge_sums(l, e, slice(0, 16), slice(384, 768))
    ends = edge_sums(l, e, slice(0, 16), slice(768, 1024)) + ends_stay[...]
    for ref in (up2, dn2, own_low, own_high):
        ref[...] = jnp.zeros(ref.shape, F32)
    put_planes(up2, 0, upward[0:1], upward[3:4])
    put_planes(own_high, 0, upward[1:2], upward[2:3])
    put_planes(own_low, 0, downward[0:1], downward[3:4])
    put_planes(dn2, 0, downward[1:2], downward[2:3])
    put_planes(zu, 21, ends[0:1], ends[3:4])
    put_planes(zd, 21, ends[1:2], ends[2:3])


def second_kernel(
    spot, z_low, z_high, low2, high2, own_low, own_high, final, arrive, a_hi, a_lo, b_hi, b_lo,
    core_stay, ends_stay,
    h_out, hb_out, ya, yb,
    l0h, l0l, l2h, l2l, moved, h,
):
    for i in range(3):
        moved[:, i, :] = lane_tile(z_low, i)[0:21]
        moved[:, 3 + i, :] = lane_tile(z_high, i)[0:21]
    for i in range(2):
        moved[:, 6 + i, :] = lane_tile(final, i)
    place = [arrive[i] for i in range(3)]
    cell_x, cell_y, _ = cells_of((arrive[3] + 0.5).astype(I32))
    a_v, b_c = to_grid([moved[i] for i in range(21)], [arrive[4 + i] for i in range(9)])
    l, w = (l0h, l0l, l2h, l2l), (a_hi, a_lo, b_hi, b_lo)
    scatter_rows(a_v, b_c, place, cell_x, cell_y, *l)
    h[...] = core_sums(l, w) + core_stay[...]
    ends = edge_sums(l, w) + ends_stay[...]
    ends = jnp.concatenate([ends[0:8], jnp.zeros((8, 112), F32)], axis=1)
    halo = jnp.where(iota((8, 256), 0) < 2, ends, 0.0)
    low = z_low[21:23, 0:256] + low2[0:2] + own_low[0:2]
    high = z_high[21:23, 0:256] + high2[0:2] + own_high[0:2]
    z_fold(3, spot, h, halo, low, high, h_out, hb_out, ya, yb)


def deform_kernel(live, stayed, z_low, z_high, final, send, affine, bf_out, lh, ll, hot):
    tiles = []
    for ref, count in ((z_low, 3), (z_high, 3), (final, 2)):
        for t in range(count):
            tiles.append(
                lambda r, ref=ref, t=t: ref[12 + r : 13 + r, t * 128 : t * 128 + 128]
            )
    rows = [send[t : t + 1] for t in (2, 3, 4, 5, 6, 7, 0, 1)]
    total = carry(tiles, rows, lh, ll, hot, 9)
    use = in_use(live, 0)
    a_f = [(stayed[12 + i] + total[i * 8 : i * 8 + 8]) * use for i in range(9)]
    k = dense(affine, 0, 9)
    for i in range(3):
        for j in range(3):
            bf_out[3 * i + j] = a_f[3 * i + j] + TIME_STEP * sum(
                k[3 * m + i] * a_f[3 * m + j] for m in range(3)
            )


def gather_second_kernel(
    extents, live, spot, h, hb, from_low, from_high, early, bf, w_hi, w_lo, d_hi, d_lo,
    mass_core, mass_halo,
    result,
    total, g_hi, g_lo, s0, sz, rows12, packed,
):
    which = 0
    halo = x_fold(3, h, hb, from_low, from_high, total)
    node_values(
        spot, extents, total, halo,
        lambda x: mass_core[x * 8 : x * 8 + 8], mass_halo[...], g_hi, g_lo,
    )
    frac, (cell_x, cell_y, _), deform = fields(early)
    gather(frac, cell_x, cell_y, g_hi, g_lo, w_hi, w_lo, d_hi, d_lo, s0, sz, rows12)
    use = in_use(live, which)
    out = particle(rows12, frac, [bf[i] for i in range(9)], deform, use)
    for i in range(21):
        packed[i] = out[i]
    for k in range(CHUNKS):
        result[:, k * 128 : k * 128 + 128] = packed[:, k, :]


def shape(*dims, dtype=F32):
    return jax.ShapeDtypeStruct(dims, dtype)


def call(kernel, name, specs, outs, scratch=()):
    return pl.pallas_call(
        kernel,
        name=name,
        in_specs=list(specs),
        out_specs=[VMEM] * len(outs),
        out_shape=list(outs),
        scratch_shapes=[pltpu.VMEM(*v) if isinstance(v, tuple) else v for v in scratch],
        compiler_params=pltpu.CompilerParams(vmem_limit_bytes=40 * 1024 * 1024),
    )


def both_ways(up, down, axis, step=1):
    count = lax.axis_size(axis)
    low = lax.ppermute(up, axis, [(i, i + step) for i in range(count - step)])
    high = lax.ppermute(down, axis, [(i + step, i) for i in range(count - step)])
    return low, high


def both_pairs(first, second, axis):
    count = lax.axis_size(axis)
    a = [(i, i ^ 1) for i in range(count) if i ^ 1 < count]
    b = [p for i in range(1, count - 1, 2) for p in ((i, i + 1), (i + 1, i))]
    ra = lax.ppermute(first, axis, a)
    rb = lax.ppermute(second, axis, b) if b else jnp.zeros_like(second)
    return ra, rb


def body(
    fractions, centers, deform, next_affine, cell_mass, final_adjoint,
    live_count, send_slot, receive_slot, receive_count, prior_slot,
):
    at_y = lax.axis_index("gy")
    at_z = lax.axis_index("gz")
    spot = [lax.axis_index("gx") * 4, at_y * 4, at_z * 128, at_y % 2, at_z % 2]
    spot = jnp.stack(spot + [jnp.zeros_like(at_y)] * 3).astype(I32)
    spot = jnp.broadcast_to(spot[:, None], (8, 128))
    extents = (lax.axis_size("gx") * 4, lax.axis_size("gy") * 4, lax.axis_size("gz") * 128)

    fractions, deform, next_affine = (
        jnp.transpose(v, (1, 0, 2)) for v in (fractions, deform, next_affine)
    )
    slots_back = jnp.transpose(send_slot, (1, 0, 2))
    slots_out = jnp.transpose(receive_slot, (1, 0, 2))
    prior = prior_slot.reshape(8, 128)

    wide = shape(ZROWS, 1024, dtype=BF16)
    weights = [wide] * 4
    lrows = [((144, 1024), BF16)] * 4
    gscratch = [
        ((144, 256), BF16), ((144, 256), BF16),
        ((144, 1024), F32), ((144, 1024), F32), ((12, 8, 128), F32),
    ]

    def fold(comps, h, hb, ya, yb):
        ra, rb = both_pairs(ya, yb, "gy")
        rows = comps * 16 + 8
        h, hb, xu, xd = call(
            functools.partial(y_kernel, comps), f"fold_y{comps}", [VMEM] * 5,
            [shape(comps * 48, 128), shape(8, 256), shape(rows, 128), shape(rows, 128)],
        )(spot, h, hb, ra, rb)
        low, high = both_ways(xu, xd, "gx")
        return h, hb, low, high

    firsts = (
        live_count, final_adjoint, fractions, centers, deform, next_affine, cell_mass, slots_back
    )
    h, hb, both, bf, *w, send, now, early = call(
        first_kernel, "scatter_first", [VMEM] + [HBM] * 8,
        [shape(240, 128), shape(8, 256), shape(32, 384), shape(9, 8, 128)]
        + weights + [shape(8, 128, dtype=I32), shape(104, 128), shape(112, 128)],
        lrows + [((128, 128), BF16), ((16, 384), F32), ((16, 384), F32)]
        + [(v.shape, v.dtype) for v in firsts] + [pltpu.SemaphoreType.DMA((8,))],
    )(spot, *(pltpu.with_memory_space_constraint(v, pltpu.HBM) for v in firsts))
    count = lax.axis_size("gz")
    both = lax.ppermute(both, "gz", [(i, i ^ 1) for i in range(count) if i ^ 1 < count])
    hop = [(i, i + 2) for i in range(0, count - 2, 2)] + [(i, i - 2) for i in range(3, count, 2)]
    far = lax.ppermute(both[16:32], "gz", hop) if hop else jnp.zeros_like(both[16:32])
    (pick,) = call(pick_kernel, "fill_pick", [VMEM, VMEM], [shape(9, 128, dtype=I32)])(
        receive_count, slots_out
    )
    weights2 = call(
        weights_kernel, "weights_second", [VMEM] * 2, weights + weights + [shape(14, 8, 128)],
        [((128, 128), BF16)],
    )(early, send)
    w2, wa, arrive = weights2[0:4], weights2[4:8], weights2[8]

    def first_z(*refs):
        z_kernel(5, *refs[:5], *refs[6:])

    h, hb, ya, yb = call(
        first_z, "fold_z5", [VMEM] * 5 + [pl.BlockSpec(memory_space=pl.ANY)],
        [shape(240, 128), shape(8, 256), shape(72, 128), shape(72, 128)],
    )(spot, h, hb, both, far, arrive)
    h, hb, low, high = fold(5, h, hb, ya, yb)
    second, xu, xd, mid, mass_core, mass_halo = call(
        functools.partial(gather_first_kernel, extents), "gather_first", [VMEM] * 13,
        [shape(21, 8, 128), shape(21, 384), shape(21, 384), shape(21, 384), shape(48, 128), shape(8, 256)],
        [((240, 128), F32)] + gscratch + [((176, 128), F32), ((128, 128), BF16)],
    )(live_count, spot, h, hb, low, high, now, bf, *w, pick)

    x_low, x_high = both_ways(xu, xd, "gx")
    stayed, core_stay, ends_stay = call(
        stay_kernel, "stay", [VMEM] * 8,
        [shape(21, 8, 128), shape(144, 128), shape(16, 144)],
        [((176, 1024), BF16)] * 2 + [((128, 1024), BF16)] + lrows,
    )(live_count, second, prior, early, *w2)

    def route(*refs):
        route_y_kernel(*refs[:4], *refs[5:])

    ya, yb = call(
        route, "route_y", [VMEM] * 4 + [pl.BlockSpec(memory_space=pl.ANY)], [shape(21, 384)] * 2
    )(spot, mid, x_low, x_high, ends_stay)
    ra, rb = both_pairs(ya, yb, "gy")
    zu, zd, up2, dn2, own_low, own_high, final = call(
        near_kernel, "scatter_near", [VMEM] * 10,
        [shape(24, 384)] * 2 + [shape(2, 256)] * 4 + [shape(21, 256)],
        lrows + [((21, 8, 128), F32), ((14, 8, 128), F32)] + [((16, 1024), BF16)] * 4,
    )(spot, mid, x_low, x_high, ra, rb, both, far, arrive, ends_stay)
    z_low, z_high = both_ways(zu, zd, "gz")
    low2, high2 = both_ways(up2, dn2, "gz", 2)
    h, hb, ya, yb = call(
        second_kernel, "scatter_second", [VMEM] * 15,
        [shape(144, 128), shape(8, 256), shape(48, 128), shape(48, 128)],
        lrows + [((21, 8, 128), F32), ((144, 128), F32)],
    )(
        spot, z_low, z_high, low2, high2, own_low, own_high, final, arrive, *wa,
        core_stay, ends_stay,
    )
    (bf,) = call(
        deform_kernel, "deform_second", [VMEM] * 7, [shape(9, 8, 128)],
        [((80, 1024), BF16)] * 2 + [((128, 1024), BF16)],
    )(live_count, stayed, z_low, z_high, final, send, next_affine)
    h, hb, low, high = fold(3, h, hb, ya, yb)
    (result,) = call(
        functools.partial(gather_second_kernel, extents), "gather_second", [VMEM] * 14,
        [shape(21, 1024)],
        [((144, 128), F32)] + gscratch + [((21, 8, 128), F32)],
    )(live_count, spot, h, hb, low, high, early, bf, *w2, mass_core, mass_halo)
    return result


def solution(mesh):
    spread = AXES
    in_specs = (
        P(None, None, spread), P(None, spread), P(None, None, spread), P(None, None, spread),
        P(None, "gx", "gy", "gz"), P(None, spread), P(spread, None), P(spread, None, None),
        P(spread, None, None), P(spread, None), P(spread),
    )
    return jax.shard_map(
        body, mesh=mesh, in_specs=in_specs, out_specs=P(None, spread), check_vma=False
    )
```

```python
import functools

import jax
import jax.numpy as jnp
from jax import lax
from jax.experimental import pallas as pl
from jax.experimental.pallas import tpu as pltpu
from jax.sharding import PartitionSpec as P

TIME_STEP = 0.2
APIC_SCALE = 4.0
STRESS_SCALE = 0.3
F32 = jnp.float32
BF16 = jnp.bfloat16
I32 = jnp.int32
AXES = ("gx", "gy", "gz")
VMEM = pl.BlockSpec(memory_space=pltpu.VMEM)
HBM = pl.BlockSpec(memory_space=pltpu.HBM)
CHUNKS = 8
ZROWS = 144


def contract(a, b, da, db, precision=None):
    return lax.dot_general(
        a, b, (((da,), (db,)), ((), ())), preferred_element_type=F32, precision=precision
    )


def nt(a, b):
    return contract(a, b, 1, 1)


def nn(a, b):
    return contract(a, b, 1, 0)


def split(x):
    hi = x.astype(BF16)
    return hi, (x - hi.astype(F32)).astype(BF16)


def rounded(x):
    hi = x.astype(BF16).astype(F32)
    return hi, x - hi


def spline(f):
    return 0.5 * (0.5 - f) * (0.5 - f), 0.75 - f * f, 0.5 * (0.5 + f) * (0.5 + f)


def iota(shape, axis):
    return lax.broadcasted_iota(I32, shape, axis)


def dense(ref, step, rows):
    value = ref[:, step, :] if step is not None else ref[...]
    value = value.reshape(rows, CHUNKS, 128)
    return [value[i] for i in range(rows)]


def axis_tables(fx, cell_x, count):
    low, mid, high = spline(fx)
    plain, signed = [], []
    for plane in range(count):
        is_low, is_mid, is_high = cell_x == plane, cell_x + 1 == plane, cell_x + 2 == plane
        plain.append(jnp.where(is_low, low, jnp.where(is_mid, mid, jnp.where(is_high, high, 0.0))))
        signed.append(jnp.where(is_low, -low, jnp.where(is_high, high, 0.0)))
    return plain, signed


def y_tables(fy, cell_y, chunk):
    low, mid, high = (v[chunk : chunk + 1] for v in spline(fy))
    away = iota((8, 128), 0) - (cell_y[chunk : chunk + 1] + 1)
    plain = jnp.where(away == -1, low, jnp.where(away == 0, mid, jnp.where(away == 1, high, 0.0)))
    signed = jnp.where(away == -1, -low, jnp.where(away == 1, high, 0.0))
    return plain, signed


def build_z(fz, cell_z, w_hi, w_lo, d_hi, d_lo, chunks=CHUNKS, edges_only=False):
    low, mid, high = spline(fz)
    low_h, low_l = rounded(low)
    mid_h, mid_l = rounded(mid)
    high_h, high_l = rounded(high)
    to_low = jnp.where(cell_z == 0, 129, cell_z - 1)
    to_high = cell_z + 1
    inner = iota((128, 128), 0)
    edge = iota((16, 128), 0)
    edge = jnp.where(edge < 2, edge + 128, jnp.where(edge == 2, 0, jnp.where(edge == 3, 127, 999)))
    parts = ((slice(0, 128), inner), (slice(128, ZROWS), edge))
    if edges_only:
        parts = ((slice(0, 16), edge),)
    for chunk in range(chunks):
        at = slice(chunk, chunk + 1)
        lanes = slice(chunk * 128, chunk * 128 + 128)
        for rows, index in parts:
            is_low, is_mid, is_high = index == to_low[at], index == cell_z[at], index == to_high[at]
            for plain, signed, (a, b, c) in (
                (w_hi, d_hi, (low_h, mid_h, high_h)),
                (w_lo, d_lo, (low_l, mid_l, high_l)),
            ):
                ends = jnp.where(is_high, c[at], 0.0)
                plain[rows, lanes] = jnp.where(
                    is_low, a[at], jnp.where(is_mid, b[at], ends)
                ).astype(BF16)
                signed[rows, lanes] = jnp.where(is_low, -a[at], ends).astype(BF16)


def row_of(info, i, rows=8):
    return jnp.broadcast_to(info[i : i + 1, :], (rows, 128))


def by_side(info, one, other, axis_row=3):
    return jnp.where(row_of(info, axis_row, one.shape[0]) == 0, one, other)


def by_z_side(info, one, other):
    tiles = [
        by_side(info, lane_tile(one, t), lane_tile(other, t), 4) for t in range(one.shape[1] // 128)
    ]
    return jnp.concatenate(tiles, axis=1)


def fields(ref):
    tiles = [ref[i * 8 : i * 8 + 8] for i in range(13)]
    return tiles[0:3], cells_of((tiles[3] + 0.5).astype(I32)), tiles[4:13]


def in_use(live, step):
    slots = iota((8, 128), 0) * 128 + iota((8, 128), 1)
    return (slots < jnp.broadcast_to(live[0:1, step : step + 1], (8, 128))).astype(F32)


STEPS = (0, 1, -1)


def offset_row(offset):
    place = (offset[0] + 1) * 9 + (offset[1] + 1) * 3 + offset[2] + 1
    return place - (place > 13)


def fill_send(slots, send):
    inward = [(x, y, 0) for y in STEPS for x in STEPS][1:]
    order = inward + [(x, y, 1) for y in STEPS for x in STEPS] + [None] * 3
    order += [(x, y, -1) for y in STEPS for x in STEPS]
    send[...] = jnp.zeros(send.shape, I32)
    for n, offset in enumerate(order):
        if offset is not None:
            lane = n % 4 * 32
            send[n // 4 : n // 4 + 1, lane : lane + 32] = slots[25 - offset_row(offset)]


def pick_kernel(counts, slots, pick):
    pick[...] = jnp.full(pick.shape, -1, I32)
    order = iota((1, 32), 1)
    for x in (-1, 0, 1):
        for y in (-1, 0, 1):
            for z in (-1, 0, 1):
                if (x, y, z) != (0, 0, 0):
                    n, row, lane = offset_row((x, y, z)), (x + 1) * 3 + y + 1, (z + 1) * 32
                    pick[row : row + 1, lane : lane + 32] = jnp.where(
                        order < jnp.broadcast_to(counts[0:1, n : n + 1], (1, 32)), slots[n], -1
                    )


def cells_of(centre):
    return centre // 512, centre // 128 % 4, centre % 128


def to_grid(adj, deform):
    a_v, a_c, a_f = adj[0:3], adj[3:12], adj[12:21]
    b_c = [
        a_c[3 * i + j] + TIME_STEP * sum(a_f[3 * i + m] * deform[3 * j + m] for m in range(3))
        for i in range(3)
        for j in range(3)
    ]
    return a_v, b_c


def transfer(adj, deform, affine):
    a_v, b_c = to_grid(adj, deform)
    a_f = adj[12:21]
    b_f = [
        a_f[3 * i + j] + TIME_STEP * sum(affine[3 * m + i] * a_f[3 * m + j] for m in range(3))
        for i in range(3)
        for j in range(3)
    ]
    return a_v, b_c, b_f


def scatter_rows(a_v, b_c, frac, cell_x, cell_y, l0h, l0l, l2h, l2l, chunks=CHUNKS):
    base, slope = [], []
    for c in range(3):
        base.append(a_v[c] - APIC_SCALE * sum(b_c[3 * c + j] * frac[j] for j in range(3)))
        slope.append([APIC_SCALE * b_c[3 * c + j] for j in range(3)])
    wx, wx1 = axis_tables(frac[0], cell_x, 6)
    for k in range(chunks):
        at = slice(k, k + 1)
        lanes = slice(k * 128, k * 128 + 128)
        wy, wy1 = y_tables(frac[1], cell_y, k)
        for c in range(3):
            a = wy * base[c][at] + wy1 * slope[c][1][at]
            b = wy * slope[c][0][at]
            d = wy * slope[c][2][at]
            for pair in range(3):
                rows = slice(c * 48 + pair * 16, c * 48 + pair * 16 + 16)
                planes = (2 * pair, 2 * pair + 1)
                l0 = jnp.concatenate([wx[x][at] * a + wx1[x][at] * b for x in planes], axis=0)
                l2 = jnp.concatenate([wx[x][at] * d for x in planes], axis=0)
                l0h[rows, lanes], l0l[rows, lanes] = split(l0)
                l2h[rows, lanes], l2l[rows, lanes] = split(l2)


def paired(l, w):
    l0h, l0l, l2h, l2l = l
    w_hi, w_lo, d_hi, d_lo = w
    return ((l0h, w_hi), (l0l, w_hi), (l0h, w_lo), (l2h, d_hi), (l2l, d_hi), (l2h, d_lo))


def core_sums(l, w):
    return sum(nt(a[...], b[0:128]) for a, b in paired(l, w))


def edge_sums(l, w, rows=slice(128, ZROWS), lanes=slice(0, 1024)):
    return sum(nt(b[rows, lanes], a[:, lanes]) for a, b in paired(l, w))


def put_planes(ref, at, first, second):
    width = first.shape[1]
    ref[at : at + 1, :width] = first
    ref[at + 1 : at + 2, :width] = second


def static_rows(table, send, rows, hot, put):
    hi, lo = split(table[...])
    low_row, row = iota((128, 128), 0), iota((8, 128), 0)
    for t, n in enumerate(rows):
        index = send[n : n + 1]
        hot[...] = (low_row == index % 128).astype(F32).astype(BF16)
        got = (nn(hi, hot[...]) + nn(lo, hot[...])).reshape(14, 8, 128)
        chosen = row == index // 128
        put(t, jnp.sum(jnp.where(chosen[None], got, 0.0), axis=1))


def first_kernel(
    spot, live_at, adjoint_at, fractions_at, centers_at, deform_at, affine_at, mass_at, slots_at,
    h, hb, both, bf_out, w_hi, w_lo, d_hi, d_lo, send, now, early,
    l0h, l0l, l2h, l2l, hot, zu, zd,
    live, adjoint, fractions, centers, deform, affine, mass, slots_back, arrived,
):
    sources = (slots_at, fractions_at, centers_at, deform_at, live_at, adjoint_at, affine_at, mass_at)
    places = (slots_back, fractions, centers, deform, live, adjoint, affine, mass)
    copies = [
        pltpu.make_async_copy(a, b, arrived.at[i]) for i, (a, b) in enumerate(zip(sources, places))
    ]
    for copy in copies:
        copy.start()
    w = (w_hi, w_lo, d_hi, d_lo)
    l = (l0h, l0l, l2h, l2l)
    zu[...] = jnp.zeros(zu.shape, F32)
    zd[...] = jnp.zeros(zd.shape, F32)
    for copy in copies[:3]:
        copy.wait()
    fill_send(slots_back, send)
    frac = dense(fractions, 1, 3)
    centre = centers[1:2, :].reshape(CHUNKS, 128)
    cell_x, cell_y, cell_z = cells_of(centre)
    build_z(frac[2], cell_z, *w)
    for copy in copies[3:]:
        copy.wait()
    deform_now = dense(deform, 1, 9)
    for i, tile in enumerate(frac + [centre.astype(F32)] + deform_now):
        now[i * 8 : i * 8 + 8] = tile
    early[104:112] = jnp.zeros((8, 128), F32)
    use = in_use(live, 1)
    now[104:112] = use
    now[112:120] = in_use(live, 0)
    known = dense(fractions, 0, 3) + [centers[0:1, :].reshape(CHUNKS, 128).astype(F32)]
    for i, tile in enumerate(known + dense(deform, 0, 9)):
        early[i * 8 : i * 8 + 8] = tile

    def put(t, got):
        dest = (zd, zu)[t // 3]
        dest[0:14, t % 3 * 128 : t % 3 * 128 + 128] = got

    static_rows(early, send, range(2, 8), hot, put)
    adj = [v * use for v in dense(adjoint, None, 21)]
    a_v, b_c, b_f = transfer(adj, deform_now, dense(affine, 1, 9))
    for i in range(9):
        bf_out[i] = b_f[i]
    scatter_rows(a_v, b_c, frac, cell_x, cell_y, *l)
    h[0:144] = core_sums(l, w)
    h[144:240] = jnp.zeros((96, 128), F32)
    for s in range(2):
        for x in range(4):
            row = 144 + s * 48 + (x + 1) * 8 + 1
            h[row : row + 4] = mass[s, x]
    lane, row = iota((16, 128), 1), iota((16, 128), 0)
    pick = (((row == 2) & (lane == 0)) | ((row == 3) & (lane == 127))).astype(F32)
    mass_ends = contract(pick, h[144:240], 1, 1, lax.Precision.HIGHEST)
    ends = jnp.concatenate([edge_sums(l, w), mass_ends], axis=1)
    hb[...] = jnp.zeros(hb.shape, F32)
    put_planes(hb, 0, ends[0:1], ends[1:2])
    put_planes(zu, 13, ends[0:1], ends[3:4])
    put_planes(zd, 13, ends[1:2], ends[2:3])
    both[0:16] = by_z_side(spot, zu, zd)
    both[16:32] = by_z_side(spot, zd, zu)


def wide_rows(hb):
    return jnp.concatenate(
        [hb[0:1, :128], hb[0:1, 128:], hb[1:2, :128], hb[1:2, 128:], jnp.zeros((4, 128), F32)], axis=0
    )


def from_wide(rows):
    top = jnp.concatenate([rows[0:1], rows[1:2]], axis=1)
    low = jnp.concatenate([rows[2:3], rows[3:4]], axis=1)
    return jnp.concatenate([top, low, jnp.zeros((6, 256), F32)], axis=0)


def transposed(rows):
    return jnp.concatenate([rows, jnp.zeros((120, 256), F32)], axis=0).T


def z_kernel(comps, spot, h, hb, both, far, h_out, hb_out, ya, yb):
    direct, relayed = both[13:15, 0:256], far[13:15, 0:256]
    low, high = by_z_side(spot, relayed, direct), by_z_side(spot, direct, relayed)
    z_fold(comps, spot, h, hb[...], low, high, h_out, hb_out, ya, yb)


def z_fold(comps, first, h, halo, low, high, h_out, hb_out, ya, yb):
    pad = jnp.zeros((6, 256), F32)
    halo = halo + jnp.concatenate([high[1:2], low[1:2], pad], axis=0)
    hb_out[...] = halo
    wall = transposed(jnp.concatenate([low[0:1], high[0:1], pad], axis=0))
    lane = iota((8, 128), 1)
    row = iota((8, 128), 0)
    blocks = comps * 6
    up, down = None, None
    for q in range(blocks):
        rows = slice(q * 8, q * 8 + 8)
        tile = (
            h[rows]
            + jnp.where(lane == 0, wall[rows, 0:1], 0.0)
            + jnp.where(lane == 127, wall[rows, 1:2], 0.0)
        )
        h_out[rows] = tile
        place = 2 * (q % 4)
        chosen = (row >= place) & (row < place + 2)
        a = pltpu.roll(tile, (place - 4) % 8, 0) if place != 4 else tile
        b = pltpu.roll(tile, place, 0) if place else tile
        up = jnp.where(chosen, a, 0.0 if up is None else up)
        down = jnp.where(chosen, b, 0.0 if down is None else down)
        if q % 4 == 3 or q == blocks - 1:
            out = slice(q // 4 * 8, q // 4 * 8 + 8)
            ya[out] = by_side(first, up, down)
            yb[out] = by_side(first, down, up)
            up, down = None, None
    packed = (blocks + 3) // 4 * 8
    ya[packed : packed + 8] = wide_rows(halo)
    yb[packed : packed + 8] = wide_rows(halo)


def y_kernel(comps, spot, h, hb, ra, rb, h_out, hb_out, xu, xd):
    first = spot
    row = iota((8, 128), 0)
    blocks = comps * 6
    packed = (blocks + 3) // 4 * 8
    for q in range(blocks):
        rows = slice(q * 8, q * 8 + 8)
        place = 2 * (q % 4)
        src = slice(q // 4 * 8, q // 4 * 8 + 8)
        a, b = by_side(first, rb[src], ra[src]), by_side(first, ra[src], rb[src])
        a = pltpu.roll(a, (-place) % 8, 0) if place else a
        b = pltpu.roll(b, (4 - place) % 8, 0) if place != 4 else b
        tile = (
            h[rows] + jnp.where(row < 2, a, 0.0) + jnp.where((row >= 4) & (row < 6), b, 0.0)
        )
        h_out[rows] = tile
        c, x = q // 6, q % 6
        if x >= 4:
            xu[c * 16 + (x - 4) * 8 : c * 16 + (x - 4) * 8 + 8] = tile
        if x < 2:
            xd[c * 16 + x * 8 : c * 16 + x * 8 + 8] = tile
    place = iota((8, 256), 1) % 8
    a, b = ra[packed : packed + 8], rb[packed : packed + 8]
    a, b = by_side(first, b, a), by_side(first, a, b)
    a = pltpu.roll(from_wide(a), 252, 1)
    b = pltpu.roll(from_wide(b), 4, 1)
    halo = hb[...] + jnp.where(place < 2, a, 0.0) + jnp.where((place >= 4) & (place < 6), b, 0.0)
    hb_out[...] = halo
    xu[comps * 16 : comps * 16 + 8] = wide_rows(halo)
    xd[comps * 16 : comps * 16 + 8] = wide_rows(halo)


def x_fold(comps, h, hb, from_low, from_high, total):
    for c in range(comps):
        total[c * 48 : c * 48 + 16] = h[c * 48 : c * 48 + 16] + from_low[c * 16 : c * 16 + 16]
        total[c * 48 + 16 : c * 48 + 32] = h[c * 48 + 16 : c * 48 + 32]
        total[c * 48 + 32 : c * 48 + 48] = (
            h[c * 48 + 32 : c * 48 + 48] + from_high[c * 16 : c * 16 + 16]
        )
    plane = iota((8, 256), 1) % 48 // 8
    a = pltpu.roll(from_wide(from_low[comps * 16 : comps * 16 + 8]), 224, 1)
    b = pltpu.roll(from_wide(from_high[comps * 16 : comps * 16 + 8]), 32, 1)
    return hb[...] + jnp.where(plane < 2, a, 0.0) + jnp.where(plane >= 4, b, 0.0)


def node_values(spot, extents, total, halo, mass_at, mass_halo, g_hi, g_lo):
    first_x, first_y, first_z = (row_of(spot, i) for i in range(3))
    far_x, far_y, far_z = (jnp.concatenate([v, v], axis=1) for v in (first_x, first_y, first_z))
    lane, row = iota((8, 128), 1), iota((8, 128), 0)
    node_z = first_z + lane
    node_y = first_y + row - 1
    keep_yz = (
        (node_z >= 1) & (node_z <= extents[2] - 2) & (node_y >= 1) & (node_y <= extents[1] - 2)
    )
    wide = iota((8, 256), 1)
    side = iota((8, 256), 0)
    halo_x = far_x + wide % 48 // 8 - 1
    halo_y = far_y + wide % 8 - 1
    halo_z = far_z + jnp.where(side == 0, 128, -1)
    keep = (
        (halo_x >= 1) & (halo_x <= extents[0] - 2)
        & (halo_y >= 1) & (halo_y <= extents[1] - 2)
        & (halo_z >= 1) & (halo_z <= extents[2] - 2)
        & (side < 2) & (wide < 144) & (wide % 8 < 6)
    )
    ends = jnp.where(keep, halo / jnp.where(keep, mass_halo, 1.0), 0.0)
    columns = transposed(ends)
    g_hi[:, 128:256], g_lo[:, 128:256] = split(columns[0:144])
    for x in range(6):
        node_x = first_x + x - 1
        keep_here = keep_yz & (row < 6) & (node_x >= 1) & (node_x <= extents[0] - 2)
        mass = jnp.where(keep_here, mass_at(x), 1.0)
        for c in range(3):
            rows = slice(c * 48 + x * 8, c * 48 + x * 8 + 8)
            total[rows] = jnp.where(keep_here, total[rows] / mass, 0.0)
    g_hi[:, 0:128], g_lo[:, 0:128] = split(total[0:144])


def gather(frac, cell_x, cell_y, g_hi, g_lo, w_hi, w_lo, d_hi, d_lo, s0, sz, rows12):
    a, b = g_hi[:, 0:ZROWS], g_lo[:, 0:ZROWS]
    s0[...] = nn(a, w_hi[...]) + nn(b, w_hi[...]) + nn(a, w_lo[...])
    sz[...] = nn(a, d_hi[...]) + nn(b, d_hi[...]) + nn(a, d_lo[...])
    wx, wx1 = axis_tables(frac[0], cell_x, 6)
    for k in range(CHUNKS):
        at = slice(k, k + 1)
        lanes = slice(k * 128, k * 128 + 128)
        wy, wy1 = y_tables(frac[1], cell_y, k)
        for c in range(3):
            plain = [s0[c * 48 + x * 8 : c * 48 + x * 8 + 8, lanes] for x in range(6)]
            slope = [sz[c * 48 + x * 8 : c * 48 + x * 8 + 8, lanes] for x in range(6)]
            r0 = sum(wx[x][at] * plain[x] for x in range(6))
            r1 = sum(wx1[x][at] * plain[x] for x in range(6))
            rz = sum(wx[x][at] * slope[x] for x in range(6))
            for i, v in enumerate((wy * r0, wy * r1, wy1 * r0, wy * rz)):
                rows12[c * 4 + i, at, :] = jnp.sum(v, axis=0, keepdims=True)


def particle(rows12, frac, b_f, deform, use):
    r_v = [rows12[c * 4] for c in range(3)]
    area = [rows12[c * 4 + 1 + j] - r_v[c] * frac[j] for c in range(3) for j in range(3)]
    stress = [-STRESS_SCALE * v for v in area]
    cof = []
    for i in range(3):
        for j in range(3):
            i1, i2, j1, j2 = (i + 1) % 3, (i + 2) % 3, (j + 1) % 3, (j + 2) % 3
            cof.append(
                deform[3 * i1 + j1] * deform[3 * i2 + j2] - deform[3 * i1 + j2] * deform[3 * i2 + j1]
            )
    det = sum(deform[j] * cof[j] for j in range(3))
    ratio = (stress[0] + stress[4] + stress[8]) / det
    out = r_v + area
    for i in range(3):
        for j in range(3):
            shear = sum((stress[3 * i + m] + stress[3 * m + i]) * deform[3 * m + j] for m in range(3))
            out.append(b_f[3 * i + j] + shear + ratio * cof[3 * i + j])
    return [v * use for v in out]


def gather_first_kernel(
    extents, spot, h, hb, from_low, from_high, now, bf, w_hi, w_lo, d_hi, d_lo, pick,
    second, xu, xd, mid, mass_core, mass_halo,
    total, g_hi, g_lo, s0, sz, rows12, buf, hot,
):
    halo = x_fold(5, h, hb, from_low, from_high, total)
    mass_core[...] = total[144:192]
    wide = iota((8, 256), 1)

    def spread(step):
        start = 144 + step * 48
        out = jnp.ones((8, 256), F32)
        for c in range(3):
            moved = pltpu.roll(halo, (c * 48 - start) % 256, 1)
            out = jnp.where((wide >= c * 48) & (wide < c * 48 + 48), moved, out)
        return out

    mass_halo[...] = spread(0)
    node_values(
        spot, extents, total, halo,
        lambda x: total[192 + x * 8 : 192 + x * 8 + 8], spread(1), g_hi, g_lo,
    )
    frac, (cell_x, cell_y, _), deform = fields(now)
    gather(frac, cell_x, cell_y, g_hi, g_lo, w_hi, w_lo, d_hi, d_lo, s0, sz, rows12)
    use = now[104:112]
    out = particle(rows12, frac, [bf[i] for i in range(9)], deform, use)
    for i in range(21):
        second[i] = out[i]
        buf[i * 8 : i * 8 + 8] = out[i]
    buf[168:176] = jnp.zeros((8, 128), F32)
    hi, lo = split(buf[...])
    low_row = iota((128, 128), 0)
    row = iota((8, 128), 0)
    for t in range(9):
        index = pick[t : t + 1]
        hot[...] = (low_row == index % 128).astype(F32).astype(BF16)
        got = nn(hi, hot[...]) + nn(lo, hot[...])
        chosen = (row == index // 128) & (index >= 0)
        got = got.reshape(22, 8, 128)[0:21]
        got = jnp.sum(jnp.where(chosen[None], got, 0.0), axis=1)
        dest, place = ((xd, t), (mid, t - 3), (xu, t - 6))[t // 3]
        dest[:, place * 128 : place * 128 + 128] = got


def pieces(groups, at, tiles):
    lane = iota((21, 128), 1)
    out = [jnp.zeros((21, 128), F32) for _ in range(tiles)]
    for i, group in enumerate(groups):
        place = 32 * (i % 4)
        moved = pltpu.roll(group, (place - at) % 128, 1) if place != at else group
        out[i // 4] = jnp.where((lane >= place) & (lane < place + 32), moved, out[i // 4])
    return out


def lane_tile(ref, i):
    return ref[:, i * 128 : i * 128 + 128]


def route_y_kernel(spot, mid, from_low, from_high, ya, yb):
    first = spot
    for i, ref in enumerate((mid, from_low, from_high)):
        down, up = lane_tile(ref, 0), lane_tile(ref, 2)
        ya[:, i * 128 : i * 128 + 128] = by_side(first, up, down)
        yb[:, i * 128 : i * 128 + 128] = by_side(first, down, up)


def carry(tiles, indices, lh, ll, hot, count=21):
    row, low_row = iota((8, 128), 0), iota((128, 128), 0)
    for t, (values, index) in enumerate(zip(tiles, indices)):
        lanes = slice(t * 128, t * 128 + 128)
        hot[:, lanes] = (low_row == index % 128).astype(F32).astype(BF16)
        chosen = row == index // 128
        for pair in range((count + 1) // 2):
            both = []
            for r in (2 * pair, 2 * pair + 1):
                blank = jnp.zeros((8, 128), F32)
                both.append(blank if r >= count else jnp.where(chosen, values(r), 0.0))
            rows = slice(pair * 16, pair * 16 + 16)
            lh[rows, lanes], ll[rows, lanes] = split(jnp.concatenate(both, axis=0))
    return nt(lh[...], hot[...]) + nt(ll[...], hot[...])


def weights_kernel(early, send, w_hi, w_lo, d_hi, d_lo, a_hi, a_lo, b_hi, b_lo, arrive, hot):
    frac, cells, _ = fields(early)
    build_z(frac[2], cells[2], w_hi, w_lo, d_hi, d_lo)

    def put(t, got):
        arrive[:, t, :] = got

    static_rows(early, send, (2, 3, 4, 5, 6, 7, 0, 1), hot, put)
    _, _, cell_z = cells_of((arrive[3] + 0.5).astype(I32))
    build_z(arrive[2], cell_z, a_hi, a_lo, b_hi, b_lo)


def stay_kernel(
    now, second, prior, early, w_hi, w_lo, d_hi, d_lo,
    stayed, core, ends,
    lh, ll, hot, l0h, l0l, l2h, l2l,
):
    tiles = [lambda r, t=t: second[r, t : t + 1, :] for t in range(8)]
    total = carry(tiles, [prior[t : t + 1] for t in range(8)], lh, ll, hot)
    use = now[112:120]
    adj = [total[i * 8 : i * 8 + 8] * use for i in range(21)]
    for i in range(21):
        stayed[i] = adj[i]
    frac, (cell_x, cell_y, _), deform = fields(early)
    a_v, b_c = to_grid(adj, deform)
    l, w = (l0h, l0l, l2h, l2l), (w_hi, w_lo, d_hi, d_lo)
    scatter_rows(a_v, b_c, frac, cell_x, cell_y, *l)
    core[...] = core_sums(l, w)
    ends[...] = edge_sums(l, w)


def near_kernel(
    spot, mid, x_low, x_high, ra, rb, both, far, arrive, ends_stay,
    swap, along, against, own_low, own_high, final,
    l0h, l0l, l2h, l2l, moved, static, e0, e1, e2, e3, zu, zd, up2, dn2,
):
    groups = [lane_tile(mid, 1), lane_tile(x_low, 1), lane_tile(x_high, 1)]
    groups += [by_side(spot, lane_tile(rb, i), lane_tile(ra, i)) for i in range(3)]
    groups += [by_side(spot, lane_tile(ra, i), lane_tile(rb, i)) for i in range(3)]
    zu[...] = jnp.zeros(zu.shape, F32)
    zd[...] = jnp.zeros(zd.shape, F32)
    direct, relayed = both[0:16], far[...]
    static_low = by_z_side(spot, relayed, direct)
    static_high = by_z_side(spot, direct, relayed)
    for ref, at, first, known in ((zu, 64, 0, static_high), (zd, 0, 3, static_low)):
        for i, tile in enumerate(pieces(groups, at, 3)):
            ref[0:21, i * 128 : i * 128 + 128] = tile
            moved[:, first + i, :] = tile
            static[:, first + i, :] = lane_tile(known, i)[0:14]
    for i, tile in enumerate(pieces(groups[1:], 32, 2)):
        final[:, i * 128 : i * 128 + 128] = tile
        moved[:, 6 + i, :] = tile
        static[:, 6 + i, :] = arrive[:, 6 + i, :]
    l = (l0h, l0l, l2h, l2l)
    e = (e0, e1, e2, e3)
    place = [static[i] for i in range(3)]
    cell_x, cell_y, cell_z = cells_of((static[3] + 0.5).astype(I32))
    build_z(place[2], cell_z, *e, edges_only=True)
    a_v, b_c = to_grid([moved[i] for i in range(21)], [static[4 + i] for i in range(9)])
    scatter_rows(a_v, b_c, place, cell_x, cell_y, *l)
    upward = edge_sums(l, e, slice(0, 16), slice(0, 384))
    downward = edge_sums(l, e, slice(0, 16), slice(384, 768))
    ends = edge_sums(l, e, slice(0, 16), slice(768, 1024)) + ends_stay[...]
    for ref in (up2, dn2, own_low, own_high):
        ref[...] = jnp.zeros(ref.shape, F32)
    put_planes(up2, 0, upward[0:1], upward[3:4])
    put_planes(own_high, 0, upward[1:2], upward[2:3])
    put_planes(own_low, 0, downward[0:1], downward[3:4])
    put_planes(dn2, 0, downward[1:2], downward[2:3])
    put_planes(zu, 21, ends[0:1], ends[3:4])
    put_planes(zd, 21, ends[1:2], ends[2:3])
    swap[0:24] = by_z_side(spot, zu, zd)
    swap[24:48] = by_z_side(spot, zd, zu)
    along[...] = by_z_side(spot, up2, dn2)
    against[...] = by_z_side(spot, dn2, up2)


def second_kernel(
    spot, both, far, against, own_low, own_high, final, arrive, a_hi, a_lo, b_hi, b_lo,
    core_stay, ends_stay,
    h_out, hb_out, ya, yb, moved,
    l0h, l0l, l2h, l2l, h,
):
    for i in range(3):
        near, relayed = lane_tile(both, i)[0:24], lane_tile(far, i)
        moved[:, i, :] = by_side(spot, relayed, near, 4)[0:21]
        moved[:, 3 + i, :] = by_side(spot, near, relayed, 4)[0:21]
    for i in range(2):
        moved[:, 6 + i, :] = lane_tile(final, i)
    place = [arrive[i] for i in range(3)]
    cell_x, cell_y, _ = cells_of((arrive[3] + 0.5).astype(I32))
    a_v, b_c = to_grid([moved[i] for i in range(21)], [arrive[4 + i] for i in range(9)])
    l, w = (l0h, l0l, l2h, l2l), (a_hi, a_lo, b_hi, b_lo)
    scatter_rows(a_v, b_c, place, cell_x, cell_y, *l)
    h[...] = core_sums(l, w) + core_stay[...]
    ends = edge_sums(l, w) + ends_stay[...]
    ends = jnp.concatenate([ends[0:8], jnp.zeros((8, 112), F32)], axis=1)
    halo = jnp.where(iota((8, 256), 0) < 2, ends, 0.0)
    near, relayed = both[21:23, 0:256] + against[0:2], far[21:23, 0:256]
    low = by_z_side(spot, relayed, near) + own_low[0:2]
    high = by_z_side(spot, near, relayed) + own_high[0:2]
    z_fold(3, spot, h, halo, low, high, h_out, hb_out, ya, yb)


def relay_kernel(both, along, _, out):
    out[...] = both[24:48]
    out[21:23, 0:256] = both[45:47, 0:256] + along[0:2]


def deform_kernel(now, stayed, moved, send, affine, bf_out, lh, ll, hot):
    tiles = [lambda r, t=t: moved[12 + r, t : t + 1, :] for t in range(8)]
    rows = [send[t : t + 1] for t in (2, 3, 4, 5, 6, 7, 0, 1)]
    total = carry(tiles, rows, lh, ll, hot, 9)
    use = now[112:120]
    a_f = [(stayed[12 + i] + total[i * 8 : i * 8 + 8]) * use for i in range(9)]
    k = dense(affine, 0, 9)
    for i in range(3):
        for j in range(3):
            bf_out[3 * i + j] = a_f[3 * i + j] + TIME_STEP * sum(
                k[3 * m + i] * a_f[3 * m + j] for m in range(3)
            )


def gather_second_kernel(
    extents, spot, h, hb, from_low, from_high, now, early, bf, w_hi, w_lo, d_hi, d_lo,
    mass_core, mass_halo,
    result,
    total, g_hi, g_lo, s0, sz, rows12, packed,
):
    halo = x_fold(3, h, hb, from_low, from_high, total)
    node_values(
        spot, extents, total, halo,
        lambda x: mass_core[x * 8 : x * 8 + 8], mass_halo[...], g_hi, g_lo,
    )
    frac, (cell_x, cell_y, _), deform = fields(early)
    gather(frac, cell_x, cell_y, g_hi, g_lo, w_hi, w_lo, d_hi, d_lo, s0, sz, rows12)
    use = now[112:120]
    out = particle(rows12, frac, [bf[i] for i in range(9)], deform, use)
    for i in range(21):
        packed[i] = out[i]
    for k in range(CHUNKS):
        result[:, k * 128 : k * 128 + 128] = packed[:, k, :]


def shape(*dims, dtype=F32):
    return jax.ShapeDtypeStruct(dims, dtype)


def call(kernel, name, specs, outs, scratch=()):
    return pl.pallas_call(
        kernel,
        name=name,
        in_specs=list(specs),
        out_specs=[VMEM] * len(outs),
        out_shape=list(outs),
        scratch_shapes=[pltpu.VMEM(*v) if isinstance(v, tuple) else v for v in scratch],
        compiler_params=pltpu.CompilerParams(vmem_limit_bytes=40 * 1024 * 1024),
    )


def both_ways(up, down, axis, step=1):
    count = lax.axis_size(axis)
    low = lax.ppermute(up, axis, [(i, i + step) for i in range(count - step)])
    high = lax.ppermute(down, axis, [(i + step, i) for i in range(count - step)])
    return low, high


def both_pairs(first, second, axis):
    count = lax.axis_size(axis)
    a = [(i, i ^ 1) for i in range(count) if i ^ 1 < count]
    b = [p for i in range(1, count - 1, 2) for p in ((i, i + 1), (i + 1, i))]
    ra = lax.ppermute(first, axis, a)
    rb = lax.ppermute(second, axis, b) if b else jnp.zeros_like(second)
    return ra, rb


def body(
    fractions, centers, deform, next_affine, cell_mass, final_adjoint,
    live_count, send_slot, receive_slot, receive_count, prior_slot,
):
    at_y = lax.axis_index("gy")
    at_z = lax.axis_index("gz")
    spot = [lax.axis_index("gx") * 4, at_y * 4, at_z * 128, at_y % 2, at_z % 2]
    spot = jnp.stack(spot + [jnp.zeros_like(at_y)] * 3).astype(I32)
    spot = jnp.broadcast_to(spot[:, None], (8, 128))
    extents = (lax.axis_size("gx") * 4, lax.axis_size("gy") * 4, lax.axis_size("gz") * 128)

    fractions, deform, next_affine = (
        jnp.transpose(v, (1, 0, 2)) for v in (fractions, deform, next_affine)
    )
    slots_back = jnp.transpose(send_slot, (1, 0, 2))
    slots_out = jnp.transpose(receive_slot, (1, 0, 2))
    prior = prior_slot.reshape(8, 128)

    wide = shape(ZROWS, 1024, dtype=BF16)
    weights = [wide] * 4
    lrows = [((144, 1024), BF16)] * 4
    gscratch = [
        ((144, 256), BF16), ((144, 256), BF16),
        ((144, 1024), F32), ((144, 1024), F32), ((12, 8, 128), F32),
    ]

    def fold(comps, h, hb, ya, yb):
        ra, rb = both_pairs(ya, yb, "gy")
        rows = comps * 16 + 8
        h, hb, xu, xd = call(
            functools.partial(y_kernel, comps), f"fold_y{comps}", [VMEM] * 5,
            [shape(comps * 48, 128), shape(8, 256), shape(rows, 128), shape(rows, 128)],
        )(spot, h, hb, ra, rb)
        low, high = both_ways(xu, xd, "gx")
        return h, hb, low, high

    firsts = (
        live_count, final_adjoint, fractions, centers, deform, next_affine, cell_mass, slots_back
    )
    h, hb, both, bf, *w, send, now, early = call(
        first_kernel, "scatter_first", [VMEM] + [HBM] * 8,
        [shape(240, 128), shape(8, 256), shape(32, 384), shape(9, 8, 128)]
        + weights + [shape(8, 128, dtype=I32), shape(120, 128), shape(112, 128)],
        lrows + [((128, 128), BF16), ((16, 384), F32), ((16, 384), F32)]
        + [(v.shape, v.dtype) for v in firsts] + [pltpu.SemaphoreType.DMA((8,))],
    )(spot, *(pltpu.with_memory_space_constraint(v, pltpu.HBM) for v in firsts))
    count = lax.axis_size("gz")
    pairs = [(i, i ^ 1) for i in range(count) if i ^ 1 < count]
    hop = [(i, i + 2) for i in range(0, count - 2, 2)] + [(i, i - 2) for i in range(3, count, 2)]
    both = lax.ppermute(both, "gz", pairs)
    far = lax.ppermute(both[16:32], "gz", hop)
    (pick,) = call(pick_kernel, "fill_pick", [VMEM, VMEM], [shape(9, 128, dtype=I32)])(
        receive_count, slots_out
    )
    weights2 = call(
        weights_kernel, "weights_second", [VMEM] * 2, weights + weights + [shape(14, 8, 128)],
        [((128, 128), BF16)],
    )(early, send)
    w2, wa, arrive = weights2[0:4], weights2[4:8], weights2[8]

    def first_z(*refs):
        z_kernel(5, *refs[:5], *refs[6:])

    h, hb, ya, yb = call(
        first_z, "fold_z5", [VMEM] * 5 + [pl.BlockSpec(memory_space=pl.ANY)],
        [shape(240, 128), shape(8, 256), shape(72, 128), shape(72, 128)],
    )(spot, h, hb, both, far, arrive)
    h, hb, low, high = fold(5, h, hb, ya, yb)
    second, xu, xd, mid, mass_core, mass_halo = call(
        functools.partial(gather_first_kernel, extents), "gather_first", [VMEM] * 12,
        [shape(21, 8, 128), shape(21, 384), shape(21, 384), shape(21, 384), shape(48, 128), shape(8, 256)],
        [((240, 128), F32)] + gscratch + [((176, 128), F32), ((128, 128), BF16)],
    )(spot, h, hb, low, high, now, bf, *w, pick)

    x_low, x_high = both_ways(xu, xd, "gx")
    stayed, core_stay, ends_stay = call(
        stay_kernel, "stay", [VMEM] * 8,
        [shape(21, 8, 128), shape(144, 128), shape(16, 144)],
        [((176, 1024), BF16)] * 2 + [((128, 1024), BF16)] + lrows,
    )(now, second, prior, early, *w2)

    def route(*refs):
        route_y_kernel(*refs[:4], *refs[5:])

    ya, yb = call(
        route, "route_y", [VMEM] * 4 + [pl.BlockSpec(memory_space=pl.ANY)], [shape(21, 384)] * 2
    )(spot, mid, x_low, x_high, ends_stay)
    ra, rb = both_pairs(ya, yb, "gy")
    swap, along, against, own_low, own_high, final = call(
        near_kernel, "scatter_near", [VMEM] * 10,
        [shape(48, 384)] + [shape(2, 256)] * 4 + [shape(21, 256)],
        lrows + [((21, 8, 128), F32), ((14, 8, 128), F32)] + [((16, 1024), BF16)] * 4
        + [((24, 384), F32)] * 2 + [((2, 256), F32)] * 2,
    )(spot, mid, x_low, x_high, ra, rb, both, far, arrive, ends_stay)
    both = lax.ppermute(swap, "gz", pairs)
    against = lax.ppermute(against, "gz", [(b, a) for a, b in hop])
    (far,) = call(
        relay_kernel, "relay", [VMEM] * 2 + [pl.BlockSpec(memory_space=pl.ANY)], [shape(24, 384)]
    )(both, along, against)
    far = lax.ppermute(far, "gz", hop)
    h, hb, ya, yb, moved = call(
        second_kernel, "scatter_second", [VMEM] * 14,
        [shape(144, 128), shape(8, 256), shape(48, 128), shape(48, 128), shape(21, 8, 128)],
        lrows + [((144, 128), F32)],
    )(
        spot, both, far, against, own_low, own_high, final, arrive, *wa, core_stay, ends_stay
    )
    (bf,) = call(
        deform_kernel, "deform_second", [VMEM] * 5, [shape(9, 8, 128)],
        [((80, 1024), BF16)] * 2 + [((128, 1024), BF16)],
    )(now, stayed, moved, send, next_affine)
    h, hb, low, high = fold(3, h, hb, ya, yb)
    (result,) = call(
        functools.partial(gather_second_kernel, extents), "gather_second", [VMEM] * 14,
        [shape(21, 1024)],
        [((144, 128), F32)] + gscratch + [((21, 8, 128), F32)],
    )(spot, h, hb, low, high, now, early, bf, *w2, mass_core, mass_halo)
    return result


def solution(mesh):
    spread = AXES
    in_specs = (
        P(None, None, spread), P(None, spread), P(None, None, spread), P(None, None, spread),
        P(None, "gx", "gy", "gz"), P(None, spread), P(spread, None), P(spread, None, None),
        P(spread, None, None), P(spread, None), P(spread),
    )
    return jax.shard_map(
        body, mesh=mesh, in_specs=in_specs, out_specs=P(None, spread), check_vma=False
    )
```

```python
import functools

import jax
import jax.numpy as jnp
from jax import lax
from jax.experimental import pallas as pl
from jax.experimental.pallas import tpu as pltpu
from jax.sharding import PartitionSpec as P

TIME_STEP = 0.2
APIC_SCALE = 4.0
STRESS_SCALE = 0.3
F32 = jnp.float32
BF16 = jnp.bfloat16
I32 = jnp.int32
AXES = ("gx", "gy", "gz")
VMEM = pl.BlockSpec(memory_space=pltpu.VMEM)
HBM = pl.BlockSpec(memory_space=pltpu.HBM)
CHUNKS = 8
ZROWS = 144


def contract(a, b, da, db, precision=None):
    return lax.dot_general(
        a, b, (((da,), (db,)), ((), ())), preferred_element_type=F32, precision=precision
    )


def nt(a, b):
    return contract(a, b, 1, 1)


def nn(a, b):
    return contract(a, b, 1, 0)


def split(x):
    hi = x.astype(BF16)
    return hi, (x - hi.astype(F32)).astype(BF16)


def rounded(x):
    hi = x.astype(BF16).astype(F32)
    return hi, x - hi


def spline(f):
    return 0.5 * (0.5 - f) * (0.5 - f), 0.75 - f * f, 0.5 * (0.5 + f) * (0.5 + f)


def iota(shape, axis):
    return lax.broadcasted_iota(I32, shape, axis)


def dense(ref, step, rows):
    value = ref[:, step, :] if step is not None else ref[...]
    value = value.reshape(rows, CHUNKS, 128)
    return [value[i] for i in range(rows)]


def axis_tables(fx, cell_x, count):
    low, mid, high = spline(fx)
    plain, signed = [], []
    for plane in range(count):
        is_low, is_mid, is_high = cell_x == plane, cell_x + 1 == plane, cell_x + 2 == plane
        plain.append(jnp.where(is_low, low, jnp.where(is_mid, mid, jnp.where(is_high, high, 0.0))))
        signed.append(jnp.where(is_low, -low, jnp.where(is_high, high, 0.0)))
    return plain, signed


def y_tables(fy, cell_y, chunk):
    low, mid, high = (v[chunk : chunk + 1] for v in spline(fy))
    away = iota((8, 128), 0) - (cell_y[chunk : chunk + 1] + 1)
    plain = jnp.where(away == -1, low, jnp.where(away == 0, mid, jnp.where(away == 1, high, 0.0)))
    signed = jnp.where(away == -1, -low, jnp.where(away == 1, high, 0.0))
    return plain, signed


def build_z(fz, cell_z, w_hi, w_lo, d_hi, d_lo, chunks=CHUNKS, edges_only=False):
    low, mid, high = spline(fz)
    low_h, low_l = rounded(low)
    mid_h, mid_l = rounded(mid)
    high_h, high_l = rounded(high)
    to_low = jnp.where(cell_z == 0, 129, cell_z - 1)
    to_high = cell_z + 1
    inner = iota((128, 128), 0)
    edge = iota((16, 128), 0)
    edge = jnp.where(edge < 2, edge + 128, jnp.where(edge == 2, 0, jnp.where(edge == 3, 127, 999)))
    parts = ((slice(0, 128), inner), (slice(128, ZROWS), edge))
    if edges_only:
        parts = ((slice(0, 16), edge),)
    for chunk in range(chunks):
        at = slice(chunk, chunk + 1)
        lanes = slice(chunk * 128, chunk * 128 + 128)
        for rows, index in parts:
            is_low, is_mid, is_high = index == to_low[at], index == cell_z[at], index == to_high[at]
            for plain, signed, (a, b, c) in (
                (w_hi, d_hi, (low_h, mid_h, high_h)),
                (w_lo, d_lo, (low_l, mid_l, high_l)),
            ):
                ends = jnp.where(is_high, c[at], 0.0)
                plain[rows, lanes] = jnp.where(
                    is_low, a[at], jnp.where(is_mid, b[at], ends)
                ).astype(BF16)
                signed[rows, lanes] = jnp.where(is_low, -a[at], ends).astype(BF16)


def row_of(info, i, rows=8):
    return jnp.broadcast_to(info[i : i + 1, :], (rows, 128))


def by_side(info, one, other, axis_row=3):
    return jnp.where(row_of(info, axis_row, one.shape[0]) == 0, one, other)


def by_z_side(info, one, other):
    tiles = [
        by_side(info, lane_tile(one, t), lane_tile(other, t), 4) for t in range(one.shape[1] // 128)
    ]
    return jnp.concatenate(tiles, axis=1)


def fields(ref):
    tiles = [ref[i * 8 : i * 8 + 8] for i in range(13)]
    return tiles[0:3], cells_of((tiles[3] + 0.5).astype(I32)), tiles[4:13]


def in_use(live, step):
    slots = iota((8, 128), 0) * 128 + iota((8, 128), 1)
    return (slots < jnp.broadcast_to(live[0:1, step : step + 1], (8, 128))).astype(F32)


STEPS = (0, 1, -1)


def offset_row(offset):
    place = (offset[0] + 1) * 9 + (offset[1] + 1) * 3 + offset[2] + 1
    return place - (place > 13)


def fill_send(slots, send):
    inward = [(x, y, 0) for y in STEPS for x in STEPS][1:]
    order = inward + [(x, y, 1) for y in STEPS for x in STEPS] + [None] * 3
    order += [(x, y, -1) for y in STEPS for x in STEPS]
    send[...] = jnp.zeros(send.shape, I32)
    for n, offset in enumerate(order):
        if offset is not None:
            lane = n % 4 * 32
            send[n // 4 : n // 4 + 1, lane : lane + 32] = slots[25 - offset_row(offset)]


def pick_kernel(counts, slots, pick):
    pick[...] = jnp.full(pick.shape, -1, I32)
    order = iota((1, 32), 1)
    for x in (-1, 0, 1):
        for y in (-1, 0, 1):
            for z in (-1, 0, 1):
                if (x, y, z) != (0, 0, 0):
                    n, row, lane = offset_row((x, y, z)), (x + 1) * 3 + y + 1, (z + 1) * 32
                    pick[row : row + 1, lane : lane + 32] = jnp.where(
                        order < jnp.broadcast_to(counts[0:1, n : n + 1], (1, 32)), slots[n], -1
                    )


def cells_of(centre):
    return centre >> 9, (centre >> 7) & 3, centre & 127


def to_grid(adj, deform):
    a_v, a_c, a_f = adj[0:3], adj[3:12], adj[12:21]
    b_c = [
        a_c[3 * i + j] + TIME_STEP * sum(a_f[3 * i + m] * deform[3 * j + m] for m in range(3))
        for i in range(3)
        for j in range(3)
    ]
    return a_v, b_c


def transfer(adj, deform, affine):
    a_v, b_c = to_grid(adj, deform)
    a_f = adj[12:21]
    b_f = [
        a_f[3 * i + j] + TIME_STEP * sum(affine[3 * m + i] * a_f[3 * m + j] for m in range(3))
        for i in range(3)
        for j in range(3)
    ]
    return a_v, b_c, b_f


def scatter_rows(a_v, b_c, frac, cell_x, cell_y, l0h, l0l, l2h, l2l, chunks=CHUNKS):
    base, slope = [], []
    for c in range(3):
        base.append(a_v[c] - APIC_SCALE * sum(b_c[3 * c + j] * frac[j] for j in range(3)))
        slope.append([APIC_SCALE * b_c[3 * c + j] for j in range(3)])
    wx, wx1 = axis_tables(frac[0], cell_x, 6)
    for k in range(chunks):
        at = slice(k, k + 1)
        lanes = slice(k * 128, k * 128 + 128)
        wy, wy1 = y_tables(frac[1], cell_y, k)
        for c in range(3):
            a = wy * base[c][at] + wy1 * slope[c][1][at]
            b = wy * slope[c][0][at]
            d = wy * slope[c][2][at]
            for pair in range(3):
                rows = slice(c * 48 + pair * 16, c * 48 + pair * 16 + 16)
                planes = (2 * pair, 2 * pair + 1)
                l0 = jnp.concatenate([wx[x][at] * a + wx1[x][at] * b for x in planes], axis=0)
                l2 = jnp.concatenate([wx[x][at] * d for x in planes], axis=0)
                l0h[rows, lanes], l0l[rows, lanes] = split(l0)
                l2h[rows, lanes], l2l[rows, lanes] = split(l2)


def paired(l, w):
    l0h, l0l, l2h, l2l = l
    w_hi, w_lo, d_hi, d_lo = w
    return ((l0h, w_hi), (l0l, w_hi), (l0h, w_lo), (l2h, d_hi), (l2l, d_hi), (l2h, d_lo))


def all_sums(l, w):
    full = sum(nt(a[...], b[...]) for a, b in paired(l, w))
    tail = jnp.concatenate([full[:, 128:ZROWS], jnp.zeros((144, 112), F32)], axis=1)
    tail = jnp.concatenate([tail, jnp.zeros((112, 128), F32)], axis=0).T
    return full[:, 0:128], tail[0:16, 0:144]


def edge_sums(l, w, rows=slice(128, ZROWS), lanes=slice(0, 1024)):
    return sum(nt(b[rows, lanes], a[:, lanes]) for a, b in paired(l, w))


def put_planes(ref, at, first, second):
    width = first.shape[1]
    ref[at : at + 1, :width] = first
    ref[at + 1 : at + 2, :width] = second


def static_rows(table, send, rows, hot, put):
    hi, lo = split(table[...])
    low_row, row = iota((128, 128), 0), iota((8, 128), 0)
    for t, n in enumerate(rows):
        index = send[n : n + 1]
        hot[...] = (low_row == (index & 127)).astype(F32).astype(BF16)
        got = (nn(hi, hot[...]) + nn(lo, hot[...])).reshape(14, 8, 128)
        chosen = row == (index >> 7)
        put(t, jnp.sum(jnp.where(chosen[None], got, 0.0), axis=1))


def first_kernel(
    spot, live_at, adjoint_at, fractions_at, centers_at, deform_at, affine_at, mass_at, slots_at,
    h, hb, both, bf_out, w_hi, w_lo, d_hi, d_lo, send, now, early,
    l0h, l0l, l2h, l2l, hot, zu, zd,
    live, adjoint, fractions, centers, deform, affine, mass, slots_back, arrived,
):
    sources = (slots_at, fractions_at, centers_at, deform_at, live_at, adjoint_at, affine_at, mass_at)
    places = (slots_back, fractions, centers, deform, live, adjoint, affine, mass)
    copies = [
        pltpu.make_async_copy(a, b, arrived.at[i]) for i, (a, b) in enumerate(zip(sources, places))
    ]
    for copy in copies:
        copy.start()
    w = (w_hi, w_lo, d_hi, d_lo)
    l = (l0h, l0l, l2h, l2l)
    zu[...] = jnp.zeros(zu.shape, F32)
    zd[...] = jnp.zeros(zd.shape, F32)
    for copy in copies[:3]:
        copy.wait()
    fill_send(slots_back, send)
    frac = dense(fractions, 1, 3)
    centre = centers[1:2, :].reshape(CHUNKS, 128)
    cell_x, cell_y, cell_z = cells_of(centre)
    build_z(frac[2], cell_z, *w)
    for copy in copies[3:]:
        copy.wait()
    deform_now = dense(deform, 1, 9)
    for i, tile in enumerate(frac + [centre.astype(F32)] + deform_now):
        now[i * 8 : i * 8 + 8] = tile
    early[104:112] = jnp.zeros((8, 128), F32)
    use = in_use(live, 1)
    now[104:112] = use
    now[112:120] = in_use(live, 0)
    known = dense(fractions, 0, 3) + [centers[0:1, :].reshape(CHUNKS, 128).astype(F32)]
    for i, tile in enumerate(known + dense(deform, 0, 9)):
        early[i * 8 : i * 8 + 8] = tile

    def put(t, got):
        dest = (zd, zu)[t // 3]
        dest[0:14, t % 3 * 128 : t % 3 * 128 + 128] = got

    static_rows(early, send, range(2, 8), hot, put)
    adj = [v * use for v in dense(adjoint, None, 21)]
    a_v, b_c, b_f = transfer(adj, deform_now, dense(affine, 1, 9))
    for i in range(9):
        bf_out[i] = b_f[i]
    scatter_rows(a_v, b_c, frac, cell_x, cell_y, *l)
    core, ends = all_sums(l, w)
    h[0:144] = core
    h[144:240] = jnp.zeros((96, 128), F32)
    for s in range(2):
        for x in range(4):
            row = 144 + s * 48 + (x + 1) * 8 + 1
            h[row : row + 4] = mass[s, x]
    lane, row = iota((16, 128), 1), iota((16, 128), 0)
    pick = (((row == 2) & (lane == 0)) | ((row == 3) & (lane == 127))).astype(F32)
    mass_ends = contract(pick, h[144:240], 1, 1, lax.Precision.HIGHEST)
    ends = jnp.concatenate([ends, mass_ends], axis=1)
    hb[...] = jnp.zeros(hb.shape, F32)
    put_planes(hb, 0, ends[0:1], ends[1:2])
    put_planes(zu, 13, ends[0:1], ends[3:4])
    put_planes(zd, 13, ends[1:2], ends[2:3])
    both[0:16] = by_z_side(spot, zu, zd)
    both[16:32] = by_z_side(spot, zd, zu)


def wide_rows(hb):
    return jnp.concatenate(
        [hb[0:1, :128], hb[0:1, 128:], hb[1:2, :128], hb[1:2, 128:], jnp.zeros((4, 128), F32)], axis=0
    )


def from_wide(rows):
    top = jnp.concatenate([rows[0:1], rows[1:2]], axis=1)
    low = jnp.concatenate([rows[2:3], rows[3:4]], axis=1)
    return jnp.concatenate([top, low, jnp.zeros((6, 256), F32)], axis=0)


def transposed(rows):
    return jnp.concatenate([rows, jnp.zeros((120, 256), F32)], axis=0).T


def z_kernel(comps, spot, h, hb, both, far, h_out, hb_out, ya, yb):
    direct, relayed = both[13:15, 0:256], far[13:15, 0:256]
    low, high = by_z_side(spot, relayed, direct), by_z_side(spot, direct, relayed)
    z_fold(comps, spot, h, hb[...], low, high, h_out, hb_out, ya, yb)


def z_fold(comps, first, h, halo, low, high, h_out, hb_out, ya, yb):
    pad = jnp.zeros((6, 256), F32)
    halo = halo + jnp.concatenate([high[1:2], low[1:2], pad], axis=0)
    hb_out[...] = halo
    wall = transposed(jnp.concatenate([low[0:1], high[0:1], pad], axis=0))
    lane = iota((8, 128), 1)
    row = iota((8, 128), 0)
    blocks = comps * 6
    up, down = None, None
    for q in range(blocks):
        rows = slice(q * 8, q * 8 + 8)
        tile = (
            h[rows]
            + jnp.where(lane == 0, wall[rows, 0:1], 0.0)
            + jnp.where(lane == 127, wall[rows, 1:2], 0.0)
        )
        h_out[rows] = tile
        place = 2 * (q % 4)
        chosen = (row >= place) & (row < place + 2)
        a = pltpu.roll(tile, (place - 4) % 8, 0) if place != 4 else tile
        b = pltpu.roll(tile, place, 0) if place else tile
        up = jnp.where(chosen, a, 0.0 if up is None else up)
        down = jnp.where(chosen, b, 0.0 if down is None else down)
        if q % 4 == 3 or q == blocks - 1:
            out = slice(q // 4 * 8, q // 4 * 8 + 8)
            ya[out] = by_side(first, up, down)
            yb[out] = by_side(first, down, up)
            up, down = None, None
    packed = (blocks + 3) // 4 * 8
    ya[packed : packed + 8] = wide_rows(halo)
    yb[packed : packed + 8] = wide_rows(halo)


def y_kernel(comps, spot, h, hb, ra, rb, h_out, hb_out, xu, xd):
    first = spot
    row = iota((8, 128), 0)
    blocks = comps * 6
    packed = (blocks + 3) // 4 * 8
    for q in range(blocks):
        rows = slice(q * 8, q * 8 + 8)
        place = 2 * (q % 4)
        src = slice(q // 4 * 8, q // 4 * 8 + 8)
        a, b = by_side(first, rb[src], ra[src]), by_side(first, ra[src], rb[src])
        a = pltpu.roll(a, (-place) % 8, 0) if place else a
        b = pltpu.roll(b, (4 - place) % 8, 0) if place != 4 else b
        tile = (
            h[rows] + jnp.where(row < 2, a, 0.0) + jnp.where((row >= 4) & (row < 6), b, 0.0)
        )
        h_out[rows] = tile
        c, x = q // 6, q % 6
        if x >= 4:
            xu[c * 16 + (x - 4) * 8 : c * 16 + (x - 4) * 8 + 8] = tile
        if x < 2:
            xd[c * 16 + x * 8 : c * 16 + x * 8 + 8] = tile
    place = iota((8, 256), 1) % 8
    a, b = ra[packed : packed + 8], rb[packed : packed + 8]
    a, b = by_side(first, b, a), by_side(first, a, b)
    a = pltpu.roll(from_wide(a), 252, 1)
    b = pltpu.roll(from_wide(b), 4, 1)
    halo = hb[...] + jnp.where(place < 2, a, 0.0) + jnp.where((place >= 4) & (place < 6), b, 0.0)
    hb_out[...] = halo
    xu[comps * 16 : comps * 16 + 8] = wide_rows(halo)
    xd[comps * 16 : comps * 16 + 8] = wide_rows(halo)


def x_fold(comps, h, hb, from_low, from_high, total):
    for c in range(comps):
        total[c * 48 : c * 48 + 16] = h[c * 48 : c * 48 + 16] + from_low[c * 16 : c * 16 + 16]
        total[c * 48 + 16 : c * 48 + 32] = h[c * 48 + 16 : c * 48 + 32]
        total[c * 48 + 32 : c * 48 + 48] = (
            h[c * 48 + 32 : c * 48 + 48] + from_high[c * 16 : c * 16 + 16]
        )
    plane = iota((8, 256), 1) % 48 // 8
    a = pltpu.roll(from_wide(from_low[comps * 16 : comps * 16 + 8]), 224, 1)
    b = pltpu.roll(from_wide(from_high[comps * 16 : comps * 16 + 8]), 32, 1)
    return hb[...] + jnp.where(plane < 2, a, 0.0) + jnp.where(plane >= 4, b, 0.0)


def node_values(spot, extents, total, halo, mass_at, mass_halo, g_hi, g_lo):
    first_x, first_y, first_z = (row_of(spot, i) for i in range(3))
    far_x, far_y, far_z = (jnp.concatenate([v, v], axis=1) for v in (first_x, first_y, first_z))
    lane, row = iota((8, 128), 1), iota((8, 128), 0)
    node_z = first_z + lane
    node_y = first_y + row - 1
    keep_yz = (
        (node_z >= 1) & (node_z <= extents[2] - 2) & (node_y >= 1) & (node_y <= extents[1] - 2)
    )
    wide = iota((8, 256), 1)
    side = iota((8, 256), 0)
    halo_x = far_x + wide % 48 // 8 - 1
    halo_y = far_y + wide % 8 - 1
    halo_z = far_z + jnp.where(side == 0, 128, -1)
    keep = (
        (halo_x >= 1) & (halo_x <= extents[0] - 2)
        & (halo_y >= 1) & (halo_y <= extents[1] - 2)
        & (halo_z >= 1) & (halo_z <= extents[2] - 2)
        & (side < 2) & (wide < 144) & (wide % 8 < 6)
    )
    ends = jnp.where(keep, halo / jnp.where(keep, mass_halo, 1.0), 0.0)
    columns = transposed(ends)
    g_hi[:, 128:256], g_lo[:, 128:256] = split(columns[0:144])
    for x in range(6):
        node_x = first_x + x - 1
        keep_here = keep_yz & (row < 6) & (node_x >= 1) & (node_x <= extents[0] - 2)
        mass = jnp.where(keep_here, mass_at(x), 1.0)
        for c in range(3):
            rows = slice(c * 48 + x * 8, c * 48 + x * 8 + 8)
            total[rows] = jnp.where(keep_here, total[rows] / mass, 0.0)
    g_hi[:, 0:128], g_lo[:, 0:128] = split(total[0:144])


def gather(frac, cell_x, cell_y, g_hi, g_lo, w_hi, w_lo, d_hi, d_lo, s0, sz, rows12):
    a, b = g_hi[:, 0:ZROWS], g_lo[:, 0:ZROWS]
    s0[...] = nn(a, w_hi[...]) + nn(b, w_hi[...]) + nn(a, w_lo[...])
    sz[...] = nn(a, d_hi[...]) + nn(b, d_hi[...]) + nn(a, d_lo[...])
    wx, wx1 = axis_tables(frac[0], cell_x, 6)
    for k in range(CHUNKS):
        at = slice(k, k + 1)
        lanes = slice(k * 128, k * 128 + 128)
        wy, wy1 = y_tables(frac[1], cell_y, k)
        for c in range(3):
            plain = [s0[c * 48 + x * 8 : c * 48 + x * 8 + 8, lanes] for x in range(6)]
            slope = [sz[c * 48 + x * 8 : c * 48 + x * 8 + 8, lanes] for x in range(6)]
            r0 = sum(wx[x][at] * plain[x] for x in range(6))
            r1 = sum(wx1[x][at] * plain[x] for x in range(6))
            rz = sum(wx[x][at] * slope[x] for x in range(6))
            for i, v in enumerate((wy * r0, wy * r1, wy1 * r0, wy * rz)):
                rows12[c * 4 + i, at, :] = jnp.sum(v, axis=0, keepdims=True)


def particle(rows12, frac, b_f, deform, use):
    r_v = [rows12[c * 4] for c in range(3)]
    area = [rows12[c * 4 + 1 + j] - r_v[c] * frac[j] for c in range(3) for j in range(3)]
    stress = [-STRESS_SCALE * v for v in area]
    cof = []
    for i in range(3):
        for j in range(3):
            i1, i2, j1, j2 = (i + 1) % 3, (i + 2) % 3, (j + 1) % 3, (j + 2) % 3
            cof.append(
                deform[3 * i1 + j1] * deform[3 * i2 + j2] - deform[3 * i1 + j2] * deform[3 * i2 + j1]
            )
    det = sum(deform[j] * cof[j] for j in range(3))
    ratio = (stress[0] + stress[4] + stress[8]) / det
    out = r_v + area
    for i in range(3):
        for j in range(3):
            shear = sum((stress[3 * i + m] + stress[3 * m + i]) * deform[3 * m + j] for m in range(3))
            out.append(b_f[3 * i + j] + shear + ratio * cof[3 * i + j])
    return [v * use for v in out]


def gather_first_kernel(
    extents, spot, h, hb, from_low, from_high, now, bf, w_hi, w_lo, d_hi, d_lo, pick,
    second, xu, xd, mid, mass_core, mass_halo,
    total, g_hi, g_lo, s0, sz, rows12, buf, hot,
):
    halo = x_fold(5, h, hb, from_low, from_high, total)
    mass_core[...] = total[144:192]
    wide = iota((8, 256), 1)

    def spread(step):
        start = 144 + step * 48
        out = jnp.ones((8, 256), F32)
        for c in range(3):
            moved = pltpu.roll(halo, (c * 48 - start) % 256, 1)
            out = jnp.where((wide >= c * 48) & (wide < c * 48 + 48), moved, out)
        return out

    mass_halo[...] = spread(0)
    node_values(
        spot, extents, total, halo,
        lambda x: total[192 + x * 8 : 192 + x * 8 + 8], spread(1), g_hi, g_lo,
    )
    frac, (cell_x, cell_y, _), deform = fields(now)
    gather(frac, cell_x, cell_y, g_hi, g_lo, w_hi, w_lo, d_hi, d_lo, s0, sz, rows12)
    use = now[104:112]
    out = particle(rows12, frac, [bf[i] for i in range(9)], deform, use)
    for i in range(21):
        second[i] = out[i]
        buf[i * 8 : i * 8 + 8] = out[i]
    buf[168:176] = jnp.zeros((8, 128), F32)
    hi, lo = split(buf[...])
    low_row = iota((128, 128), 0)
    row = iota((8, 128), 0)
    for t in range(9):
        index = pick[t : t + 1]
        hot[...] = (low_row == (index & 127)).astype(F32).astype(BF16)
        got = nn(hi, hot[...]) + nn(lo, hot[...])
        chosen = (row == (index >> 7)) & (index >= 0)
        got = got.reshape(22, 8, 128)[0:21]
        got = jnp.sum(jnp.where(chosen[None], got, 0.0), axis=1)
        dest, place = ((xd, t), (mid, t - 3), (xu, t - 6))[t // 3]
        dest[:, place * 128 : place * 128 + 128] = got


def pieces(groups, at, tiles):
    lane = iota((21, 128), 1)
    out = [jnp.zeros((21, 128), F32) for _ in range(tiles)]
    for i, group in enumerate(groups):
        place = 32 * (i % 4)
        moved = pltpu.roll(group, (place - at) % 128, 1) if place != at else group
        out[i // 4] = jnp.where((lane >= place) & (lane < place + 32), moved, out[i // 4])
    return out


def lane_tile(ref, i):
    return ref[:, i * 128 : i * 128 + 128]


def route_y_kernel(spot, mid, from_low, from_high, ya, yb):
    first = spot
    for i, ref in enumerate((mid, from_low, from_high)):
        down, up = lane_tile(ref, 0), lane_tile(ref, 2)
        ya[:, i * 128 : i * 128 + 128] = by_side(first, up, down)
        yb[:, i * 128 : i * 128 + 128] = by_side(first, down, up)


def carry(tiles, indices, lh, ll, hot, count=21):
    row, low_row = iota((8, 128), 0), iota((128, 128), 0)
    for t, (values, index) in enumerate(zip(tiles, indices)):
        lanes = slice(t * 128, t * 128 + 128)
        hot[:, lanes] = (low_row == (index & 127)).astype(F32).astype(BF16)
        chosen = row == (index >> 7)
        for pair in range((count + 1) // 2):
            both = []
            for r in (2 * pair, 2 * pair + 1):
                blank = jnp.zeros((8, 128), F32)
                both.append(blank if r >= count else jnp.where(chosen, values(r), 0.0))
            rows = slice(pair * 16, pair * 16 + 16)
            lh[rows, lanes], ll[rows, lanes] = split(jnp.concatenate(both, axis=0))
    return nt(lh[...], hot[...]) + nt(ll[...], hot[...])


def weights_kernel(early, send, w_hi, w_lo, d_hi, d_lo, a_hi, a_lo, b_hi, b_lo, arrive, hot):
    frac, cells, _ = fields(early)
    build_z(frac[2], cells[2], w_hi, w_lo, d_hi, d_lo)

    def put(t, got):
        arrive[:, t, :] = got

    static_rows(early, send, (2, 3, 4, 5, 6, 7, 0, 1), hot, put)
    _, _, cell_z = cells_of((arrive[3] + 0.5).astype(I32))
    build_z(arrive[2], cell_z, a_hi, a_lo, b_hi, b_lo)


def stay_kernel(
    now, second, prior, early, w_hi, w_lo, d_hi, d_lo,
    stayed, core, ends,
    lh, ll, hot, l0h, l0l, l2h, l2l,
):
    tiles = [lambda r, t=t: second[r, t : t + 1, :] for t in range(8)]
    total = carry(tiles, [prior[t : t + 1] for t in range(8)], lh, ll, hot)
    use = now[112:120]
    adj = [total[i * 8 : i * 8 + 8] * use for i in range(21)]
    for i in range(21):
        stayed[i] = adj[i]
    frac, (cell_x, cell_y, _), deform = fields(early)
    a_v, b_c = to_grid(adj, deform)
    l, w = (l0h, l0l, l2h, l2l), (w_hi, w_lo, d_hi, d_lo)
    scatter_rows(a_v, b_c, frac, cell_x, cell_y, *l)
    core[...], ends[...] = all_sums(l, w)


def near_kernel(
    spot, mid, x_low, x_high, ra, rb, both, far, arrive, ends_stay,
    swap, along, against, own_low, own_high, final,
    l0h, l0l, l2h, l2l, moved, static, e0, e1, e2, e3, zu, zd, up2, dn2,
):
    groups = [lane_tile(mid, 1), lane_tile(x_low, 1), lane_tile(x_high, 1)]
    groups += [by_side(spot, lane_tile(rb, i), lane_tile(ra, i)) for i in range(3)]
    groups += [by_side(spot, lane_tile(ra, i), lane_tile(rb, i)) for i in range(3)]
    zu[...] = jnp.zeros(zu.shape, F32)
    zd[...] = jnp.zeros(zd.shape, F32)
    direct, relayed = both[0:16], far[...]
    static_low = by_z_side(spot, relayed, direct)
    static_high = by_z_side(spot, direct, relayed)
    for ref, at, first, known in ((zu, 64, 0, static_high), (zd, 0, 3, static_low)):
        for i, tile in enumerate(pieces(groups, at, 3)):
            ref[0:21, i * 128 : i * 128 + 128] = tile
            moved[:, first + i, :] = tile
            static[:, first + i, :] = lane_tile(known, i)[0:14]
    for i, tile in enumerate(pieces(groups[1:], 32, 2)):
        final[:, i * 128 : i * 128 + 128] = tile
        moved[:, 6 + i, :] = tile
        static[:, 6 + i, :] = arrive[:, 6 + i, :]
    l = (l0h, l0l, l2h, l2l)
    e = (e0, e1, e2, e3)
    place = [static[i] for i in range(3)]
    cell_x, cell_y, cell_z = cells_of((static[3] + 0.5).astype(I32))
    build_z(place[2], cell_z, *e, edges_only=True)
    a_v, b_c = to_grid([moved[i] for i in range(21)], [static[4 + i] for i in range(9)])
    scatter_rows(a_v, b_c, place, cell_x, cell_y, *l)
    upward = edge_sums(l, e, slice(0, 16), slice(0, 384))
    downward = edge_sums(l, e, slice(0, 16), slice(384, 768))
    ends = edge_sums(l, e, slice(0, 16), slice(768, 1024)) + ends_stay[...]
    for ref in (up2, dn2, own_low, own_high):
        ref[...] = jnp.zeros(ref.shape, F32)
    put_planes(up2, 0, upward[0:1], upward[3:4])
    put_planes(own_high, 0, upward[1:2], upward[2:3])
    put_planes(own_low, 0, downward[0:1], downward[3:4])
    put_planes(dn2, 0, downward[1:2], downward[2:3])
    put_planes(zu, 21, ends[0:1], ends[3:4])
    put_planes(zd, 21, ends[1:2], ends[2:3])
    swap[0:24] = by_z_side(spot, zu, zd)
    swap[24:48] = by_z_side(spot, zd, zu)
    along[...] = by_z_side(spot, up2, dn2)
    against[...] = by_z_side(spot, dn2, up2)


def second_kernel(
    spot, both, far, against, own_low, own_high, final, arrive, a_hi, a_lo, b_hi, b_lo,
    core_stay, ends_stay,
    h_out, hb_out, ya, yb, moved,
    l0h, l0l, l2h, l2l, h,
):
    for i in range(3):
        near, relayed = lane_tile(both, i)[0:24], lane_tile(far, i)
        moved[:, i, :] = by_side(spot, relayed, near, 4)[0:21]
        moved[:, 3 + i, :] = by_side(spot, near, relayed, 4)[0:21]
    for i in range(2):
        moved[:, 6 + i, :] = lane_tile(final, i)
    place = [arrive[i] for i in range(3)]
    cell_x, cell_y, _ = cells_of((arrive[3] + 0.5).astype(I32))
    a_v, b_c = to_grid([moved[i] for i in range(21)], [arrive[4 + i] for i in range(9)])
    l, w = (l0h, l0l, l2h, l2l), (a_hi, a_lo, b_hi, b_lo)
    scatter_rows(a_v, b_c, place, cell_x, cell_y, *l)
    core, ends = all_sums(l, w)
    h[...] = core + core_stay[...]
    ends = ends + ends_stay[...]
    ends = jnp.concatenate([ends[0:8], jnp.zeros((8, 112), F32)], axis=1)
    halo = jnp.where(iota((8, 256), 0) < 2, ends, 0.0)
    near, relayed = both[21:23, 0:256] + against[0:2], far[21:23, 0:256]
    low = by_z_side(spot, relayed, near) + own_low[0:2]
    high = by_z_side(spot, near, relayed) + own_high[0:2]
    z_fold(3, spot, h, halo, low, high, h_out, hb_out, ya, yb)


def relay_kernel(both, along, _, out):
    out[...] = both[24:48]
    out[21:23, 0:256] = both[45:47, 0:256] + along[0:2]


def deform_kernel(now, stayed, moved, send, affine, bf_out, lh, ll, hot):
    tiles = [lambda r, t=t: moved[12 + r, t : t + 1, :] for t in range(8)]
    rows = [send[t : t + 1] for t in (2, 3, 4, 5, 6, 7, 0, 1)]
    total = carry(tiles, rows, lh, ll, hot, 9)
    use = now[112:120]
    a_f = [(stayed[12 + i] + total[i * 8 : i * 8 + 8]) * use for i in range(9)]
    k = dense(affine, 0, 9)
    for i in range(3):
        for j in range(3):
            bf_out[3 * i + j] = a_f[3 * i + j] + TIME_STEP * sum(
                k[3 * m + i] * a_f[3 * m + j] for m in range(3)
            )


def gather_second_kernel(
    extents, spot, h, hb, from_low, from_high, now, early, bf, w_hi, w_lo, d_hi, d_lo,
    mass_core, mass_halo,
    result,
    total, g_hi, g_lo, s0, sz, rows12, packed,
):
    halo = x_fold(3, h, hb, from_low, from_high, total)
    node_values(
        spot, extents, total, halo,
        lambda x: mass_core[x * 8 : x * 8 + 8], mass_halo[...], g_hi, g_lo,
    )
    frac, (cell_x, cell_y, _), deform = fields(early)
    gather(frac, cell_x, cell_y, g_hi, g_lo, w_hi, w_lo, d_hi, d_lo, s0, sz, rows12)
    use = now[112:120]
    out = particle(rows12, frac, [bf[i] for i in range(9)], deform, use)
    for i in range(21):
        packed[i] = out[i]
    for k in range(CHUNKS):
        result[:, k * 128 : k * 128 + 128] = packed[:, k, :]


def shape(*dims, dtype=F32):
    return jax.ShapeDtypeStruct(dims, dtype)


def call(kernel, name, specs, outs, scratch=()):
    return pl.pallas_call(
        kernel,
        name=name,
        in_specs=list(specs),
        out_specs=[VMEM] * len(outs),
        out_shape=list(outs),
        scratch_shapes=[pltpu.VMEM(*v) if isinstance(v, tuple) else v for v in scratch],
        compiler_params=pltpu.CompilerParams(vmem_limit_bytes=40 * 1024 * 1024),
    )


def both_ways(up, down, axis, step=1):
    count = lax.axis_size(axis)
    low = lax.ppermute(up, axis, [(i, i + step) for i in range(count - step)])
    high = lax.ppermute(down, axis, [(i + step, i) for i in range(count - step)])
    return low, high


def both_pairs(first, second, axis):
    count = lax.axis_size(axis)
    a = [(i, i ^ 1) for i in range(count) if i ^ 1 < count]
    b = [p for i in range(1, count - 1, 2) for p in ((i, i + 1), (i + 1, i))]
    ra = lax.ppermute(first, axis, a)
    rb = lax.ppermute(second, axis, b) if b else jnp.zeros_like(second)
    return ra, rb


def body(
    fractions, centers, deform, next_affine, cell_mass, final_adjoint,
    live_count, send_slot, receive_slot, receive_count, prior_slot,
):
    at_y = lax.axis_index("gy")
    at_z = lax.axis_index("gz")
    spot = [lax.axis_index("gx") * 4, at_y * 4, at_z * 128, at_y % 2, at_z % 2]
    spot = jnp.stack(spot + [jnp.zeros_like(at_y)] * 3).astype(I32)
    spot = jnp.broadcast_to(spot[:, None], (8, 128))
    extents = (lax.axis_size("gx") * 4, lax.axis_size("gy") * 4, lax.axis_size("gz") * 128)

    fractions, deform, next_affine = (
        jnp.transpose(v, (1, 0, 2)) for v in (fractions, deform, next_affine)
    )
    slots_back = jnp.transpose(send_slot, (1, 0, 2))
    slots_out = jnp.transpose(receive_slot, (1, 0, 2))
    prior = prior_slot.reshape(8, 128)

    wide = shape(ZROWS, 1024, dtype=BF16)
    weights = [wide] * 4
    lrows = [((144, 1024), BF16)] * 4
    gscratch = [
        ((144, 256), BF16), ((144, 256), BF16),
        ((144, 1024), F32), ((144, 1024), F32), ((12, 8, 128), F32),
    ]

    def fold(comps, h, hb, ya, yb, after=()):
        ra, rb = both_pairs(ya, yb, "gy")
        rows = comps * 16 + 8

        def kernel(*refs):
            y_kernel(comps, *refs[:5], *refs[5 + len(after) :])

        h, hb, xu, xd = call(
            kernel, f"fold_y{comps}", [VMEM] * 5 + [pl.BlockSpec(memory_space=pl.ANY)] * len(after),
            [shape(comps * 48, 128), shape(8, 256), shape(rows, 128), shape(rows, 128)],
        )(spot, h, hb, ra, rb, *after)
        low, high = both_ways(xu, xd, "gx")
        return h, hb, low, high

    firsts = (
        live_count, final_adjoint, fractions, centers, deform, next_affine, cell_mass, slots_back
    )
    h, hb, both, bf, *w, send, now, early = call(
        first_kernel, "scatter_first", [VMEM] + [HBM] * 8,
        [shape(240, 128), shape(8, 256), shape(32, 384), shape(9, 8, 128)]
        + weights + [shape(8, 128, dtype=I32), shape(120, 128), shape(112, 128)],
        lrows + [((128, 128), BF16), ((16, 384), F32), ((16, 384), F32)]
        + [(v.shape, v.dtype) for v in firsts] + [pltpu.SemaphoreType.DMA((8,))],
    )(spot, *(pltpu.with_memory_space_constraint(v, pltpu.HBM) for v in firsts))
    count = lax.axis_size("gz")
    pairs = [(i, i ^ 1) for i in range(count) if i ^ 1 < count]
    hop = [(i, i + 2) for i in range(0, count - 2, 2)] + [(i, i - 2) for i in range(3, count, 2)]
    both = lax.ppermute(both, "gz", pairs)
    far = lax.ppermute(both[16:32], "gz", hop)
    (pick,) = call(pick_kernel, "fill_pick", [VMEM, VMEM], [shape(9, 128, dtype=I32)])(
        receive_count, slots_out
    )
    weights2 = call(
        weights_kernel, "weights_second", [VMEM] * 2, weights + weights + [shape(14, 8, 128)],
        [((128, 128), BF16)],
    )(early, send)
    w2, wa, arrive = weights2[0:4], weights2[4:8], weights2[8]
    h, hb, ya, yb = call(
        functools.partial(z_kernel, 5), "fold_z5", [VMEM] * 5,
        [shape(240, 128), shape(8, 256), shape(72, 128), shape(72, 128)],
    )(spot, h, hb, both, far)
    h, hb, low, high = fold(5, h, hb, ya, yb, (arrive,))
    second, xu, xd, mid, mass_core, mass_halo = call(
        functools.partial(gather_first_kernel, extents), "gather_first", [VMEM] * 12,
        [shape(21, 8, 128), shape(21, 384), shape(21, 384), shape(21, 384), shape(48, 128), shape(8, 256)],
        [((240, 128), F32)] + gscratch + [((176, 128), F32), ((128, 128), BF16)],
    )(spot, h, hb, low, high, now, bf, *w, pick)

    x_low, x_high = both_ways(xu, xd, "gx")
    stayed, core_stay, ends_stay = call(
        stay_kernel, "stay", [VMEM] * 8,
        [shape(21, 8, 128), shape(144, 128), shape(16, 144)],
        [((176, 1024), BF16)] * 2 + [((128, 1024), BF16)] + lrows,
    )(now, second, prior, early, *w2)

    def route(*refs):
        route_y_kernel(*refs[:4], *refs[5:])

    ya, yb = call(
        route, "route_y", [VMEM] * 4 + [pl.BlockSpec(memory_space=pl.ANY)], [shape(21, 384)] * 2
    )(spot, mid, x_low, x_high, ends_stay)
    ra, rb = both_pairs(ya, yb, "gy")
    swap, along, against, own_low, own_high, final = call(
        near_kernel, "scatter_near", [VMEM] * 10,
        [shape(48, 384)] + [shape(2, 256)] * 4 + [shape(21, 256)],
        lrows + [((21, 8, 128), F32), ((14, 8, 128), F32)] + [((16, 1024), BF16)] * 4
        + [((24, 384), F32)] * 2 + [((2, 256), F32)] * 2,
    )(spot, mid, x_low, x_high, ra, rb, both, far, arrive, ends_stay)
    both = lax.ppermute(swap, "gz", pairs)
    against = lax.ppermute(against, "gz", [(b, a) for a, b in hop])
    (far,) = call(
        relay_kernel, "relay", [VMEM] * 2 + [pl.BlockSpec(memory_space=pl.ANY)], [shape(24, 384)]
    )(both, along, against)
    far = lax.ppermute(far, "gz", hop)
    h, hb, ya, yb, moved = call(
        second_kernel, "scatter_second", [VMEM] * 14,
        [shape(144, 128), shape(8, 256), shape(48, 128), shape(48, 128), shape(21, 8, 128)],
        lrows + [((144, 128), F32)],
    )(
        spot, both, far, against, own_low, own_high, final, arrive, *wa, core_stay, ends_stay
    )
    (bf,) = call(
        deform_kernel, "deform_second", [VMEM] * 5, [shape(9, 8, 128)],
        [((80, 1024), BF16)] * 2 + [((128, 1024), BF16)],
    )(now, stayed, moved, send, next_affine)
    h, hb, low, high = fold(3, h, hb, ya, yb)
    (result,) = call(
        functools.partial(gather_second_kernel, extents), "gather_second", [VMEM] * 14,
        [shape(21, 1024)],
        [((144, 128), F32)] + gscratch + [((21, 8, 128), F32)],
    )(spot, h, hb, low, high, now, early, bf, *w2, mass_core, mass_halo)
    return result


def solution(mesh):
    spread = AXES
    in_specs = (
        P(None, None, spread), P(None, spread), P(None, None, spread), P(None, None, spread),
        P(None, "gx", "gy", "gz"), P(None, spread), P(spread, None), P(spread, None, None),
        P(spread, None, None), P(spread, None), P(spread),
    )
    return jax.shard_map(
        body, mesh=mesh, in_specs=in_specs, out_specs=P(None, spread), check_vma=False
    )
```

```python
import functools

import jax
import jax.numpy as jnp
from jax import lax
from jax.experimental import pallas as pl
from jax.experimental.pallas import tpu as pltpu
from jax.sharding import PartitionSpec as P

TIME_STEP = 0.2
APIC_SCALE = 4.0
STRESS_SCALE = 0.3
F32 = jnp.float32
BF16 = jnp.bfloat16
I32 = jnp.int32
AXES = ("gx", "gy", "gz")
VMEM = pl.BlockSpec(memory_space=pltpu.VMEM)
HBM = pl.BlockSpec(memory_space=pltpu.HBM)
CHUNKS = 8
ZROWS = 144


def contract(a, b, da, db, precision=None):
    return lax.dot_general(
        a, b, (((da,), (db,)), ((), ())), preferred_element_type=F32, precision=precision
    )


def nt(a, b):
    return contract(a, b, 1, 1)


def nn(a, b):
    return contract(a, b, 1, 0)


def split(x):
    hi = x.astype(BF16)
    return hi, (x - hi.astype(F32)).astype(BF16)


def rounded(x):
    hi = x.astype(BF16).astype(F32)
    return hi, x - hi


def spline(f):
    return 0.5 * (0.5 - f) * (0.5 - f), 0.75 - f * f, 0.5 * (0.5 + f) * (0.5 + f)


def iota(shape, axis):
    return lax.broadcasted_iota(I32, shape, axis)


def dense(ref, step, rows):
    value = ref[:, step, :] if step is not None else ref[...]
    value = value.reshape(rows, CHUNKS, 128)
    return [value[i] for i in range(rows)]


def axis_tables(fx, cell_x, count):
    low, mid, high = spline(fx)
    plain, signed = [], []
    for plane in range(count):
        is_low, is_mid, is_high = cell_x == plane, cell_x + 1 == plane, cell_x + 2 == plane
        plain.append(jnp.where(is_low, low, jnp.where(is_mid, mid, jnp.where(is_high, high, 0.0))))
        signed.append(jnp.where(is_low, -low, jnp.where(is_high, high, 0.0)))
    return plain, signed


def y_tables(fy, cell_y, chunk):
    low, mid, high = (v[chunk : chunk + 1] for v in spline(fy))
    away = iota((8, 128), 0) - (cell_y[chunk : chunk + 1] + 1)
    plain = jnp.where(away == -1, low, jnp.where(away == 0, mid, jnp.where(away == 1, high, 0.0)))
    signed = jnp.where(away == -1, -low, jnp.where(away == 1, high, 0.0))
    return plain, signed


def build_z(fz, cell_z, w_hi, w_lo, d_hi, d_lo, chunks=CHUNKS, edges_only=False):
    low, mid, high = spline(fz)
    low_h, low_l = rounded(low)
    mid_h, mid_l = rounded(mid)
    high_h, high_l = rounded(high)
    to_low = jnp.where(cell_z == 0, 129, cell_z - 1)
    to_high = cell_z + 1
    inner = iota((128, 128), 0)
    edge = iota((16, 128), 0)
    edge = jnp.where(edge < 2, edge + 128, jnp.where(edge == 2, 0, jnp.where(edge == 3, 127, 999)))
    parts = ((slice(0, 128), inner), (slice(128, ZROWS), edge))
    if edges_only:
        parts = ((slice(0, 16), edge),)
    for chunk in range(chunks):
        at = slice(chunk, chunk + 1)
        lanes = slice(chunk * 128, chunk * 128 + 128)
        for rows, index in parts:
            is_low, is_mid, is_high = index == to_low[at], index == cell_z[at], index == to_high[at]
            for plain, signed, (a, b, c) in (
                (w_hi, d_hi, (low_h, mid_h, high_h)),
                (w_lo, d_lo, (low_l, mid_l, high_l)),
            ):
                ends = jnp.where(is_high, c[at], 0.0)
                plain[rows, lanes] = jnp.where(
                    is_low, a[at], jnp.where(is_mid, b[at], ends)
                ).astype(BF16)
                signed[rows, lanes] = jnp.where(is_low, -a[at], ends).astype(BF16)


def row_of(info, i, rows=8):
    return jnp.broadcast_to(info[i : i + 1, :], (rows, 128))


def by_side(info, one, other, axis_row=3):
    return jnp.where(row_of(info, axis_row, one.shape[0]) == 0, one, other)


def by_sides(info, one, other, axis_row=3):
    count = one.shape[1] // 128
    tiles = [by_side(info, lane_tile(one, t), lane_tile(other, t), axis_row) for t in range(count)]
    return jnp.concatenate(tiles, axis=1)


def by_z_side(info, one, other):
    return by_sides(info, one, other, 4)


def fields(ref):
    tiles = [ref[i * 8 : i * 8 + 8] for i in range(13)]
    return tiles[0:3], cells_of((tiles[3] + 0.5).astype(I32)), tiles[4:13]


def in_use(live, step):
    slots = iota((8, 128), 0) * 128 + iota((8, 128), 1)
    return (slots < jnp.broadcast_to(live[0:1, step : step + 1], (8, 128))).astype(F32)


STEPS = (0, 1, -1)


def offset_row(offset):
    place = (offset[0] + 1) * 9 + (offset[1] + 1) * 3 + offset[2] + 1
    return place - (place > 13)


def fill_send(slots, send):
    inward = [(x, y, 0) for y in STEPS for x in STEPS][1:]
    order = inward + [(x, y, 1) for y in STEPS for x in STEPS] + [None] * 3
    order += [(x, y, -1) for y in STEPS for x in STEPS]
    send[...] = jnp.zeros(send.shape, I32)
    for n, offset in enumerate(order):
        if offset is not None:
            lane = n % 4 * 32
            send[n // 4 : n // 4 + 1, lane : lane + 32] = slots[25 - offset_row(offset)]


def pick_kernel(counts, slots, pick):
    pick[...] = jnp.full(pick.shape, -1, I32)
    order = iota((1, 32), 1)
    for x in (-1, 0, 1):
        for y in (-1, 0, 1):
            for z in (-1, 0, 1):
                if (x, y, z) != (0, 0, 0):
                    n, row, lane = offset_row((x, y, z)), (x + 1) * 3 + y + 1, (z + 1) * 32
                    pick[row : row + 1, lane : lane + 32] = jnp.where(
                        order < jnp.broadcast_to(counts[0:1, n : n + 1], (1, 32)), slots[n], -1
                    )


def cells_of(centre):
    return centre >> 9, (centre >> 7) & 3, centre & 127


def to_grid(adj, deform):
    a_v, a_c, a_f = adj[0:3], adj[3:12], adj[12:21]
    b_c = [
        a_c[3 * i + j] + TIME_STEP * sum(a_f[3 * i + m] * deform[3 * j + m] for m in range(3))
        for i in range(3)
        for j in range(3)
    ]
    return a_v, b_c


def transfer(adj, deform, affine):
    a_v, b_c = to_grid(adj, deform)
    a_f = adj[12:21]
    b_f = [
        a_f[3 * i + j] + TIME_STEP * sum(affine[3 * m + i] * a_f[3 * m + j] for m in range(3))
        for i in range(3)
        for j in range(3)
    ]
    return a_v, b_c, b_f


def scatter_rows(a_v, b_c, frac, cell_x, cell_y, l0h, l0l, l2h, l2l, chunks=CHUNKS):
    base, slope = [], []
    for c in range(3):
        base.append(a_v[c] - APIC_SCALE * sum(b_c[3 * c + j] * frac[j] for j in range(3)))
        slope.append([APIC_SCALE * b_c[3 * c + j] for j in range(3)])
    wx, wx1 = axis_tables(frac[0], cell_x, 6)
    for k in range(chunks):
        at = slice(k, k + 1)
        lanes = slice(k * 128, k * 128 + 128)
        wy, wy1 = y_tables(frac[1], cell_y, k)
        for c in range(3):
            a = wy * base[c][at] + wy1 * slope[c][1][at]
            b = wy * slope[c][0][at]
            d = wy * slope[c][2][at]
            for pair in range(3):
                rows = slice(c * 48 + pair * 16, c * 48 + pair * 16 + 16)
                planes = (2 * pair, 2 * pair + 1)
                l0 = jnp.concatenate([wx[x][at] * a + wx1[x][at] * b for x in planes], axis=0)
                l2 = jnp.concatenate([wx[x][at] * d for x in planes], axis=0)
                l0h[rows, lanes], l0l[rows, lanes] = split(l0)
                l2h[rows, lanes], l2l[rows, lanes] = split(l2)


def paired(l, w):
    l0h, l0l, l2h, l2l = l
    w_hi, w_lo, d_hi, d_lo = w
    return ((l0h, w_hi), (l0l, w_hi), (l0h, w_lo), (l2h, d_hi), (l2l, d_hi), (l2h, d_lo))


def all_sums(l, w):
    full = sum(nt(a[...], b[...]) for a, b in paired(l, w))
    tail = jnp.concatenate([full[:, 128:ZROWS], jnp.zeros((144, 112), F32)], axis=1)
    tail = jnp.concatenate([tail, jnp.zeros((112, 128), F32)], axis=0).T
    return full[:, 0:128], tail[0:16, 0:144]


def edge_sums(l, w, rows=slice(128, ZROWS), lanes=slice(0, 1024)):
    return sum(nt(b[rows, lanes], a[:, lanes]) for a, b in paired(l, w))


def put_planes(ref, at, first, second):
    width = first.shape[1]
    ref[at : at + 1, :width] = first
    ref[at + 1 : at + 2, :width] = second


def static_rows(table, send, rows, hot, put):
    hi, lo = split(table[...])
    low_row, row = iota((128, 128), 0), iota((8, 128), 0)
    for t, n in enumerate(rows):
        index = send[n : n + 1]
        hot[...] = (low_row == (index & 127)).astype(F32).astype(BF16)
        got = (nn(hi, hot[...]) + nn(lo, hot[...])).reshape(14, 8, 128)
        chosen = row == (index >> 7)
        put(t, jnp.sum(jnp.where(chosen[None], got, 0.0), axis=1))


def first_kernel(
    spot, live_at, adjoint_at, fractions_at, centers_at, deform_at, affine_at, mass_at, slots_at,
    h, hb, both, bf_out, w_hi, w_lo, d_hi, d_lo, send, now, early,
    l0h, l0l, l2h, l2l, hot, zu, zd,
    live, adjoint, fractions, centers, deform, affine, mass, slots_back, arrived,
):
    sources = (slots_at, fractions_at, centers_at, deform_at, live_at, adjoint_at, affine_at, mass_at)
    places = (slots_back, fractions, centers, deform, live, adjoint, affine, mass)
    copies = [
        pltpu.make_async_copy(a, b, arrived.at[i]) for i, (a, b) in enumerate(zip(sources, places))
    ]
    for copy in copies:
        copy.start()
    w = (w_hi, w_lo, d_hi, d_lo)
    l = (l0h, l0l, l2h, l2l)
    zu[...] = jnp.zeros(zu.shape, F32)
    zd[...] = jnp.zeros(zd.shape, F32)
    for copy in copies[:3]:
        copy.wait()
    fill_send(slots_back, send)
    frac = dense(fractions, 1, 3)
    centre = centers[1:2, :].reshape(CHUNKS, 128)
    cell_x, cell_y, cell_z = cells_of(centre)
    build_z(frac[2], cell_z, *w)
    for copy in copies[3:]:
        copy.wait()
    deform_now = dense(deform, 1, 9)
    for i, tile in enumerate(frac + [centre.astype(F32)] + deform_now):
        now[i * 8 : i * 8 + 8] = tile
    early[104:112] = jnp.zeros((8, 128), F32)
    use = in_use(live, 1)
    now[104:112] = use
    now[112:120] = in_use(live, 0)
    known = dense(fractions, 0, 3) + [centers[0:1, :].reshape(CHUNKS, 128).astype(F32)]
    for i, tile in enumerate(known + dense(deform, 0, 9)):
        early[i * 8 : i * 8 + 8] = tile

    def put(t, got):
        dest = (zd, zu)[t // 3]
        dest[0:14, t % 3 * 128 : t % 3 * 128 + 128] = got

    static_rows(early, send, range(2, 8), hot, put)
    adj = [v * use for v in dense(adjoint, None, 21)]
    a_v, b_c, b_f = transfer(adj, deform_now, dense(affine, 1, 9))
    for i in range(9):
        bf_out[i] = b_f[i]
    scatter_rows(a_v, b_c, frac, cell_x, cell_y, *l)
    core, ends = all_sums(l, w)
    h[0:144] = core
    h[144:240] = jnp.zeros((96, 128), F32)
    for s in range(2):
        for x in range(4):
            row = 144 + s * 48 + (x + 1) * 8 + 1
            h[row : row + 4] = mass[s, x]
    lane, row = iota((16, 128), 1), iota((16, 128), 0)
    pick = (((row == 2) & (lane == 0)) | ((row == 3) & (lane == 127))).astype(F32)
    mass_ends = contract(pick, h[144:240], 1, 1, lax.Precision.HIGHEST)
    ends = jnp.concatenate([ends, mass_ends], axis=1)
    hb[...] = jnp.zeros(hb.shape, F32)
    put_planes(hb, 0, ends[0:1], ends[1:2])
    put_planes(zu, 13, ends[0:1], ends[3:4])
    put_planes(zd, 13, ends[1:2], ends[2:3])
    both[0:16] = by_z_side(spot, zu, zd)
    both[16:32] = by_z_side(spot, zd, zu)


def wide_rows(hb):
    return jnp.concatenate(
        [hb[0:1, :128], hb[0:1, 128:], hb[1:2, :128], hb[1:2, 128:], jnp.zeros((4, 128), F32)], axis=0
    )


def from_wide(rows):
    top = jnp.concatenate([rows[0:1], rows[1:2]], axis=1)
    low = jnp.concatenate([rows[2:3], rows[3:4]], axis=1)
    return jnp.concatenate([top, low, jnp.zeros((6, 256), F32)], axis=0)


def transposed(rows):
    return jnp.concatenate([rows, jnp.zeros((120, 256), F32)], axis=0).T


def z_kernel(comps, spot, h, hb, both, far, h_out, hb_out, ya, yb):
    direct, relayed = both[13:15, 0:256], far[13:15, 0:256]
    low, high = by_z_side(spot, relayed, direct), by_z_side(spot, direct, relayed)
    z_fold(comps, spot, h, hb[...], low, high, h_out, hb_out, ya, yb)


def z_fold(comps, first, h, halo, low, high, h_out, hb_out, ya, yb):
    pad = jnp.zeros((6, 256), F32)
    halo = halo + jnp.concatenate([high[1:2], low[1:2], pad], axis=0)
    hb_out[...] = halo
    wall = transposed(jnp.concatenate([low[0:1], high[0:1], pad], axis=0))
    lane = iota((8, 128), 1)
    row = iota((8, 128), 0)
    blocks = comps * 6
    up, down = None, None
    for q in range(blocks):
        rows = slice(q * 8, q * 8 + 8)
        tile = (
            h[rows]
            + jnp.where(lane == 0, wall[rows, 0:1], 0.0)
            + jnp.where(lane == 127, wall[rows, 1:2], 0.0)
        )
        h_out[rows] = tile
        place = 2 * (q % 4)
        chosen = (row >= place) & (row < place + 2)
        a = pltpu.roll(tile, (place - 4) % 8, 0) if place != 4 else tile
        b = pltpu.roll(tile, place, 0) if place else tile
        up = jnp.where(chosen, a, 0.0 if up is None else up)
        down = jnp.where(chosen, b, 0.0 if down is None else down)
        if q % 4 == 3 or q == blocks - 1:
            out = slice(q // 4 * 8, q // 4 * 8 + 8)
            ya[out] = by_side(first, up, down)
            yb[out] = by_side(first, down, up)
            up, down = None, None
    packed = (blocks + 3) // 4 * 8
    ya[packed : packed + 8] = wide_rows(halo)
    yb[packed : packed + 8] = wide_rows(halo)


def y_kernel(comps, spot, h, hb, ra, rb, h_out, hb_out, xa, xb, xu, xd):
    first = spot
    row = iota((8, 128), 0)
    blocks = comps * 6
    packed = (blocks + 3) // 4 * 8
    for q in range(blocks):
        rows = slice(q * 8, q * 8 + 8)
        place = 2 * (q % 4)
        src = slice(q // 4 * 8, q // 4 * 8 + 8)
        a, b = by_side(first, rb[src], ra[src]), by_side(first, ra[src], rb[src])
        a = pltpu.roll(a, (-place) % 8, 0) if place else a
        b = pltpu.roll(b, (4 - place) % 8, 0) if place != 4 else b
        tile = (
            h[rows] + jnp.where(row < 2, a, 0.0) + jnp.where((row >= 4) & (row < 6), b, 0.0)
        )
        h_out[rows] = tile
        c, x = q // 6, q % 6
        if x >= 4:
            xu[c * 16 + (x - 4) * 8 : c * 16 + (x - 4) * 8 + 8] = tile
        if x < 2:
            xd[c * 16 + x * 8 : c * 16 + x * 8 + 8] = tile
    place = iota((8, 256), 1) % 8
    a, b = ra[packed : packed + 8], rb[packed : packed + 8]
    a, b = by_side(first, b, a), by_side(first, a, b)
    a = pltpu.roll(from_wide(a), 252, 1)
    b = pltpu.roll(from_wide(b), 4, 1)
    halo = hb[...] + jnp.where(place < 2, a, 0.0) + jnp.where((place >= 4) & (place < 6), b, 0.0)
    hb_out[...] = halo
    xu[comps * 16 : comps * 16 + 8] = wide_rows(halo)
    xd[comps * 16 : comps * 16 + 8] = wide_rows(halo)
    xa[...] = by_side(spot, xu[...], xd[...])
    xb[...] = by_side(spot, xd[...], xu[...])


def x_fold(comps, spot, h, hb, ra, rb, total):
    from_low, from_high = by_side(spot, ra[...], rb[...]), by_side(spot, rb[...], ra[...])
    for c in range(comps):
        total[c * 48 : c * 48 + 16] = h[c * 48 : c * 48 + 16] + from_low[c * 16 : c * 16 + 16]
        total[c * 48 + 16 : c * 48 + 32] = h[c * 48 + 16 : c * 48 + 32]
        total[c * 48 + 32 : c * 48 + 48] = (
            h[c * 48 + 32 : c * 48 + 48] + from_high[c * 16 : c * 16 + 16]
        )
    plane = iota((8, 256), 1) % 48 // 8
    a = pltpu.roll(from_wide(from_low[comps * 16 : comps * 16 + 8]), 224, 1)
    b = pltpu.roll(from_wide(from_high[comps * 16 : comps * 16 + 8]), 32, 1)
    return hb[...] + jnp.where(plane < 2, a, 0.0) + jnp.where(plane >= 4, b, 0.0)


def node_values(spot, extents, total, halo, mass_at, mass_halo, g_hi, g_lo):
    first_x, first_y, first_z = (row_of(spot, i) for i in range(3))
    far_x, far_y, far_z = (jnp.concatenate([v, v], axis=1) for v in (first_x, first_y, first_z))
    lane, row = iota((8, 128), 1), iota((8, 128), 0)
    node_z = first_z + lane
    node_y = first_y + row - 1
    keep_yz = (
        (node_z >= 1) & (node_z <= extents[2] - 2) & (node_y >= 1) & (node_y <= extents[1] - 2)
    )
    wide = iota((8, 256), 1)
    side = iota((8, 256), 0)
    halo_x = far_x + wide % 48 // 8 - 1
    halo_y = far_y + wide % 8 - 1
    halo_z = far_z + jnp.where(side == 0, 128, -1)
    keep = (
        (halo_x >= 1) & (halo_x <= extents[0] - 2)
        & (halo_y >= 1) & (halo_y <= extents[1] - 2)
        & (halo_z >= 1) & (halo_z <= extents[2] - 2)
        & (side < 2) & (wide < 144) & (wide % 8 < 6)
    )
    ends = jnp.where(keep, halo / jnp.where(keep, mass_halo, 1.0), 0.0)
    columns = transposed(ends)
    g_hi[:, 128:256], g_lo[:, 128:256] = split(columns[0:144])
    for x in range(6):
        node_x = first_x + x - 1
        keep_here = keep_yz & (row < 6) & (node_x >= 1) & (node_x <= extents[0] - 2)
        mass = jnp.where(keep_here, mass_at(x), 1.0)
        for c in range(3):
            rows = slice(c * 48 + x * 8, c * 48 + x * 8 + 8)
            total[rows] = jnp.where(keep_here, total[rows] / mass, 0.0)
    g_hi[:, 0:128], g_lo[:, 0:128] = split(total[0:144])


def gather(frac, cell_x, cell_y, g_hi, g_lo, w_hi, w_lo, d_hi, d_lo, s0, sz, rows12):
    a, b = g_hi[:, 0:ZROWS], g_lo[:, 0:ZROWS]
    s0[...] = nn(a, w_hi[...]) + nn(b, w_hi[...]) + nn(a, w_lo[...])
    sz[...] = nn(a, d_hi[...]) + nn(b, d_hi[...]) + nn(a, d_lo[...])
    wx, wx1 = axis_tables(frac[0], cell_x, 6)
    for k in range(CHUNKS):
        at = slice(k, k + 1)
        lanes = slice(k * 128, k * 128 + 128)
        wy, wy1 = y_tables(frac[1], cell_y, k)
        for c in range(3):
            plain = [s0[c * 48 + x * 8 : c * 48 + x * 8 + 8, lanes] for x in range(6)]
            slope = [sz[c * 48 + x * 8 : c * 48 + x * 8 + 8, lanes] for x in range(6)]
            r0 = sum(wx[x][at] * plain[x] for x in range(6))
            r1 = sum(wx1[x][at] * plain[x] for x in range(6))
            rz = sum(wx[x][at] * slope[x] for x in range(6))
            for i, v in enumerate((wy * r0, wy * r1, wy1 * r0, wy * rz)):
                rows12[c * 4 + i, at, :] = jnp.sum(v, axis=0, keepdims=True)


def particle(rows12, frac, b_f, deform, use):
    r_v = [rows12[c * 4] for c in range(3)]
    area = [rows12[c * 4 + 1 + j] - r_v[c] * frac[j] for c in range(3) for j in range(3)]
    stress = [-STRESS_SCALE * v for v in area]
    cof = []
    for i in range(3):
        for j in range(3):
            i1, i2, j1, j2 = (i + 1) % 3, (i + 2) % 3, (j + 1) % 3, (j + 2) % 3
            cof.append(
                deform[3 * i1 + j1] * deform[3 * i2 + j2] - deform[3 * i1 + j2] * deform[3 * i2 + j1]
            )
    det = sum(deform[j] * cof[j] for j in range(3))
    ratio = (stress[0] + stress[4] + stress[8]) / det
    out = r_v + area
    for i in range(3):
        for j in range(3):
            shear = sum((stress[3 * i + m] + stress[3 * m + i]) * deform[3 * m + j] for m in range(3))
            out.append(b_f[3 * i + j] + shear + ratio * cof[3 * i + j])
    return [v * use for v in out]


def gather_first_kernel(
    extents, spot, h, hb, from_low, from_high, now, bf, w_hi, w_lo, d_hi, d_lo, pick,
    second, xa, xb, mid, mass_core, mass_halo,
    xu, xd, total, g_hi, g_lo, s0, sz, rows12, buf, hot,
):
    halo = x_fold(5, spot, h, hb, from_low, from_high, total)
    mass_core[...] = total[144:192]
    wide = iota((8, 256), 1)

    def spread(step):
        start = 144 + step * 48
        out = jnp.ones((8, 256), F32)
        for c in range(3):
            moved = pltpu.roll(halo, (c * 48 - start) % 256, 1)
            out = jnp.where((wide >= c * 48) & (wide < c * 48 + 48), moved, out)
        return out

    mass_halo[...] = spread(0)
    node_values(
        spot, extents, total, halo,
        lambda x: total[192 + x * 8 : 192 + x * 8 + 8], spread(1), g_hi, g_lo,
    )
    frac, (cell_x, cell_y, _), deform = fields(now)
    gather(frac, cell_x, cell_y, g_hi, g_lo, w_hi, w_lo, d_hi, d_lo, s0, sz, rows12)
    use = now[104:112]
    out = particle(rows12, frac, [bf[i] for i in range(9)], deform, use)
    for i in range(21):
        second[i] = out[i]
        buf[i * 8 : i * 8 + 8] = out[i]
    buf[168:176] = jnp.zeros((8, 128), F32)
    hi, lo = split(buf[...])
    low_row = iota((128, 128), 0)
    row = iota((8, 128), 0)
    for t in range(9):
        index = pick[t : t + 1]
        hot[...] = (low_row == (index & 127)).astype(F32).astype(BF16)
        got = nn(hi, hot[...]) + nn(lo, hot[...])
        chosen = (row == (index >> 7)) & (index >= 0)
        got = got.reshape(22, 8, 128)[0:21]
        got = jnp.sum(jnp.where(chosen[None], got, 0.0), axis=1)
        dest, place = ((xd, t), (mid, t - 3), (xu, t - 6))[t // 3]
        dest[:, place * 128 : place * 128 + 128] = got
    xa[...] = by_sides(spot, xu, xd)
    xb[...] = by_sides(spot, xd, xu)


def pieces(groups, at, tiles):
    lane = iota((21, 128), 1)
    out = [jnp.zeros((21, 128), F32) for _ in range(tiles)]
    for i, group in enumerate(groups):
        place = 32 * (i % 4)
        moved = pltpu.roll(group, (place - at) % 128, 1) if place != at else group
        out[i // 4] = jnp.where((lane >= place) & (lane < place + 32), moved, out[i // 4])
    return out


def lane_tile(ref, i):
    return ref[:, i * 128 : i * 128 + 128]


def route_y_kernel(spot, mid, xa, xb, ya, yb):
    first = spot
    parts = (mid, by_sides(spot, xa, xb), by_sides(spot, xb, xa))
    for i, ref in enumerate(parts):
        down, up = lane_tile(ref, 0), lane_tile(ref, 2)
        ya[:, i * 128 : i * 128 + 128] = by_side(first, up, down)
        yb[:, i * 128 : i * 128 + 128] = by_side(first, down, up)


def carry(tiles, indices, lh, ll, hot, count=21):
    row, low_row = iota((8, 128), 0), iota((128, 128), 0)
    for t, (values, index) in enumerate(zip(tiles, indices)):
        lanes = slice(t * 128, t * 128 + 128)
        hot[:, lanes] = (low_row == (index & 127)).astype(F32).astype(BF16)
        chosen = row == (index >> 7)
        for pair in range((count + 1) // 2):
            both = []
            for r in (2 * pair, 2 * pair + 1):
                blank = jnp.zeros((8, 128), F32)
                both.append(blank if r >= count else jnp.where(chosen, values(r), 0.0))
            rows = slice(pair * 16, pair * 16 + 16)
            lh[rows, lanes], ll[rows, lanes] = split(jnp.concatenate(both, axis=0))
    return nt(lh[...], hot[...]) + nt(ll[...], hot[...])


def weights_kernel(early, send, w_hi, w_lo, d_hi, d_lo, a_hi, a_lo, b_hi, b_lo, arrive, hot):
    frac, cells, _ = fields(early)
    build_z(frac[2], cells[2], w_hi, w_lo, d_hi, d_lo)

    def put(t, got):
        arrive[:, t, :] = got

    static_rows(early, send, (2, 3, 4, 5, 6, 7, 0, 1), hot, put)
    _, _, cell_z = cells_of((arrive[3] + 0.5).astype(I32))
    build_z(arrive[2], cell_z, a_hi, a_lo, b_hi, b_lo)


def stay_kernel(
    now, second, prior, early, w_hi, w_lo, d_hi, d_lo,
    stayed, core, ends,
    lh, ll, hot, l0h, l0l, l2h, l2l,
):
    tiles = [lambda r, t=t: second[r, t : t + 1, :] for t in range(8)]
    total = carry(tiles, [prior[t : t + 1] for t in range(8)], lh, ll, hot)
    use = now[112:120]
    adj = [total[i * 8 : i * 8 + 8] * use for i in range(21)]
    for i in range(21):
        stayed[i] = adj[i]
    frac, (cell_x, cell_y, _), deform = fields(early)
    a_v, b_c = to_grid(adj, deform)
    l, w = (l0h, l0l, l2h, l2l), (w_hi, w_lo, d_hi, d_lo)
    scatter_rows(a_v, b_c, frac, cell_x, cell_y, *l)
    core[...], ends[...] = all_sums(l, w)


def near_kernel(
    spot, mid, x_low, x_high, ra, rb, both, far, arrive, ends_stay,
    swap, along, against, own_low, own_high, final,
    l0h, l0l, l2h, l2l, moved, static, e0, e1, e2, e3, zu, zd, up2, dn2,
):
    xa, xb = lane_tile(x_low, 1), lane_tile(x_high, 1)
    groups = [lane_tile(mid, 1), by_side(spot, xa, xb), by_side(spot, xb, xa)]
    groups += [by_side(spot, lane_tile(rb, i), lane_tile(ra, i)) for i in range(3)]
    groups += [by_side(spot, lane_tile(ra, i), lane_tile(rb, i)) for i in range(3)]
    zu[...] = jnp.zeros(zu.shape, F32)
    zd[...] = jnp.zeros(zd.shape, F32)
    direct, relayed = both[0:16], far[...]
    static_low = by_z_side(spot, relayed, direct)
    static_high = by_z_side(spot, direct, relayed)
    for ref, at, first, known in ((zu, 64, 0, static_high), (zd, 0, 3, static_low)):
        for i, tile in enumerate(pieces(groups, at, 3)):
            ref[0:21, i * 128 : i * 128 + 128] = tile
            moved[:, first + i, :] = tile
            static[:, first + i, :] = lane_tile(known, i)[0:14]
    for i, tile in enumerate(pieces(groups[1:], 32, 2)):
        final[:, i * 128 : i * 128 + 128] = tile
        moved[:, 6 + i, :] = tile
        static[:, 6 + i, :] = arrive[:, 6 + i, :]
    l = (l0h, l0l, l2h, l2l)
    e = (e0, e1, e2, e3)
    place = [static[i] for i in range(3)]
    cell_x, cell_y, cell_z = cells_of((static[3] + 0.5).astype(I32))
    build_z(place[2], cell_z, *e, edges_only=True)
    a_v, b_c = to_grid([moved[i] for i in range(21)], [static[4 + i] for i in range(9)])
    scatter_rows(a_v, b_c, place, cell_x, cell_y, *l)
    upward = edge_sums(l, e, slice(0, 16), slice(0, 384))
    downward = edge_sums(l, e, slice(0, 16), slice(384, 768))
    ends = edge_sums(l, e, slice(0, 16), slice(768, 1024)) + ends_stay[...]
    for ref in (up2, dn2, own_low, own_high):
        ref[...] = jnp.zeros(ref.shape, F32)
    put_planes(up2, 0, upward[0:1], upward[3:4])
    put_planes(own_high, 0, upward[1:2], upward[2:3])
    put_planes(own_low, 0, downward[0:1], downward[3:4])
    put_planes(dn2, 0, downward[1:2], downward[2:3])
    put_planes(zu, 21, ends[0:1], ends[3:4])
    put_planes(zd, 21, ends[1:2], ends[2:3])
    swap[0:24] = by_z_side(spot, zu, zd)
    swap[24:48] = by_z_side(spot, zd, zu)
    along[...] = by_z_side(spot, up2, dn2)
    against[...] = by_z_side(spot, dn2, up2)


def second_kernel(
    spot, both, far, against, own_low, own_high, final, arrive, a_hi, a_lo, b_hi, b_lo,
    core_stay, ends_stay,
    h_out, hb_out, ya, yb, moved,
    l0h, l0l, l2h, l2l, h,
):
    for i in range(3):
        near, relayed = lane_tile(both, i)[0:24], lane_tile(far, i)
        moved[:, i, :] = by_side(spot, relayed, near, 4)[0:21]
        moved[:, 3 + i, :] = by_side(spot, near, relayed, 4)[0:21]
    for i in range(2):
        moved[:, 6 + i, :] = lane_tile(final, i)
    place = [arrive[i] for i in range(3)]
    cell_x, cell_y, _ = cells_of((arrive[3] + 0.5).astype(I32))
    a_v, b_c = to_grid([moved[i] for i in range(21)], [arrive[4 + i] for i in range(9)])
    l, w = (l0h, l0l, l2h, l2l), (a_hi, a_lo, b_hi, b_lo)
    scatter_rows(a_v, b_c, place, cell_x, cell_y, *l)
    core, ends = all_sums(l, w)
    h[...] = core + core_stay[...]
    ends = ends + ends_stay[...]
    ends = jnp.concatenate([ends[0:8], jnp.zeros((8, 112), F32)], axis=1)
    halo = jnp.where(iota((8, 256), 0) < 2, ends, 0.0)
    near, relayed = both[21:23, 0:256] + against[0:2], far[21:23, 0:256]
    low = by_z_side(spot, relayed, near) + own_low[0:2]
    high = by_z_side(spot, near, relayed) + own_high[0:2]
    z_fold(3, spot, h, halo, low, high, h_out, hb_out, ya, yb)


def relay_kernel(both, along, _, out):
    out[...] = both[24:48]
    out[21:23, 0:256] = both[45:47, 0:256] + along[0:2]


def deform_kernel(now, stayed, moved, send, affine, bf_out, lh, ll, hot):
    tiles = [lambda r, t=t: moved[12 + r, t : t + 1, :] for t in range(8)]
    rows = [send[t : t + 1] for t in (2, 3, 4, 5, 6, 7, 0, 1)]
    total = carry(tiles, rows, lh, ll, hot, 9)
    use = now[112:120]
    a_f = [(stayed[12 + i] + total[i * 8 : i * 8 + 8]) * use for i in range(9)]
    k = dense(affine, 0, 9)
    for i in range(3):
        for j in range(3):
            bf_out[3 * i + j] = a_f[3 * i + j] + TIME_STEP * sum(
                k[3 * m + i] * a_f[3 * m + j] for m in range(3)
            )


def gather_second_kernel(
    extents, spot, h, hb, from_low, from_high, now, early, bf, w_hi, w_lo, d_hi, d_lo,
    mass_core, mass_halo,
    result,
    total, g_hi, g_lo, s0, sz, rows12, packed,
):
    halo = x_fold(3, spot, h, hb, from_low, from_high, total)
    node_values(
        spot, extents, total, halo,
        lambda x: mass_core[x * 8 : x * 8 + 8], mass_halo[...], g_hi, g_lo,
    )
    frac, (cell_x, cell_y, _), deform = fields(early)
    gather(frac, cell_x, cell_y, g_hi, g_lo, w_hi, w_lo, d_hi, d_lo, s0, sz, rows12)
    use = now[112:120]
    out = particle(rows12, frac, [bf[i] for i in range(9)], deform, use)
    for i in range(21):
        packed[i] = out[i]
    for k in range(CHUNKS):
        result[:, k * 128 : k * 128 + 128] = packed[:, k, :]


def shape(*dims, dtype=F32):
    return jax.ShapeDtypeStruct(dims, dtype)


def call(kernel, name, specs, outs, scratch=()):
    return pl.pallas_call(
        kernel,
        name=name,
        in_specs=list(specs),
        out_specs=[VMEM] * len(outs),
        out_shape=list(outs),
        scratch_shapes=[pltpu.VMEM(*v) if isinstance(v, tuple) else v for v in scratch],
        compiler_params=pltpu.CompilerParams(vmem_limit_bytes=40 * 1024 * 1024),
    )


def crossed(first, second):
    wide, tall = lax.axis_size("gx"), lax.axis_size("gy")
    up = [(x * tall + y, (x + 1) * tall + y) for x in range(wide - 1) for y in range(tall)]
    a = [p if p[0] % tall % 2 == 0 else p[::-1] for p in up]
    b = [p[::-1] for p in a]
    return lax.ppermute(first, ("gx", "gy"), a), lax.ppermute(second, ("gx", "gy"), b)


def both_pairs(first, second, axis):
    count = lax.axis_size(axis)
    a = [(i, i ^ 1) for i in range(count) if i ^ 1 < count]
    b = [p for i in range(1, count - 1, 2) for p in ((i, i + 1), (i + 1, i))]
    ra = lax.ppermute(first, axis, a)
    rb = lax.ppermute(second, axis, b) if b else jnp.zeros_like(second)
    return ra, rb


def body(
    fractions, centers, deform, next_affine, cell_mass, final_adjoint,
    live_count, send_slot, receive_slot, receive_count, prior_slot,
):
    at_y = lax.axis_index("gy")
    at_z = lax.axis_index("gz")
    spot = [lax.axis_index("gx") * 4, at_y * 4, at_z * 128, at_y % 2, at_z % 2]
    spot = jnp.stack(spot + [jnp.zeros_like(at_y)] * 3).astype(I32)
    spot = jnp.broadcast_to(spot[:, None], (8, 128))
    extents = (lax.axis_size("gx") * 4, lax.axis_size("gy") * 4, lax.axis_size("gz") * 128)

    fractions, deform, next_affine = (
        jnp.transpose(v, (1, 0, 2)) for v in (fractions, deform, next_affine)
    )
    slots_back = jnp.transpose(send_slot, (1, 0, 2))
    slots_out = jnp.transpose(receive_slot, (1, 0, 2))
    prior = prior_slot.reshape(8, 128)

    wide = shape(ZROWS, 1024, dtype=BF16)
    weights = [wide] * 4
    lrows = [((144, 1024), BF16)] * 4
    gscratch = [
        ((144, 256), BF16), ((144, 256), BF16),
        ((144, 1024), F32), ((144, 1024), F32), ((12, 8, 128), F32),
    ]

    def fold(comps, h, hb, ya, yb, after=()):
        ra, rb = both_pairs(ya, yb, "gy")
        rows = comps * 16 + 8

        def kernel(*refs):
            y_kernel(comps, *refs[:5], *refs[5 + len(after) :])

        h, hb, xu, xd = call(
            kernel, f"fold_y{comps}", [VMEM] * 5 + [pl.BlockSpec(memory_space=pl.ANY)] * len(after),
            [shape(comps * 48, 128), shape(8, 256), shape(rows, 128), shape(rows, 128)],
            [((rows, 128), F32)] * 2,
        )(spot, h, hb, ra, rb, *after)
        low, high = crossed(xu, xd)
        return h, hb, low, high

    firsts = (
        live_count, final_adjoint, fractions, centers, deform, next_affine, cell_mass, slots_back
    )
    h, hb, both, bf, *w, send, now, early = call(
        first_kernel, "scatter_first", [VMEM] + [HBM] * 8,
        [shape(240, 128), shape(8, 256), shape(32, 384), shape(9, 8, 128)]
        + weights + [shape(8, 128, dtype=I32), shape(120, 128), shape(112, 128)],
        lrows + [((128, 128), BF16), ((16, 384), F32), ((16, 384), F32)]
        + [(v.shape, v.dtype) for v in firsts] + [pltpu.SemaphoreType.DMA((8,))],
    )(spot, *(pltpu.with_memory_space_constraint(v, pltpu.HBM) for v in firsts))
    count = lax.axis_size("gz")
    pairs = [(i, i ^ 1) for i in range(count) if i ^ 1 < count]
    hop = [(i, i + 2) for i in range(0, count - 2, 2)] + [(i, i - 2) for i in range(3, count, 2)]
    both = lax.ppermute(both, "gz", pairs)
    far = lax.ppermute(both[16:32], "gz", hop)
    (pick,) = call(pick_kernel, "fill_pick", [VMEM, VMEM], [shape(9, 128, dtype=I32)])(
        receive_count, slots_out
    )
    weights2 = call(
        weights_kernel, "weights_second", [VMEM] * 2, weights + weights + [shape(14, 8, 128)],
        [((128, 128), BF16)],
    )(early, send)
    w2, wa, arrive = weights2[0:4], weights2[4:8], weights2[8]
    h, hb, ya, yb = call(
        functools.partial(z_kernel, 5), "fold_z5", [VMEM] * 5,
        [shape(240, 128), shape(8, 256), shape(72, 128), shape(72, 128)],
    )(spot, h, hb, both, far)
    h, hb, low, high = fold(5, h, hb, ya, yb, (arrive,))
    second, xu, xd, mid, mass_core, mass_halo = call(
        functools.partial(gather_first_kernel, extents), "gather_first", [VMEM] * 12,
        [shape(21, 8, 128), shape(21, 384), shape(21, 384), shape(21, 384), shape(48, 128), shape(8, 256)],
        [((21, 384), F32)] * 2 + [((240, 128), F32)] + gscratch + [((176, 128), F32), ((128, 128), BF16)],
    )(spot, h, hb, low, high, now, bf, *w, pick)

    x_low, x_high = crossed(xu, xd)
    stayed, core_stay, ends_stay = call(
        stay_kernel, "stay", [VMEM] * 8,
        [shape(21, 8, 128), shape(144, 128), shape(16, 144)],
        [((176, 1024), BF16)] * 2 + [((128, 1024), BF16)] + lrows,
    )(now, second, prior, early, *w2)

    def route(*refs):
        route_y_kernel(*refs[:4], *refs[5:])

    ya, yb = call(
        route, "route_y", [VMEM] * 4 + [pl.BlockSpec(memory_space=pl.ANY)], [shape(21, 384)] * 2
    )(spot, mid, x_low, x_high, ends_stay)
    ra, rb = both_pairs(ya, yb, "gy")
    swap, along, against, own_low, own_high, final = call(
        near_kernel, "scatter_near", [VMEM] * 10,
        [shape(48, 384)] + [shape(2, 256)] * 4 + [shape(21, 256)],
        lrows + [((21, 8, 128), F32), ((14, 8, 128), F32)] + [((16, 1024), BF16)] * 4
        + [((24, 384), F32)] * 2 + [((2, 256), F32)] * 2,
    )(spot, mid, x_low, x_high, ra, rb, both, far, arrive, ends_stay)
    both = lax.ppermute(swap, "gz", pairs)
    against = lax.ppermute(against, "gz", [(b, a) for a, b in hop])
    (far,) = call(
        relay_kernel, "relay", [VMEM] * 2 + [pl.BlockSpec(memory_space=pl.ANY)], [shape(24, 384)]
    )(both, along, against)
    far = lax.ppermute(far, "gz", hop)
    h, hb, ya, yb, moved = call(
        second_kernel, "scatter_second", [VMEM] * 14,
        [shape(144, 128), shape(8, 256), shape(48, 128), shape(48, 128), shape(21, 8, 128)],
        lrows + [((144, 128), F32)],
    )(
        spot, both, far, against, own_low, own_high, final, arrive, *wa, core_stay, ends_stay
    )
    (bf,) = call(
        deform_kernel, "deform_second", [VMEM] * 5, [shape(9, 8, 128)],
        [((80, 1024), BF16)] * 2 + [((128, 1024), BF16)],
    )(now, stayed, moved, send, next_affine)
    h, hb, low, high = fold(3, h, hb, ya, yb)
    (result,) = call(
        functools.partial(gather_second_kernel, extents), "gather_second", [VMEM] * 14,
        [shape(21, 1024)],
        [((144, 128), F32)] + gscratch + [((21, 8, 128), F32)],
    )(spot, h, hb, low, high, now, early, bf, *w2, mass_core, mass_halo)
    return result


def solution(mesh):
    spread = AXES
    in_specs = (
        P(None, None, spread), P(None, spread), P(None, None, spread), P(None, None, spread),
        P(None, "gx", "gy", "gz"), P(None, spread), P(spread, None), P(spread, None, None),
        P(spread, None, None), P(spread, None), P(spread),
    )
    return jax.shard_map(
        body, mesh=mesh, in_specs=in_specs, out_specs=P(None, spread), check_vma=False
    )
```

```python
import functools

import jax
import jax.numpy as jnp
from jax import lax
from jax.experimental import pallas as pl
from jax.experimental.pallas import tpu as pltpu
from jax.sharding import PartitionSpec as P

TIME_STEP = 0.2
APIC_SCALE = 4.0
STRESS_SCALE = 0.3
F32 = jnp.float32
BF16 = jnp.bfloat16
I32 = jnp.int32
AXES = ("gx", "gy", "gz")
VMEM = pl.BlockSpec(memory_space=pltpu.VMEM)
HBM = pl.BlockSpec(memory_space=pltpu.HBM)
CHUNKS = 8
ZROWS = 144


def contract(a, b, da, db, precision=None):
    return lax.dot_general(
        a, b, (((da,), (db,)), ((), ())), preferred_element_type=F32, precision=precision
    )


def nt(a, b):
    return contract(a, b, 1, 1)


def nn(a, b):
    return contract(a, b, 1, 0)


def split(x):
    hi = x.astype(BF16)
    return hi, (x - hi.astype(F32)).astype(BF16)


def rounded(x):
    hi = x.astype(BF16).astype(F32)
    return hi, x - hi


def spline(f):
    return 0.5 * (0.5 - f) * (0.5 - f), 0.75 - f * f, 0.5 * (0.5 + f) * (0.5 + f)


def iota(shape, axis):
    return lax.broadcasted_iota(I32, shape, axis)


def dense(ref, step, rows):
    value = ref[:, step, :] if step is not None else ref[...]
    value = value.reshape(rows, CHUNKS, 128)
    return [value[i] for i in range(rows)]


def axis_tables(fx, cell_x, count):
    low, mid, high = spline(fx)
    plain, signed = [], []
    for plane in range(count):
        is_low, is_mid, is_high = cell_x == plane, cell_x + 1 == plane, cell_x + 2 == plane
        plain.append(jnp.where(is_low, low, jnp.where(is_mid, mid, jnp.where(is_high, high, 0.0))))
        signed.append(jnp.where(is_low, -low, jnp.where(is_high, high, 0.0)))
    return plain, signed


def y_tables(fy, cell_y, chunk):
    low, mid, high = (v[chunk : chunk + 1] for v in spline(fy))
    away = iota((8, 128), 0) - (cell_y[chunk : chunk + 1] + 1)
    plain = jnp.where(away == -1, low, jnp.where(away == 0, mid, jnp.where(away == 1, high, 0.0)))
    signed = jnp.where(away == -1, -low, jnp.where(away == 1, high, 0.0))
    return plain, signed


def build_z(fz, cell_z, w_hi, w_lo, d_hi, d_lo, chunks=CHUNKS, edges_only=False):
    low, mid, high = spline(fz)
    low_h, low_l = rounded(low)
    mid_h, mid_l = rounded(mid)
    high_h, high_l = rounded(high)
    to_low = jnp.where(cell_z == 0, 129, cell_z - 1)
    to_high = cell_z + 1
    rows16 = iota((16, 128), 0)
    edge = jnp.where(rows16 == 2, 0, jnp.where(rows16 == 3, 127, 999))
    edge = jnp.where(rows16 < 2, rows16 + 128, edge)
    groups = [] if edges_only else [(g * 16, rows16 + g * 16) for g in range(8)]
    groups.append((0 if edges_only else 128, edge))
    groups = [(at, index.astype(F32).astype(BF16)) for at, index in groups]
    nothing = jnp.zeros((16, 128), BF16)

    def wide(row):
        return jnp.broadcast_to(row.astype(F32), (16, 128)).astype(BF16)

    for chunk in range(chunks):
        at = slice(chunk, chunk + 1)
        lanes = slice(chunk * 128, chunk * 128 + 128)
        targets = [wide(v[at]) for v in (to_low, cell_z, to_high)]
        sets = []
        for plain, signed, parts in (
            (w_hi, d_hi, (low_h, mid_h, high_h)),
            (w_lo, d_lo, (low_l, mid_l, high_l)),
        ):
            sets.append((plain, signed, [wide(v[at]) for v in parts + (-parts[0],)]))
        for first, index in groups:
            rows = slice(first, first + 16)
            is_low, is_mid, is_high = (index == v for v in targets)
            for plain, signed, (a, b, c, d) in sets:
                ends = jnp.where(is_high, c, nothing)
                plain[rows, lanes] = jnp.where(is_low, a, jnp.where(is_mid, b, ends))
                signed[rows, lanes] = jnp.where(is_low, d, ends)


def row_of(info, i, rows=8):
    return jnp.broadcast_to(info[i : i + 1, :], (rows, 128))


def by_side(info, one, other, axis_row=3):
    return jnp.where(row_of(info, axis_row, one.shape[0]) == 0, one, other)


def by_z_side(info, one, other):
    tiles = [
        by_side(info, lane_tile(one, t), lane_tile(other, t), 4) for t in range(one.shape[1] // 128)
    ]
    return jnp.concatenate(tiles, axis=1)


def fields(ref):
    tiles = [ref[i * 8 : i * 8 + 8] for i in range(13)]
    return tiles[0:3], cells_of((tiles[3] + 0.5).astype(I32)), tiles[4:13]


def in_use(live, step):
    slots = iota((8, 128), 0) * 128 + iota((8, 128), 1)
    return (slots < jnp.broadcast_to(live[0:1, step : step + 1], (8, 128))).astype(F32)


STEPS = (0, 1, -1)


def offset_row(offset):
    place = (offset[0] + 1) * 9 + (offset[1] + 1) * 3 + offset[2] + 1
    return place - (place > 13)


def fill_send(slots, send):
    inward = [(x, y, 0) for y in STEPS for x in STEPS][1:]
    order = inward + [(x, y, 1) for y in STEPS for x in STEPS] + [None] * 3
    order += [(x, y, -1) for y in STEPS for x in STEPS]
    send[...] = jnp.zeros(send.shape, I32)
    for n, offset in enumerate(order):
        if offset is not None:
            lane = n % 4 * 32
            send[n // 4 : n // 4 + 1, lane : lane + 32] = slots[25 - offset_row(offset)]


def pick_kernel(counts, slots, pick):
    pick[...] = jnp.full(pick.shape, -1, I32)
    order = iota((1, 32), 1)
    for x in (-1, 0, 1):
        for y in (-1, 0, 1):
            for z in (-1, 0, 1):
                if (x, y, z) != (0, 0, 0):
                    n, row, lane = offset_row((x, y, z)), (x + 1) * 3 + y + 1, (z + 1) * 32
                    pick[row : row + 1, lane : lane + 32] = jnp.where(
                        order < jnp.broadcast_to(counts[0:1, n : n + 1], (1, 32)), slots[n], -1
                    )


def cells_of(centre):
    return centre >> 9, (centre >> 7) & 3, centre & 127


def to_grid(adj, deform):
    a_v, a_c, a_f = adj[0:3], adj[3:12], adj[12:21]
    b_c = [
        a_c[3 * i + j] + TIME_STEP * sum(a_f[3 * i + m] * deform[3 * j + m] for m in range(3))
        for i in range(3)
        for j in range(3)
    ]
    return a_v, b_c


def transfer(adj, deform, affine):
    a_v, b_c = to_grid(adj, deform)
    a_f = adj[12:21]
    b_f = [
        a_f[3 * i + j] + TIME_STEP * sum(affine[3 * m + i] * a_f[3 * m + j] for m in range(3))
        for i in range(3)
        for j in range(3)
    ]
    return a_v, b_c, b_f


def scatter_rows(a_v, b_c, frac, cell_x, cell_y, l0h, l0l, l2h, l2l, chunks=CHUNKS):
    base, slope = [], []
    for c in range(3):
        base.append(a_v[c] - APIC_SCALE * sum(b_c[3 * c + j] * frac[j] for j in range(3)))
        slope.append([APIC_SCALE * b_c[3 * c + j] for j in range(3)])
    wx, wx1 = axis_tables(frac[0], cell_x, 6)
    for k in range(chunks):
        at = slice(k, k + 1)
        lanes = slice(k * 128, k * 128 + 128)
        wy, wy1 = y_tables(frac[1], cell_y, k)
        for c in range(3):
            a = wy * base[c][at] + wy1 * slope[c][1][at]
            b = wy * slope[c][0][at]
            d = wy * slope[c][2][at]
            for pair in range(3):
                rows = slice(c * 48 + pair * 16, c * 48 + pair * 16 + 16)
                planes = (2 * pair, 2 * pair + 1)
                l0 = jnp.concatenate([wx[x][at] * a + wx1[x][at] * b for x in planes], axis=0)
                l2 = jnp.concatenate([wx[x][at] * d for x in planes], axis=0)
                l0h[rows, lanes], l0l[rows, lanes] = split(l0)
                l2h[rows, lanes], l2l[rows, lanes] = split(l2)


def paired(l, w):
    l0h, l0l, l2h, l2l = l
    w_hi, w_lo, d_hi, d_lo = w
    return ((l0h, w_hi), (l0l, w_hi), (l0h, w_lo), (l2h, d_hi), (l2l, d_hi), (l2h, d_lo))


def all_sums(l, w):
    full = sum(nt(a[...], b[...]) for a, b in paired(l, w))
    tail = jnp.concatenate([full[:, 128:ZROWS], jnp.zeros((144, 112), F32)], axis=1)
    tail = jnp.concatenate([tail, jnp.zeros((112, 128), F32)], axis=0).T
    return full[:, 0:128], tail[0:16, 0:144]


def edge_sums(l, w, rows=slice(128, ZROWS), lanes=slice(0, 1024)):
    return sum(nt(b[rows, lanes], a[:, lanes]) for a, b in paired(l, w))


def put_planes(ref, at, first, second):
    width = first.shape[1]
    ref[at : at + 1, :width] = first
    ref[at + 1 : at + 2, :width] = second


def static_rows(table, send, rows, hot, put):
    hi, lo = split(table[...])
    low_row, row = iota((128, 128), 0), iota((8, 128), 0)
    for t, n in enumerate(rows):
        index = send[n : n + 1]
        hot[...] = (low_row == (index & 127)).astype(F32).astype(BF16)
        got = (nn(hi, hot[...]) + nn(lo, hot[...])).reshape(14, 8, 128)
        chosen = row == (index >> 7)
        put(t, jnp.sum(jnp.where(chosen[None], got, 0.0), axis=1))


def first_kernel(
    spot, live_at, adjoint_at, fractions_at, centers_at, deform_at, affine_at, mass_at, slots_at,
    h, hb, both, bf_out, w_hi, w_lo, d_hi, d_lo, send, now, early,
    l0h, l0l, l2h, l2l, hot, zu, zd,
    live, adjoint, fractions, centers, deform, affine, mass, slots_back, arrived,
):
    sources = (slots_at, fractions_at, centers_at, deform_at, live_at, adjoint_at, affine_at, mass_at)
    places = (slots_back, fractions, centers, deform, live, adjoint, affine, mass)
    copies = [
        pltpu.make_async_copy(a, b, arrived.at[i]) for i, (a, b) in enumerate(zip(sources, places))
    ]
    for copy in copies:
        copy.start()
    w = (w_hi, w_lo, d_hi, d_lo)
    l = (l0h, l0l, l2h, l2l)
    zu[...] = jnp.zeros(zu.shape, F32)
    zd[...] = jnp.zeros(zd.shape, F32)
    for copy in copies[:3]:
        copy.wait()
    fill_send(slots_back, send)
    frac = dense(fractions, 1, 3)
    centre = centers[1:2, :].reshape(CHUNKS, 128)
    cell_x, cell_y, cell_z = cells_of(centre)
    build_z(frac[2], cell_z, *w)
    for copy in copies[3:]:
        copy.wait()
    deform_now = dense(deform, 1, 9)
    for i, tile in enumerate(frac + [centre.astype(F32)] + deform_now):
        now[i * 8 : i * 8 + 8] = tile
    early[104:112] = jnp.zeros((8, 128), F32)
    use = in_use(live, 1)
    now[104:112] = use
    now[112:120] = in_use(live, 0)
    known = dense(fractions, 0, 3) + [centers[0:1, :].reshape(CHUNKS, 128).astype(F32)]
    for i, tile in enumerate(known + dense(deform, 0, 9)):
        early[i * 8 : i * 8 + 8] = tile

    def put(t, got):
        dest = (zd, zu)[t // 3]
        dest[0:14, t % 3 * 128 : t % 3 * 128 + 128] = got

    static_rows(early, send, range(2, 8), hot, put)
    adj = [v * use for v in dense(adjoint, None, 21)]
    a_v, b_c, b_f = transfer(adj, deform_now, dense(affine, 1, 9))
    for i in range(9):
        bf_out[i] = b_f[i]
    scatter_rows(a_v, b_c, frac, cell_x, cell_y, *l)
    core, ends = all_sums(l, w)
    h[0:144] = core
    h[144:240] = jnp.zeros((96, 128), F32)
    for s in range(2):
        for x in range(4):
            row = 144 + s * 48 + (x + 1) * 8 + 1
            h[row : row + 4] = mass[s, x]
    lane, row = iota((16, 128), 1), iota((16, 128), 0)
    pick = (((row == 2) & (lane == 0)) | ((row == 3) & (lane == 127))).astype(F32)
    mass_ends = contract(pick, h[144:240], 1, 1, lax.Precision.HIGHEST)
    ends = jnp.concatenate([ends, mass_ends], axis=1)
    hb[...] = jnp.zeros(hb.shape, F32)
    put_planes(hb, 0, ends[0:1], ends[1:2])
    put_planes(zu, 13, ends[0:1], ends[3:4])
    put_planes(zd, 13, ends[1:2], ends[2:3])
    both[0:16] = by_z_side(spot, zu, zd)
    both[16:32] = by_z_side(spot, zd, zu)


def wide_rows(hb):
    return jnp.concatenate(
        [hb[0:1, :128], hb[0:1, 128:], hb[1:2, :128], hb[1:2, 128:], jnp.zeros((4, 128), F32)], axis=0
    )


def from_wide(rows):
    top = jnp.concatenate([rows[0:1], rows[1:2]], axis=1)
    low = jnp.concatenate([rows[2:3], rows[3:4]], axis=1)
    return jnp.concatenate([top, low, jnp.zeros((6, 256), F32)], axis=0)


def transposed(rows):
    return jnp.concatenate([rows, jnp.zeros((120, 256), F32)], axis=0).T


def z_kernel(comps, spot, h, hb, both, far, h_out, hb_out, ya, yb):
    direct, relayed = both[13:15, 0:256], far[13:15, 0:256]
    low, high = by_z_side(spot, relayed, direct), by_z_side(spot, direct, relayed)
    z_fold(comps, spot, h, hb[...], low, high, h_out, hb_out, ya, yb)


def z_fold(comps, first, h, halo, low, high, h_out, hb_out, ya, yb):
    pad = jnp.zeros((6, 256), F32)
    halo = halo + jnp.concatenate([high[1:2], low[1:2], pad], axis=0)
    hb_out[...] = halo
    wall = transposed(jnp.concatenate([low[0:1], high[0:1], pad], axis=0))
    lane = iota((8, 128), 1)
    row = iota((8, 128), 0)
    blocks = comps * 6
    up, down = None, None
    for q in range(blocks):
        rows = slice(q * 8, q * 8 + 8)
        tile = (
            h[rows]
            + jnp.where(lane == 0, wall[rows, 0:1], 0.0)
            + jnp.where(lane == 127, wall[rows, 1:2], 0.0)
        )
        h_out[rows] = tile
        place = 2 * (q % 4)
        chosen = (row >= place) & (row < place + 2)
        a = pltpu.roll(tile, (place - 4) % 8, 0) if place != 4 else tile
        b = pltpu.roll(tile, place, 0) if place else tile
        up = jnp.where(chosen, a, 0.0 if up is None else up)
        down = jnp.where(chosen, b, 0.0 if down is None else down)
        if q % 4 == 3 or q == blocks - 1:
            out = slice(q // 4 * 8, q // 4 * 8 + 8)
            ya[out] = by_side(first, up, down)
            yb[out] = by_side(first, down, up)
            up, down = None, None
    packed = (blocks + 3) // 4 * 8
    ya[packed : packed + 8] = wide_rows(halo)
    yb[packed : packed + 8] = wide_rows(halo)


def y_kernel(comps, spot, h, hb, ra, rb, h_out, hb_out, xu, xd):
    first = spot
    row = iota((8, 128), 0)
    blocks = comps * 6
    packed = (blocks + 3) // 4 * 8
    for q in range(blocks):
        rows = slice(q * 8, q * 8 + 8)
        place = 2 * (q % 4)
        src = slice(q // 4 * 8, q // 4 * 8 + 8)
        a, b = by_side(first, rb[src], ra[src]), by_side(first, ra[src], rb[src])
        a = pltpu.roll(a, (-place) % 8, 0) if place else a
        b = pltpu.roll(b, (4 - place) % 8, 0) if place != 4 else b
        tile = (
            h[rows] + jnp.where(row < 2, a, 0.0) + jnp.where((row >= 4) & (row < 6), b, 0.0)
        )
        h_out[rows] = tile
        c, x = q // 6, q % 6
        if x >= 4:
            xu[c * 16 + (x - 4) * 8 : c * 16 + (x - 4) * 8 + 8] = tile
        if x < 2:
            xd[c * 16 + x * 8 : c * 16 + x * 8 + 8] = tile
    place = iota((8, 256), 1) % 8
    a, b = ra[packed : packed + 8], rb[packed : packed + 8]
    a, b = by_side(first, b, a), by_side(first, a, b)
    a = pltpu.roll(from_wide(a), 252, 1)
    b = pltpu.roll(from_wide(b), 4, 1)
    halo = hb[...] + jnp.where(place < 2, a, 0.0) + jnp.where((place >= 4) & (place < 6), b, 0.0)
    hb_out[...] = halo
    xu[comps * 16 : comps * 16 + 8] = wide_rows(halo)
    xd[comps * 16 : comps * 16 + 8] = wide_rows(halo)


def x_fold(comps, h, hb, from_low, from_high, total):
    for c in range(comps):
        total[c * 48 : c * 48 + 16] = h[c * 48 : c * 48 + 16] + from_low[c * 16 : c * 16 + 16]
        total[c * 48 + 16 : c * 48 + 32] = h[c * 48 + 16 : c * 48 + 32]
        total[c * 48 + 32 : c * 48 + 48] = (
            h[c * 48 + 32 : c * 48 + 48] + from_high[c * 16 : c * 16 + 16]
        )
    plane = iota((8, 256), 1) % 48 // 8
    a = pltpu.roll(from_wide(from_low[comps * 16 : comps * 16 + 8]), 224, 1)
    b = pltpu.roll(from_wide(from_high[comps * 16 : comps * 16 + 8]), 32, 1)
    return hb[...] + jnp.where(plane < 2, a, 0.0) + jnp.where(plane >= 4, b, 0.0)


def node_values(spot, extents, total, halo, mass_at, mass_halo, g_hi, g_lo):
    first_x, first_y, first_z = (row_of(spot, i) for i in range(3))
    far_x, far_y, far_z = (jnp.concatenate([v, v], axis=1) for v in (first_x, first_y, first_z))
    lane, row = iota((8, 128), 1), iota((8, 128), 0)
    node_z = first_z + lane
    node_y = first_y + row - 1
    keep_yz = (
        (node_z >= 1) & (node_z <= extents[2] - 2) & (node_y >= 1) & (node_y <= extents[1] - 2)
    )
    wide = iota((8, 256), 1)
    side = iota((8, 256), 0)
    halo_x = far_x + wide % 48 // 8 - 1
    halo_y = far_y + wide % 8 - 1
    halo_z = far_z + jnp.where(side == 0, 128, -1)
    keep = (
        (halo_x >= 1) & (halo_x <= extents[0] - 2)
        & (halo_y >= 1) & (halo_y <= extents[1] - 2)
        & (halo_z >= 1) & (halo_z <= extents[2] - 2)
        & (side < 2) & (wide < 144) & (wide % 8 < 6)
    )
    ends = jnp.where(keep, halo / jnp.where(keep, mass_halo, 1.0), 0.0)
    columns = transposed(ends)
    g_hi[:, 128:256], g_lo[:, 128:256] = split(columns[0:144])
    for x in range(6):
        node_x = first_x + x - 1
        keep_here = keep_yz & (row < 6) & (node_x >= 1) & (node_x <= extents[0] - 2)
        mass = jnp.where(keep_here, mass_at(x), 1.0)
        for c in range(3):
            rows = slice(c * 48 + x * 8, c * 48 + x * 8 + 8)
            total[rows] = jnp.where(keep_here, total[rows] / mass, 0.0)
    g_hi[:, 0:128], g_lo[:, 0:128] = split(total[0:144])


def gather(frac, cell_x, cell_y, g_hi, g_lo, w_hi, w_lo, d_hi, d_lo, s0, sz, rows12):
    a, b = g_hi[:, 0:ZROWS], g_lo[:, 0:ZROWS]
    s0[...] = nn(a, w_hi[...]) + nn(b, w_hi[...]) + nn(a, w_lo[...])
    sz[...] = nn(a, d_hi[...]) + nn(b, d_hi[...]) + nn(a, d_lo[...])
    wx, wx1 = axis_tables(frac[0], cell_x, 6)
    for k in range(CHUNKS):
        at = slice(k, k + 1)
        lanes = slice(k * 128, k * 128 + 128)
        wy, wy1 = y_tables(frac[1], cell_y, k)
        for c in range(3):
            plain = [s0[c * 48 + x * 8 : c * 48 + x * 8 + 8, lanes] for x in range(6)]
            slope = [sz[c * 48 + x * 8 : c * 48 + x * 8 + 8, lanes] for x in range(6)]
            r0 = sum(wx[x][at] * plain[x] for x in range(6))
            r1 = sum(wx1[x][at] * plain[x] for x in range(6))
            rz = sum(wx[x][at] * slope[x] for x in range(6))
            for i, v in enumerate((wy * r0, wy * r1, wy1 * r0, wy * rz)):
                rows12[c * 4 + i, at, :] = jnp.sum(v, axis=0, keepdims=True)


def particle(rows12, frac, b_f, deform, use):
    r_v = [rows12[c * 4] for c in range(3)]
    area = [rows12[c * 4 + 1 + j] - r_v[c] * frac[j] for c in range(3) for j in range(3)]
    stress = [-STRESS_SCALE * v for v in area]
    cof = []
    for i in range(3):
        for j in range(3):
            i1, i2, j1, j2 = (i + 1) % 3, (i + 2) % 3, (j + 1) % 3, (j + 2) % 3
            cof.append(
                deform[3 * i1 + j1] * deform[3 * i2 + j2] - deform[3 * i1 + j2] * deform[3 * i2 + j1]
            )
    det = sum(deform[j] * cof[j] for j in range(3))
    ratio = (stress[0] + stress[4] + stress[8]) / det
    out = r_v + area
    for i in range(3):
        for j in range(3):
            shear = sum((stress[3 * i + m] + stress[3 * m + i]) * deform[3 * m + j] for m in range(3))
            out.append(b_f[3 * i + j] + shear + ratio * cof[3 * i + j])
    return [v * use for v in out]


def gather_first_kernel(
    extents, spot, h, hb, from_low, from_high, now, bf, w_hi, w_lo, d_hi, d_lo, pick,
    second, xu, xd, mid, mass_core, mass_halo,
    total, g_hi, g_lo, s0, sz, rows12, buf, hot,
):
    halo = x_fold(5, h, hb, from_low, from_high, total)
    mass_core[...] = total[144:192]
    wide = iota((8, 256), 1)

    def spread(step):
        start = 144 + step * 48
        out = jnp.ones((8, 256), F32)
        for c in range(3):
            moved = pltpu.roll(halo, (c * 48 - start) % 256, 1)
            out = jnp.where((wide >= c * 48) & (wide < c * 48 + 48), moved, out)
        return out

    mass_halo[...] = spread(0)
    node_values(
        spot, extents, total, halo,
        lambda x: total[192 + x * 8 : 192 + x * 8 + 8], spread(1), g_hi, g_lo,
    )
    frac, (cell_x, cell_y, _), deform = fields(now)
    gather(frac, cell_x, cell_y, g_hi, g_lo, w_hi, w_lo, d_hi, d_lo, s0, sz, rows12)
    use = now[104:112]
    out = particle(rows12, frac, [bf[i] for i in range(9)], deform, use)
    for i in range(21):
        second[i] = out[i]
        buf[i * 8 : i * 8 + 8] = out[i]
    buf[168:176] = jnp.zeros((8, 128), F32)
    hi, lo = split(buf[...])
    low_row = iota((128, 128), 0)
    row = iota((8, 128), 0)
    for t in range(9):
        index = pick[t : t + 1]
        hot[...] = (low_row == (index & 127)).astype(F32).astype(BF16)
        got = nn(hi, hot[...]) + nn(lo, hot[...])
        chosen = (row == (index >> 7)) & (index >= 0)
        got = got.reshape(22, 8, 128)[0:21]
        got = jnp.sum(jnp.where(chosen[None], got, 0.0), axis=1)
        dest, place = ((xd, t), (mid, t - 3), (xu, t - 6))[t // 3]
        dest[:, place * 128 : place * 128 + 128] = got


def pieces(groups, at, tiles):
    lane = iota((21, 128), 1)
    out = [jnp.zeros((21, 128), F32) for _ in range(tiles)]
    for i, group in enumerate(groups):
        place = 32 * (i % 4)
        moved = pltpu.roll(group, (place - at) % 128, 1) if place != at else group
        out[i // 4] = jnp.where((lane >= place) & (lane < place + 32), moved, out[i // 4])
    return out


def lane_tile(ref, i):
    return ref[:, i * 128 : i * 128 + 128]


def route_y_kernel(spot, mid, from_low, from_high, ya, yb):
    first = spot
    for i, ref in enumerate((mid, from_low, from_high)):
        down, up = lane_tile(ref, 0), lane_tile(ref, 2)
        ya[:, i * 128 : i * 128 + 128] = by_side(first, up, down)
        yb[:, i * 128 : i * 128 + 128] = by_side(first, down, up)


def carry(tiles, indices, lh, ll, hot, count=21):
    row, low_row = iota((8, 128), 0), iota((128, 128), 0)
    for t, (values, index) in enumerate(zip(tiles, indices)):
        lanes = slice(t * 128, t * 128 + 128)
        hot[:, lanes] = (low_row == (index & 127)).astype(F32).astype(BF16)
        chosen = row == (index >> 7)
        for pair in range((count + 1) // 2):
            both = []
            for r in (2 * pair, 2 * pair + 1):
                blank = jnp.zeros((8, 128), F32)
                both.append(blank if r >= count else jnp.where(chosen, values(r), 0.0))
            rows = slice(pair * 16, pair * 16 + 16)
            lh[rows, lanes], ll[rows, lanes] = split(jnp.concatenate(both, axis=0))
    return nt(lh[...], hot[...]) + nt(ll[...], hot[...])


def weights_kernel(early, send, w_hi, w_lo, d_hi, d_lo, a_hi, a_lo, b_hi, b_lo, arrive, hot):
    frac, cells, _ = fields(early)
    build_z(frac[2], cells[2], w_hi, w_lo, d_hi, d_lo)

    def put(t, got):
        arrive[:, t, :] = got

    static_rows(early, send, (2, 3, 4, 5, 6, 7, 0, 1), hot, put)
    _, _, cell_z = cells_of((arrive[3] + 0.5).astype(I32))
    build_z(arrive[2], cell_z, a_hi, a_lo, b_hi, b_lo)


def stay_kernel(
    now, second, prior, early, w_hi, w_lo, d_hi, d_lo,
    stayed, core, ends,
    lh, ll, hot, l0h, l0l, l2h, l2l,
):
    tiles = [lambda r, t=t: second[r, t : t + 1, :] for t in range(8)]
    total = carry(tiles, [prior[t : t + 1] for t in range(8)], lh, ll, hot)
    use = now[112:120]
    adj = [total[i * 8 : i * 8 + 8] * use for i in range(21)]
    for i in range(21):
        stayed[i] = adj[i]
    frac, (cell_x, cell_y, _), deform = fields(early)
    a_v, b_c = to_grid(adj, deform)
    l, w = (l0h, l0l, l2h, l2l), (w_hi, w_lo, d_hi, d_lo)
    scatter_rows(a_v, b_c, frac, cell_x, cell_y, *l)
    core[...], ends[...] = all_sums(l, w)


def near_kernel(
    spot, mid, x_low, x_high, ra, rb, both, far, arrive, ends_stay,
    swap, along, against, own_low, own_high, final,
    l0h, l0l, l2h, l2l, moved, static, e0, e1, e2, e3, zu, zd, up2, dn2,
):
    groups = [lane_tile(mid, 1), lane_tile(x_low, 1), lane_tile(x_high, 1)]
    groups += [by_side(spot, lane_tile(rb, i), lane_tile(ra, i)) for i in range(3)]
    groups += [by_side(spot, lane_tile(ra, i), lane_tile(rb, i)) for i in range(3)]
    zu[...] = jnp.zeros(zu.shape, F32)
    zd[...] = jnp.zeros(zd.shape, F32)
    direct, relayed = both[0:16], far[...]
    static_low = by_z_side(spot, relayed, direct)
    static_high = by_z_side(spot, direct, relayed)
    for ref, at, first, known in ((zu, 64, 0, static_high), (zd, 0, 3, static_low)):
        for i, tile in enumerate(pieces(groups, at, 3)):
            ref[0:21, i * 128 : i * 128 + 128] = tile
            moved[:, first + i, :] = tile
            static[:, first + i, :] = lane_tile(known, i)[0:14]
    for i, tile in enumerate(pieces(groups[1:], 32, 2)):
        final[:, i * 128 : i * 128 + 128] = tile
        moved[:, 6 + i, :] = tile
        static[:, 6 + i, :] = arrive[:, 6 + i, :]
    l = (l0h, l0l, l2h, l2l)
    e = (e0, e1, e2, e3)
    place = [static[i] for i in range(3)]
    cell_x, cell_y, cell_z = cells_of((static[3] + 0.5).astype(I32))
    build_z(place[2], cell_z, *e, edges_only=True)
    a_v, b_c = to_grid([moved[i] for i in range(21)], [static[4 + i] for i in range(9)])
    scatter_rows(a_v, b_c, place, cell_x, cell_y, *l)
    upward = edge_sums(l, e, slice(0, 16), slice(0, 384))
    downward = edge_sums(l, e, slice(0, 16), slice(384, 768))
    ends = edge_sums(l, e, slice(0, 16), slice(768, 1024)) + ends_stay[...]
    for ref in (up2, dn2, own_low, own_high):
        ref[...] = jnp.zeros(ref.shape, F32)
    put_planes(up2, 0, upward[0:1], upward[3:4])
    put_planes(own_high, 0, upward[1:2], upward[2:3])
    put_planes(own_low, 0, downward[0:1], downward[3:4])
    put_planes(dn2, 0, downward[1:2], downward[2:3])
    put_planes(zu, 21, ends[0:1], ends[3:4])
    put_planes(zd, 21, ends[1:2], ends[2:3])
    swap[0:24] = by_z_side(spot, zu, zd)
    swap[24:48] = by_z_side(spot, zd, zu)
    along[...] = by_z_side(spot, up2, dn2)
    against[...] = by_z_side(spot, dn2, up2)


def second_kernel(
    spot, both, far, against, own_low, own_high, final, arrive, a_hi, a_lo, b_hi, b_lo,
    core_stay, ends_stay,
    h_out, hb_out, ya, yb, moved,
    l0h, l0l, l2h, l2l, h,
):
    for i in range(3):
        near, relayed = lane_tile(both, i)[0:24], lane_tile(far, i)
        moved[:, i, :] = by_side(spot, relayed, near, 4)[0:21]
        moved[:, 3 + i, :] = by_side(spot, near, relayed, 4)[0:21]
    for i in range(2):
        moved[:, 6 + i, :] = lane_tile(final, i)
    place = [arrive[i] for i in range(3)]
    cell_x, cell_y, _ = cells_of((arrive[3] + 0.5).astype(I32))
    a_v, b_c = to_grid([moved[i] for i in range(21)], [arrive[4 + i] for i in range(9)])
    l, w = (l0h, l0l, l2h, l2l), (a_hi, a_lo, b_hi, b_lo)
    scatter_rows(a_v, b_c, place, cell_x, cell_y, *l)
    core, ends = all_sums(l, w)
    h[...] = core + core_stay[...]
    ends = ends + ends_stay[...]
    ends = jnp.concatenate([ends[0:8], jnp.zeros((8, 112), F32)], axis=1)
    halo = jnp.where(iota((8, 256), 0) < 2, ends, 0.0)
    near, relayed = both[21:23, 0:256] + against[0:2], far[21:23, 0:256]
    low = by_z_side(spot, relayed, near) + own_low[0:2]
    high = by_z_side(spot, near, relayed) + own_high[0:2]
    z_fold(3, spot, h, halo, low, high, h_out, hb_out, ya, yb)


def relay_kernel(both, along, _, out):
    out[...] = both[24:48]
    out[21:23, 0:256] = both[45:47, 0:256] + along[0:2]


def deform_kernel(now, stayed, moved, send, affine, bf_out, lh, ll, hot):
    tiles = [lambda r, t=t: moved[12 + r, t : t + 1, :] for t in range(8)]
    rows = [send[t : t + 1] for t in (2, 3, 4, 5, 6, 7, 0, 1)]
    total = carry(tiles, rows, lh, ll, hot, 9)
    use = now[112:120]
    a_f = [(stayed[12 + i] + total[i * 8 : i * 8 + 8]) * use for i in range(9)]
    k = dense(affine, 0, 9)
    for i in range(3):
        for j in range(3):
            bf_out[3 * i + j] = a_f[3 * i + j] + TIME_STEP * sum(
                k[3 * m + i] * a_f[3 * m + j] for m in range(3)
            )


def gather_second_kernel(
    extents, spot, h, hb, from_low, from_high, now, early, bf, w_hi, w_lo, d_hi, d_lo,
    mass_core, mass_halo,
    result,
    total, g_hi, g_lo, s0, sz, rows12, packed,
):
    halo = x_fold(3, h, hb, from_low, from_high, total)
    node_values(
        spot, extents, total, halo,
        lambda x: mass_core[x * 8 : x * 8 + 8], mass_halo[...], g_hi, g_lo,
    )
    frac, (cell_x, cell_y, _), deform = fields(early)
    gather(frac, cell_x, cell_y, g_hi, g_lo, w_hi, w_lo, d_hi, d_lo, s0, sz, rows12)
    use = now[112:120]
    out = particle(rows12, frac, [bf[i] for i in range(9)], deform, use)
    for i in range(21):
        packed[i] = out[i]
    for k in range(CHUNKS):
        result[:, k * 128 : k * 128 + 128] = packed[:, k, :]


def shape(*dims, dtype=F32):
    return jax.ShapeDtypeStruct(dims, dtype)


def call(kernel, name, specs, outs, scratch=()):
    return pl.pallas_call(
        kernel,
        name=name,
        in_specs=list(specs),
        out_specs=[VMEM] * len(outs),
        out_shape=list(outs),
        scratch_shapes=[pltpu.VMEM(*v) if isinstance(v, tuple) else v for v in scratch],
        compiler_params=pltpu.CompilerParams(vmem_limit_bytes=40 * 1024 * 1024),
    )


def both_ways(up, down, axis, step=1):
    count = lax.axis_size(axis)
    low = lax.ppermute(up, axis, [(i, i + step) for i in range(count - step)])
    high = lax.ppermute(down, axis, [(i + step, i) for i in range(count - step)])
    return low, high


def both_pairs(first, second, axis):
    count = lax.axis_size(axis)
    a = [(i, i ^ 1) for i in range(count) if i ^ 1 < count]
    b = [p for i in range(1, count - 1, 2) for p in ((i, i + 1), (i + 1, i))]
    ra = lax.ppermute(first, axis, a)
    rb = lax.ppermute(second, axis, b) if b else jnp.zeros_like(second)
    return ra, rb


def body(
    fractions, centers, deform, next_affine, cell_mass, final_adjoint,
    live_count, send_slot, receive_slot, receive_count, prior_slot,
):
    at_y = lax.axis_index("gy")
    at_z = lax.axis_index("gz")
    spot = [lax.axis_index("gx") * 4, at_y * 4, at_z * 128, at_y % 2, at_z % 2]
    spot = jnp.stack(spot + [jnp.zeros_like(at_y)] * 3).astype(I32)
    spot = jnp.broadcast_to(spot[:, None], (8, 128))
    extents = (lax.axis_size("gx") * 4, lax.axis_size("gy") * 4, lax.axis_size("gz") * 128)

    fractions, deform, next_affine = (
        jnp.transpose(v, (1, 0, 2)) for v in (fractions, deform, next_affine)
    )
    slots_back = jnp.transpose(send_slot, (1, 0, 2))
    slots_out = jnp.transpose(receive_slot, (1, 0, 2))
    prior = prior_slot.reshape(8, 128)

    wide = shape(ZROWS, 1024, dtype=BF16)
    weights = [wide] * 4
    lrows = [((144, 1024), BF16)] * 4
    gscratch = [
        ((144, 256), BF16), ((144, 256), BF16),
        ((144, 1024), F32), ((144, 1024), F32), ((12, 8, 128), F32),
    ]

    def fold(comps, h, hb, ya, yb, after=()):
        ra, rb = both_pairs(ya, yb, "gy")
        rows = comps * 16 + 8

        def kernel(*refs):
            y_kernel(comps, *refs[:5], *refs[5 + len(after) :])

        h, hb, xu, xd = call(
            kernel, f"fold_y{comps}", [VMEM] * 5 + [pl.BlockSpec(memory_space=pl.ANY)] * len(after),
            [shape(comps * 48, 128), shape(8, 256), shape(rows, 128), shape(rows, 128)],
        )(spot, h, hb, ra, rb, *after)
        low, high = both_ways(xu, xd, "gx")
        return h, hb, low, high

    firsts = (
        live_count, final_adjoint, fractions, centers, deform, next_affine, cell_mass, slots_back
    )
    h, hb, both, bf, *w, send, now, early = call(
        first_kernel, "scatter_first", [VMEM] + [HBM] * 8,
        [shape(240, 128), shape(8, 256), shape(32, 384), shape(9, 8, 128)]
        + weights + [shape(8, 128, dtype=I32), shape(120, 128), shape(112, 128)],
        lrows + [((128, 128), BF16), ((16, 384), F32), ((16, 384), F32)]
        + [(v.shape, v.dtype) for v in firsts] + [pltpu.SemaphoreType.DMA((8,))],
    )(spot, *(pltpu.with_memory_space_constraint(v, pltpu.HBM) for v in firsts))
    count = lax.axis_size("gz")
    pairs = [(i, i ^ 1) for i in range(count) if i ^ 1 < count]
    hop = [(i, i + 2) for i in range(0, count - 2, 2)] + [(i, i - 2) for i in range(3, count, 2)]
    both = lax.ppermute(both, "gz", pairs)
    far = lax.ppermute(both[16:32], "gz", hop)
    (pick,) = call(pick_kernel, "fill_pick", [VMEM, VMEM], [shape(9, 128, dtype=I32)])(
        receive_count, slots_out
    )
    weights2 = call(
        weights_kernel, "weights_second", [VMEM] * 2, weights + weights + [shape(14, 8, 128)],
        [((128, 128), BF16)],
    )(early, send)
    w2, wa, arrive = weights2[0:4], weights2[4:8], weights2[8]
    h, hb, ya, yb = call(
        functools.partial(z_kernel, 5), "fold_z5", [VMEM] * 5,
        [shape(240, 128), shape(8, 256), shape(72, 128), shape(72, 128)],
    )(spot, h, hb, both, far)
    h, hb, low, high = fold(5, h, hb, ya, yb, (arrive,))
    second, xu, xd, mid, mass_core, mass_halo = call(
        functools.partial(gather_first_kernel, extents), "gather_first", [VMEM] * 12,
        [shape(21, 8, 128), shape(21, 384), shape(21, 384), shape(21, 384), shape(48, 128), shape(8, 256)],
        [((240, 128), F32)] + gscratch + [((176, 128), F32), ((128, 128), BF16)],
    )(spot, h, hb, low, high, now, bf, *w, pick)

    x_low, x_high = both_ways(xu, xd, "gx")
    stayed, core_stay, ends_stay = call(
        stay_kernel, "stay", [VMEM] * 8,
        [shape(21, 8, 128), shape(144, 128), shape(16, 144)],
        [((176, 1024), BF16)] * 2 + [((128, 1024), BF16)] + lrows,
    )(now, second, prior, early, *w2)

    def route(*refs):
        route_y_kernel(*refs[:4], *refs[5:])

    ya, yb = call(
        route, "route_y", [VMEM] * 4 + [pl.BlockSpec(memory_space=pl.ANY)], [shape(21, 384)] * 2
    )(spot, mid, x_low, x_high, ends_stay)
    ra, rb = both_pairs(ya, yb, "gy")
    swap, along, against, own_low, own_high, final = call(
        near_kernel, "scatter_near", [VMEM] * 10,
        [shape(48, 384)] + [shape(2, 256)] * 4 + [shape(21, 256)],
        lrows + [((21, 8, 128), F32), ((14, 8, 128), F32)] + [((16, 1024), BF16)] * 4
        + [((24, 384), F32)] * 2 + [((2, 256), F32)] * 2,
    )(spot, mid, x_low, x_high, ra, rb, both, far, arrive, ends_stay)
    both = lax.ppermute(swap, "gz", pairs)
    against = lax.ppermute(against, "gz", [(b, a) for a, b in hop])
    (far,) = call(
        relay_kernel, "relay", [VMEM] * 2 + [pl.BlockSpec(memory_space=pl.ANY)], [shape(24, 384)]
    )(both, along, against)
    far = lax.ppermute(far, "gz", hop)
    h, hb, ya, yb, moved = call(
        second_kernel, "scatter_second", [VMEM] * 14,
        [shape(144, 128), shape(8, 256), shape(48, 128), shape(48, 128), shape(21, 8, 128)],
        lrows + [((144, 128), F32)],
    )(
        spot, both, far, against, own_low, own_high, final, arrive, *wa, core_stay, ends_stay
    )
    (bf,) = call(
        deform_kernel, "deform_second", [VMEM] * 5, [shape(9, 8, 128)],
        [((80, 1024), BF16)] * 2 + [((128, 1024), BF16)],
    )(now, stayed, moved, send, next_affine)
    h, hb, low, high = fold(3, h, hb, ya, yb)
    (result,) = call(
        functools.partial(gather_second_kernel, extents), "gather_second", [VMEM] * 14,
        [shape(21, 1024)],
        [((144, 128), F32)] + gscratch + [((21, 8, 128), F32)],
    )(spot, h, hb, low, high, now, early, bf, *w2, mass_core, mass_halo)
    return result


def solution(mesh):
    spread = AXES
    in_specs = (
        P(None, None, spread), P(None, spread), P(None, None, spread), P(None, None, spread),
        P(None, "gx", "gy", "gz"), P(None, spread), P(spread, None), P(spread, None, None),
        P(spread, None, None), P(spread, None), P(spread),
    )
    return jax.shard_map(
        body, mesh=mesh, in_specs=in_specs, out_specs=P(None, spread), check_vma=False
    )
```
